32 devices in a mesh: enc: 4 (over z), dp: 8 (over y, x, core).
Axes of the slice: x: 2, y: 2, z: 4, core: 2. Of those that a mesh axis runs over, the one named last changes fastest.
Arguments:
- text: bfloat16 [16384, 768], P(('enc', 'dp')), may hold values from -6 to 6
- region_feats: bfloat16 [13312, 2048], P(('enc', 'dp')), may hold values from -6 to 6
- boxes: bfloat16 [4, 13312], P(None, ('enc', 'dp')), may hold values from 0 to 1
- caption_count: int32 [128], P(('enc', 'dp')), may hold values from 8 to 128, as said below
- region_count: int32 [128], P(('enc', 'dp')), may hold values from 36 to 100, as said below
- region_offset: int32 [32], P(('enc', 'dp')), may hold values from 0 to 31
- w_img: bfloat16 [2048, 768], P(('enc', 'dp')), may hold values from -0.125 to 0.125
- w_box: bfloat16 [4, 768], replicated, may hold values from -3 to 3
- b_img: float32 [768], replicated, may hold values from -3 to 3
- g_reg: float32 [768], replicated, may hold values from 0.25 to 1.75
- beta_reg: float32 [768], replicated, may hold values from -1.75 to 1.75
- w_query: bfloat16 [768, 768], P(('enc', 'dp')), may hold values from -0.21875 to 0.21875
- b_query: float32 [768], replicated, may hold values from -1.75 to 1.75
- w_key: bfloat16 [768, 768], P(('enc', 'dp')), may hold values from -0.21875 to 0.21875
- w_value: bfloat16 [768, 768], P(('enc', 'dp')), may hold values from -0.21875 to 0.21875
- b_value: float32 [768], replicated, may hold values from -1.75 to 1.75
- w_out: bfloat16 [768, 768], P(('enc', 'dp')), may hold values from -1.75 to 1.75
- b_out: float32 [768], replicated, may hold values from -1.75 to 1.75
- g_one: float32 [768], replicated, may hold values from 0.25 to 1.75
- beta_one: float32 [768], replicated, may hold values from -1.75 to 1.75
- w_up: bfloat16 [768, 3072], P(('enc', 'dp')), may hold values from -0.21875 to 0.21875
- b_up: float32 [3072], replicated, may hold values from -1.75 to 1.75
- w_down: bfloat16 [3072, 768], P(('enc', 'dp')), may hold values from -0.109375 to 0.109375
- b_down: float32 [768], replicated, may hold values from -1.75 to 1.75
- g_two: float32 [768], replicated, may hold values from 0.25 to 1.75
- beta_two: float32 [768], replicated, may hold values from -1.75 to 1.75
- cotangent: bfloat16 [32768, 768], P(('enc', 'dp'))
Outputs:
- output: bfloat16 [32768, 768], P(('enc', 'dp'))
- grad_text: bfloat16 [16384, 768], P(('enc', 'dp'))
- grad_feats: bfloat16 [13312, 2048], P(('enc', 'dp'))
- grad_boxes: bfloat16 [4, 13312], P(None, ('enc', 'dp'))
- grad_w_img: float32 [2048, 768], replicated
- grad_w_box: float32 [4, 768], replicated
- grad_b_img: float32 [768], replicated
- grad_g_reg: float32 [768], replicated
- grad_beta_reg: float32 [768], replicated
- grad_w_query: float32 [768, 768], replicated
- grad_b_query: float32 [768], replicated
- grad_w_key: float32 [768, 768], replicated
- grad_w_value: float32 [768, 768], replicated
- grad_b_value: float32 [768], replicated
- grad_w_out: float32 [768, 768], replicated
- grad_b_out: float32 [768], replicated
- grad_g_one: float32 [768], replicated
- grad_beta_one: float32 [768], replicated
- grad_w_up: float32 [768, 3072], replicated
- grad_b_up: float32 [3072], replicated
- grad_w_down: float32 [3072, 768], replicated
- grad_b_down: float32 [768], replicated
- grad_g_two: float32 [768], replicated
- grad_beta_two: float32 [768], replicated
The draws below stay inside these ranges and needn't reach their ends.
Inputs may be any that keep to these rules, and one draw needn't show every extreme that they name: `caption_count`: some sequence has exactly 128 caption tokens. `region_count`: in every draw some holder's 4 sequences all have 100 regions.
All inputs are finite; a program needn't handle non-finite values.
Results may differ from the reference program's by a relative error of at most 0.018.
Values may be sent and summed in bfloat16 or wider, within the bound.
No kernel may reach another device: no remote copies, remote signals or barrier semaphores. Data moves between devices by JAX's collectives and lax.ppermute only.
A program may use at most 192 MiB of HBM per device.

```python
import math
import jax
import jax.numpy as jnp
from jax import lax

D = 768
HEADS = 12
HEAD_DIM = 64
FF = 3072
FEAT = 2048
LT = 128
LR = 128
RMAX = 100
RMIN = 36
CMIN = 8
S_DEV = 4
SEQS = 128
L = 256
CAP = 13
SLOTS = 416
ROWS = 13312
N_ENC = 4
N_DP = 8


def draw_caption_count(key, part):
    key_one, key_two = jax.random.split(jax.random.fold_in(key, 11))
    counts = jax.random.randint(key_one, (SEQS,), CMIN, LT + 1)
    chosen = jax.random.randint(key_two, (), 0, SEQS)
    return jnp.where(jnp.arange(SEQS) == chosen, LT, counts).astype(jnp.int32)


def draw_region_count(key, part):
    key_one, key_two = jax.random.split(jax.random.fold_in(key, 23))
    counts = jax.random.randint(key_one, (SEQS,), RMIN, RMAX + 1)
    holder = jax.random.randint(key_two, (), 0, SEQS // S_DEV)
    return jnp.where(jnp.arange(SEQS) // S_DEV == holder, RMAX, counts).astype(jnp.int32)


def draw_cotangent(key, part):
    total_rows = SEQS * L
    row_pos = jnp.arange(total_rows, dtype=jnp.float32)[:, None] / total_rows
    samples = jax.random.normal(key, (total_rows, D), jnp.float32) * jnp.exp(row_pos * math.log(3.0))
    return samples.astype(jnp.bfloat16)


def with_ends(result, stream_key, smallest, top_value):
    longest = result.shape.index(max(result.shape))
    spots = []
    for shift in (0, 1):
        where = [jax.random.randint(jax.random.fold_in(stream_key, axis), (), 0, length) for axis, length in enumerate(result.shape)]
        where[longest] = (where[longest] + shift) % result.shape[longest]
        spots.append(tuple(where))
    return result.at[spots[0]].set(smallest).at[spots[1]].set(top_value)


def shard_levels(stream_key, extent, cuts, smallest, high):
    def one(dim, blocks):
        heights = jax.random.uniform(jax.random.fold_in(jax.random.fold_in(stream_key, 6), dim), (blocks,), jnp.float32, smallest / len(cuts), high / len(cuts))
        return jnp.repeat(jnp.exp(heights), extent[dim] // blocks).reshape((-1,) + (1,) * (len(extent) - dim - 1))

    gain = one(*cuts[0])
    for cut in cuts[1:]:
        gain = gain * one(*cut)
    return gain


def centred(key, extent, deviation, most, pieces=(), kind=jnp.bfloat16):
    values = jax.random.normal(key, extent, jnp.float32) * deviation
    if len(pieces) > 0:
        values = shard_levels(key, extent, pieces, -0.22, 0.18) * values
    return jnp.clip(values, min=-most, max=most).astype(kind)


def setup_inputs(seed: int = 0) -> dict:
    seeds = jax.random.split(jax.random.key(seed), 28)
    text = centred(seeds[0], (SEQS * LT, D), 1.0, 6.0, ((0, 32),))
    region_feats = centred(seeds[1], (ROWS, FEAT), 1.0, 6.0, ((0, 32),))
    boxes = jnp.clip(1.0 * jax.random.uniform(seeds[2], (4, ROWS), jnp.float32) ** shard_levels(seeds[2], (4, ROWS), ((1, 32),), -0.2, 0.2), 0.0, 1.0).astype(jnp.bfloat16)
    caption_count = draw_caption_count(jax.random.fold_in(seeds[27], 71), 0)
    region_count = draw_region_count(jax.random.fold_in(seeds[27], 71), 0)
    region_offset = with_ends(jax.random.randint(seeds[5], (N_ENC * N_DP,), 0, N_ENC * N_DP), jax.random.fold_in(seeds[5], 1), 0, (N_ENC * N_DP) - 1).astype(jnp.int32)
    w_img = centred(seeds[6], (FEAT, D), FEAT ** -0.5, 0.125, ((0, 32),))
    w_box = centred(seeds[7], (4, D), 4 ** -0.5, 3.0)
    b_img = centred(seeds[8], (D,), 0.5, 3.0, (), jnp.float32)
    g_reg = jnp.clip(1.0 + 0.15 * jax.random.normal(seeds[9], (D,), jnp.float32), 0.25, 1.75)
    beta_reg = centred(seeds[10], (D,), 0.3, 1.75, (), jnp.float32)
    w_query = centred(seeds[11], (D, D), D ** -0.5, 0.21875, ((0, 32),))
    b_query = centred(seeds[12], (D,), 0.3, 1.75, (), jnp.float32)
    w_key = centred(seeds[13], (D, D), D ** -0.5, 0.21875, ((0, 32),))
    w_value = centred(seeds[14], (D, D), D ** -0.5, 0.21875, ((0, 32),))
    b_value = centred(seeds[15], (D,), 0.3, 1.75, (), jnp.float32)
    w_out = centred(seeds[16], (D, D), (D // 64) ** -0.5, 1.75, ((0, 32),))
    b_out = centred(seeds[17], (D,), 0.3, 1.75, (), jnp.float32)
    g_one = jnp.clip(1.0 + 0.15 * jax.random.normal(seeds[18], (D,), jnp.float32), 0.25, 1.75)
    beta_one = centred(seeds[19], (D,), 0.3, 1.75, (), jnp.float32)
    w_up = centred(seeds[20], (D, FF), D ** -0.5, 0.21875, ((0, 32),))
    b_up = centred(seeds[21], (FF,), 0.3, 1.75, (), jnp.float32)
    w_down = centred(seeds[22], (FF, D), FF ** -0.5, 0.109375, ((0, 32),))
    b_down = centred(seeds[23], (D,), 0.3, 1.75, (), jnp.float32)
    g_two = jnp.clip(1.0 + 0.15 * jax.random.normal(seeds[24], (D,), jnp.float32), 0.25, 1.75)
    beta_two = centred(seeds[25], (D,), 0.3, 1.75, (), jnp.float32)
    cotangent = draw_cotangent(jax.random.fold_in(seeds[27], 71), 0)
    return dict(text=text, region_feats=region_feats, boxes=boxes, caption_count=caption_count, region_count=region_count, region_offset=region_offset, w_img=w_img, w_box=w_box, b_img=b_img, g_reg=g_reg, beta_reg=beta_reg, w_query=w_query, b_query=b_query, w_key=w_key, w_value=w_value, b_value=b_value, w_out=w_out, b_out=b_out, g_one=g_one, beta_one=beta_one, w_up=w_up, b_up=b_up, w_down=w_down, b_down=b_down, g_two=g_two, beta_two=beta_two, cotangent=cotangent)


@jax.custom_vjp
def low(v):
    return lax.optimization_barrier(v.astype(jnp.bfloat16)).astype(jnp.float32)

@jax.custom_vjp
def low_back(v):
    return v

def low_keep(v):
    return (low(v), None)

def low_pass(kept, grad):
    return (grad,)

def back_keep(v):
    return (v, None)

def back_low(kept, grad):
    return (low(grad),)
low.defvjp(low_keep, low_pass)
low_back.defvjp(back_keep, back_low)
epsilon = 1e-05

def matmul(left_op, right_op):
    return jnp.dot(left_op, right_op, precision=lax.Precision.HIGHEST, preferred_element_type=jnp.float32)

def norm_layer(values, gain_vec, shift_vec):
    centered = values - lax.optimization_barrier(jnp.mean(values, -1, keepdims=True))
    inverse = lax.rsqrt(lax.optimization_barrier(jnp.mean(centered * centered, -1, keepdims=True)) + epsilon)
    return centered * inverse * gain_vec + shift_vec

def reference(text, region_feats, boxes, caption_count, region_count, region_offset, w_img, w_box, b_img, g_reg, beta_reg, w_query, b_query, w_key, w_value, b_value, w_out, b_out, g_one, beta_one, w_up, b_up, w_down, b_down, g_two, beta_two, cotangent):
    device_count = N_ENC * N_DP
    members = (text, region_feats, boxes, w_img, w_box, b_img, g_reg, beta_reg, w_query, b_query, w_key, w_value, b_value, w_out, b_out, g_one, beta_one, w_up, b_up, w_down, b_down, g_two, beta_two)
    floats = tuple((member.astype(jnp.float32) for member in members))

    def forward(*params):
        text_val, feat_val, box_val, img_w, box_w, img_b, reg_gain, reg_shift, query_w, query_b, key_w, value_w, value_b, out_w, out_b, gain_one, shift_one, up_w, up_b, down_w, down_b, gain_two, shift_two = params
        pre_norm = low_back(matmul(feat_val, img_w) + matmul(box_val.T, box_w) + img_b)
        encoded = low(low_back(norm_layer(pre_norm, reg_gain, reg_shift)))

        def per_holder(holder_data):
            holder_index, text_rows, cap_counts, reg_counts, offset = holder_data
            starts = jnp.cumsum(reg_counts) - reg_counts
            slot_ids = jnp.arange(S_DEV * LR, dtype=jnp.int32)
            seq_of = slot_ids // LR
            slot_pos = slot_ids % LR
            wanted = starts[seq_of] + slot_pos
            slot_live = slot_pos < reg_counts[seq_of]
            source = (wanted % device_count + offset) % device_count
            source_row = source * SLOTS + holder_index * CAP + wanted // device_count
            source_row = jnp.where(slot_live, source_row, 0).astype(jnp.int32)
            regions = jnp.where(slot_live[:, None], jnp.take(encoded, source_row, axis=0), 0.0)
            hidden = jnp.concatenate([text_rows.reshape(S_DEV, LT, D), regions.reshape(S_DEV, LR, D)], 1)
            key_live = jnp.concatenate([jnp.arange(LT)[None, :] < cap_counts[:, None], jnp.arange(LR)[None, :] < reg_counts[:, None]], 1)
            flat_rows = hidden.reshape(S_DEV * L, D)
            query_h = low(low_back(matmul(flat_rows, query_w) + query_b)).reshape(S_DEV, L, HEADS, HEAD_DIM)
            key_h = low(low_back(matmul(flat_rows, key_w))).reshape(S_DEV, L, HEADS, HEAD_DIM)
            value_h = low(low_back(matmul(flat_rows, value_w) + value_b)).reshape(S_DEV, L, HEADS, HEAD_DIM)
            raw_scores = low_back(jnp.einsum('sqhd,skhd->shqk', query_h, key_h, precision=lax.Precision.HIGHEST) * HEAD_DIM ** (-0.5))
            scores = jnp.where(key_live[:, None, None, :], raw_scores, -1e+30)
            attn_probs = jax.nn.softmax(scores, -1)
            context = low(low_back(jnp.einsum('shqk,skhd->sqhd', low(attn_probs), value_h, precision=lax.Precision.HIGHEST))).reshape(S_DEV * L, D)
            mixed = flat_rows + low_back(matmul(context, out_w) + out_b)
            normed_one = low(norm_layer(mixed, gain_one, shift_one))
            gate_in = low_back(matmul(normed_one, up_w) + up_b)
            activated = low(jax.nn.gelu(gate_in, approximate=False))
            second_in = normed_one + low_back(matmul(activated, down_w) + down_b)
            row_live = key_live.reshape(S_DEV * L, 1).astype(jnp.float32)
            return norm_layer(second_in, gain_two, shift_two) * row_live
        stacked = lax.map(jax.checkpoint(per_holder), (jnp.arange(device_count, dtype=jnp.int32), text_val.reshape(device_count, S_DEV * LT, D), caption_count.reshape(device_count, S_DEV), region_count.reshape(device_count, S_DEV), region_offset))
        return stacked.reshape(SEQS * L, D)
    primal, pullback = jax.vjp(forward, *floats)
    gradients = pullback(cotangent.astype(jnp.float32))
    return (primal.astype(jnp.bfloat16), gradients[0].astype(jnp.bfloat16), gradients[1].astype(jnp.bfloat16), gradients[2].astype(jnp.bfloat16), gradients[3], gradients[4], gradients[5], gradients[6], gradients[7], gradients[8], gradients[9], gradients[10], gradients[11], gradients[12], gradients[13], gradients[14], gradients[15], gradients[16], gradients[17], gradients[18], gradients[19], gradients[20], gradients[21], gradients[22])
```

```python
import jax
import jax.numpy as jnp
from jax import lax
from jax.sharding import PartitionSpec as P

HEADS = 12


epsilon = 1e-05


def normalize(values, gain_vec, shift_vec):
    centered = values - jnp.mean(values, -1, keepdims=True)
    inverse = lax.rsqrt(jnp.mean(centered * centered, -1, keepdims=True) + epsilon)
    normed = centered * inverse
    return (normed * gain_vec + shift_vec, normed, inverse)


def normalize_back(upstream, normed, inverse, gain_vec):
    weighted = upstream * gain_vec
    result = inverse * (
        weighted
        - jnp.mean(weighted, -1, keepdims=True)
        - normed * jnp.mean(weighted * normed, -1, keepdims=True)
    )
    return (result, jnp.sum(upstream * normed, 0), jnp.sum(upstream, 0))


def exact_gelu(values):
    return jax.nn.gelu(values, approximate=False)


def outer_sum(row_data, row_grad):
    return jnp.einsum("ra,rb->ab", row_data, row_grad, preferred_element_type=jnp.float32)


def back_product(row_grad, weight):
    return jnp.einsum("rb,ab->ra", row_grad, weight, preferred_element_type=jnp.float32)


def column_sum(row_grad):
    return jnp.sum(row_grad.astype(jnp.float32), 0)


def axis_bits(name):
    size = lax.axis_size(name)
    bits = []
    step = 1
    while step < size:
        bits.append((name, step))
        step *= 2
    return bits


def swap_bit(tensor, bit):
    name, step = bit
    size = lax.axis_size(name)
    return lax.ppermute(tensor, name, [(i, i ^ step) for i in range(size)])


def stage_orders():
    dp_bits, enc_bits = axis_bits("dp"), axis_bits("enc")
    near, middle = dp_bits[:1], dp_bits[1:]
    half = len(middle) // 2
    return (
        near + middle + enc_bits,
        near + middle[half:] + middle[:half] + enc_bits,
    )


def scatter_sum(parts, order):
    dp_bits, enc_bits = axis_bits("dp"), axis_bits("enc")
    layout = enc_bits[::-1] + dp_bits[::-1]
    value = parts.reshape((2,) * len(layout) + parts.shape[1:])
    for bit in order:
        axis = layout.index(bit)
        layout = layout[:axis] + layout[axis + 1 :]
        mine = (lax.axis_index(bit[0]) // bit[1]) % 2
        away = lax.dynamic_index_in_dim(value, 1 - mine, axis, keepdims=False)
        kept = lax.dynamic_index_in_dim(value, mine, axis, keepdims=False)
        came = swap_bit(away, bit)
        value = (kept.astype(jnp.float32) + came.astype(jnp.float32)).astype(jnp.bfloat16)
    return value


def body(
    text,
    region_feats,
    boxes,
    caption_count,
    region_count,
    region_offset,
    w_img,
    w_box,
    b_img,
    g_reg,
    beta_reg,
    w_query,
    b_query,
    w_key,
    w_value,
    b_value,
    w_out,
    b_out,
    g_one,
    beta_one,
    w_up,
    b_up,
    w_down,
    b_down,
    g_two,
    beta_two,
    cotangent,
):
    axes = ("enc", "dp")
    first = lax.all_gather(
        jnp.concatenate([w_img, w_query, w_key, w_value, w_out], 0), axes, axis=0
    )
    up_full = lax.all_gather(w_up, axes, axis=0, tiled=True)
    down_full = lax.all_gather(w_down, axes, axis=0, tiled=True)
    cuts = []
    at = 0
    for weight in (w_img, w_query, w_key, w_value, w_out):
        rows = weight.shape[0]
        cuts.append(first[:, at : at + rows].reshape(-1, weight.shape[1]))
        at += rows
    img_full, query_full, key_full, value_full, out_full = cuts
    device_count = lax.axis_size(("enc", "dp"))
    seq_count = caption_count.shape[0]
    model_width = text.shape[1]
    text_len = text.shape[0] // seq_count
    seq_len = cotangent.shape[0] // seq_count
    region_len = seq_len - text_len
    sent_rows = region_feats.shape[0]
    per_peer = sent_rows // device_count
    head_dim = model_width // HEADS
    score_scale = head_dim ** (-0.5)
    pre_norm = (
        jnp.dot(region_feats, img_full, preferred_element_type=jnp.float32)
        + jnp.einsum("cr,cd->rd", boxes, w_box, preferred_element_type=jnp.float32)
        + b_img
    )
    encoded, enc_normed, enc_inverse = normalize(pre_norm, g_reg, beta_reg)
    received = lax.all_to_all(
        encoded.astype(jnp.bfloat16), ("enc", "dp"), split_axis=0, concat_axis=0, tiled=True
    )
    position = jnp.arange(sent_rows, dtype=jnp.int32)
    arrival = (
        position % per_peer * device_count
        + (position // per_peer - region_offset[0]) % device_count
    )
    starts = jnp.cumsum(region_count) - region_count
    slot_total = seq_count * region_len
    slot_pos = jnp.arange(slot_total, dtype=jnp.int32) % region_len
    wanted = jnp.repeat(starts, region_len, total_repeat_length=slot_total) + slot_pos
    slot_live = slot_pos < jnp.repeat(region_count, region_len, total_repeat_length=slot_total)
    placement = ((wanted[:, None] == arrival[None, :]) & slot_live[:, None]).astype(jnp.bfloat16)
    regions = jnp.dot(placement, received, preferred_element_type=jnp.float32).astype(jnp.bfloat16)
    hidden_in = jnp.concatenate(
        [
            text.reshape(seq_count, text_len, model_width),
            regions.reshape(seq_count, region_len, model_width),
        ],
        1,
    ).reshape(seq_count * seq_len, model_width)
    key_live = jnp.concatenate(
        [
            jnp.arange(text_len)[None, :] < caption_count[:, None],
            jnp.arange(region_len)[None, :] < region_count[:, None],
        ],
        1,
    )
    row_live = key_live.reshape(-1, 1).astype(jnp.float32)

    def heads_view(tensor):
        return tensor.reshape(seq_count, seq_len, HEADS, head_dim)

    query_heads = heads_view(
        (jnp.dot(hidden_in, query_full, preferred_element_type=jnp.float32) + b_query).astype(
            jnp.bfloat16
        )
    )
    key_heads = heads_view(
        jnp.dot(hidden_in, key_full, preferred_element_type=jnp.float32).astype(jnp.bfloat16)
    )
    value_heads = heads_view(
        (jnp.dot(hidden_in, value_full, preferred_element_type=jnp.float32) + b_value).astype(
            jnp.bfloat16
        )
    )
    scores = (
        jnp.einsum("sqhd,skhd->shqk", query_heads, key_heads, preferred_element_type=jnp.float32)
        * score_scale
    )
    scores = jnp.where(key_live[:, None, None, :], scores, -1e30)
    row_max = jnp.max(scores, -1, keepdims=True)
    exp_scores = jnp.exp(scores - row_max)
    attn_probs = exp_scores / jnp.sum(exp_scores, -1, keepdims=True)
    probs_low = attn_probs.astype(jnp.bfloat16)
    context = (
        jnp.einsum("shqk,skhd->sqhd", probs_low, value_heads, preferred_element_type=jnp.float32)
        .reshape(-1, model_width)
        .astype(jnp.bfloat16)
    )
    mixed = (
        hidden_in.astype(jnp.float32)
        + jnp.dot(context, out_full, preferred_element_type=jnp.float32)
        + b_out
    )
    normed_one, one_normed, one_inverse = normalize(mixed, g_one, beta_one)
    normed_one = normed_one.astype(jnp.bfloat16)
    gate_in = jnp.dot(normed_one, up_full, preferred_element_type=jnp.float32) + b_up
    activated = exact_gelu(gate_in).astype(jnp.bfloat16)
    second_in = (
        normed_one.astype(jnp.float32)
        + jnp.dot(activated, down_full, preferred_element_type=jnp.float32)
        + b_down
    )
    normed_two, two_normed, two_inverse = normalize(second_in, g_two, beta_two)
    output = (normed_two * row_live).astype(jnp.bfloat16)
    grad_second = cotangent.astype(jnp.float32) * row_live
    grad_second_in, grad_g_two, grad_beta_two = normalize_back(
        grad_second, two_normed, two_inverse, g_two
    )
    grad_down_out = grad_second_in.astype(jnp.bfloat16)
    grad_w_down = outer_sum(activated, grad_down_out)
    grad_b_down = column_sum(grad_down_out)
    grad_activated = back_product(grad_down_out, down_full)
    gelu_pull = jax.vjp(exact_gelu, gate_in)[1]
    grad_gate = gelu_pull(grad_activated)[0].astype(jnp.bfloat16)
    grad_w_up = outer_sum(normed_one, grad_gate)
    grad_b_up = column_sum(grad_gate)
    grad_first = back_product(grad_gate, up_full) + grad_second_in
    grad_mixed, grad_g_one, grad_beta_one = normalize_back(
        grad_first, one_normed, one_inverse, g_one
    )
    grad_attn = grad_mixed.astype(jnp.bfloat16)
    grad_w_out = outer_sum(context, grad_attn)
    grad_b_out = column_sum(grad_attn)
    grad_context = heads_view(back_product(grad_attn, out_full).astype(jnp.bfloat16))
    grad_probs = jnp.einsum(
        "sqhd,skhd->shqk", grad_context, value_heads, preferred_element_type=jnp.float32
    )
    grad_values = (
        jnp.einsum("shqk,sqhd->skhd", probs_low, grad_context, preferred_element_type=jnp.float32)
        .reshape(-1, model_width)
        .astype(jnp.bfloat16)
    )
    grad_scores = (
        attn_probs * (grad_probs - jnp.sum(attn_probs * grad_probs, -1, keepdims=True))
    ).astype(jnp.bfloat16)
    grad_query = (
        (
            jnp.einsum(
                "shqk,skhd->sqhd", grad_scores, key_heads, preferred_element_type=jnp.float32
            )
            * score_scale
        )
        .reshape(-1, model_width)
        .astype(jnp.bfloat16)
    )
    grad_keys = (
        (
            jnp.einsum(
                "shqk,sqhd->skhd", grad_scores, query_heads, preferred_element_type=jnp.float32
            )
            * score_scale
        )
        .reshape(-1, model_width)
        .astype(jnp.bfloat16)
    )
    grad_w_query = outer_sum(hidden_in, grad_query)
    grad_b_query = column_sum(grad_query)
    grad_w_key = outer_sum(hidden_in, grad_keys)
    grad_w_value = outer_sum(hidden_in, grad_values)
    grad_b_value = column_sum(grad_values)
    grad_hidden = (
        grad_mixed
        + back_product(grad_query, query_full)
        + back_product(grad_keys, key_full)
        + back_product(grad_values, value_full)
    )
    grad_hidden = grad_hidden.reshape(seq_count, seq_len, model_width)
    grad_text = grad_hidden[:, :text_len].reshape(-1, model_width).astype(jnp.bfloat16)
    grad_slots = grad_hidden[:, text_len:].reshape(-1, model_width).astype(jnp.bfloat16)
    grad_sent = jnp.einsum(
        "tn,td->nd", placement, grad_slots, preferred_element_type=jnp.float32
    ).astype(jnp.bfloat16)
    grad_encoded = lax.all_to_all(
        grad_sent, ("enc", "dp"), split_axis=0, concat_axis=0, tiled=True
    ).astype(jnp.float32)
    grad_pre, grad_g_reg, grad_beta_reg = normalize_back(
        grad_encoded, enc_normed, enc_inverse, g_reg
    )
    grad_pre = grad_pre.astype(jnp.bfloat16)
    grad_w_img = outer_sum(region_feats, grad_pre)
    grad_w_box = jnp.einsum("cr,rd->cd", boxes, grad_pre, preferred_element_type=jnp.float32)
    grad_b_img = column_sum(grad_pre)
    grad_feats = back_product(grad_pre, img_full).astype(jnp.bfloat16)
    grad_boxes = jnp.einsum(
        "cd,rd->cr", w_box, grad_pre, preferred_element_type=jnp.float32
    ).astype(jnp.bfloat16)
    orders = stage_orders()
    width = model_width
    ff_blocks = w_up.shape[1] // width

    def parts_of(grad):
        return grad.astype(jnp.bfloat16).reshape(device_count, -1, grad.shape[-1])

    up_cols = jnp.stack(
        [grad_w_up[:, j * width : (j + 1) * width] for j in range(ff_blocks)], 0
    ).reshape(-1, width)
    small = [
        grad_w_box,
        grad_b_img[None],
        grad_g_reg[None],
        grad_beta_reg[None],
        grad_b_query[None],
        grad_b_value[None],
        grad_b_out[None],
        grad_g_one[None],
        grad_beta_one[None],
        grad_b_up.reshape(-1, width),
        grad_b_down[None],
        grad_g_two[None],
        grad_beta_two[None],
    ]
    small = jnp.concatenate(small, 0)
    small_rows = small.shape[0]
    per_small = -(-small_rows // device_count)
    small = jnp.pad(small, ((0, per_small * device_count - small_rows), (0, 0)))
    ff_sum = jnp.concatenate(
        [
            scatter_sum(parts_of(grad_w_down), orders[0]),
            scatter_sum(parts_of(up_cols), orders[1]),
        ],
        0,
    )
    ff_all = lax.all_gather(ff_sum, axes, axis=0)
    qkv_parts = jnp.concatenate(
        [parts_of(g) for g in (grad_w_query, grad_w_key, grad_w_value, grad_w_out)], 1
    )
    img_parts = jnp.concatenate([parts_of(grad_w_img), parts_of(small)], 1)
    rest_sum = jnp.concatenate(
        [scatter_sum(qkv_parts, orders[0]), scatter_sum(img_parts, orders[1])], 0
    )
    rest_all = lax.all_gather(rest_sum, axes, axis=0)

    down_rows = w_down.shape[0]
    grad_w_down = ff_all[:, :down_rows].reshape(-1, width).astype(jnp.float32)
    up_cols = ff_all[:, down_rows:].reshape(ff_blocks, -1, width).astype(jnp.float32)
    grad_w_up = jnp.concatenate([up_cols[j] for j in range(ff_blocks)], 1)
    at = 0
    pieces = []
    for rows in [w_query.shape[0]] * 4 + [w_img.shape[0], per_small]:
        pieces.append(rest_all[:, at : at + rows].reshape(-1, width).astype(jnp.float32))
        at += rows
    grad_w_query, grad_w_key, grad_w_value, grad_w_out, grad_w_img, small = pieces
    box_rows = grad_w_box.shape[0]
    grad_w_box = small[:box_rows]
    singles = small[box_rows:small_rows]
    (
        grad_b_img,
        grad_g_reg,
        grad_beta_reg,
        grad_b_query,
        grad_b_value,
        grad_b_out,
        grad_g_one,
        grad_beta_one,
    ) = [singles[i] for i in range(8)]
    grad_b_up = singles[8 : 8 + ff_blocks].reshape(-1)
    grad_b_down, grad_g_two, grad_beta_two = [singles[8 + ff_blocks + i] for i in range(3)]
    return (
        output,
        grad_text,
        grad_feats,
        grad_boxes,
        grad_w_img,
        grad_w_box,
        grad_b_img,
        grad_g_reg,
        grad_beta_reg,
        grad_w_query,
        grad_b_query,
        grad_w_key,
        grad_w_value,
        grad_b_value,
        grad_w_out,
        grad_b_out,
        grad_g_one,
        grad_beta_one,
        grad_w_up,
        grad_b_up,
        grad_w_down,
        grad_b_down,
        grad_g_two,
        grad_beta_two,
    )


def solution(mesh):
    return jax.shard_map(
        body,
        mesh=mesh,
        in_specs=(
            P(("enc", "dp"), None),
            P(("enc", "dp"), None),
            P(None, ("enc", "dp")),
            P(("enc", "dp")),
            P(("enc", "dp")),
            P(("enc", "dp")),
            P(("enc", "dp"), None),
            P(),
            P(),
            P(),
            P(),
            P(("enc", "dp"), None),
            P(),
            P(("enc", "dp"), None),
            P(("enc", "dp"), None),
            P(),
            P(("enc", "dp"), None),
            P(),
            P(),
            P(),
            P(("enc", "dp"), None),
            P(),
            P(("enc", "dp"), None),
            P(),
            P(),
            P(),
            P(("enc", "dp"), None),
        ),
        out_specs=(
            P(("enc", "dp"), None),
            P(("enc", "dp"), None),
            P(("enc", "dp"), None),
            P(None, ("enc", "dp")),
            P(),
            P(),
            P(),
            P(),
            P(),
            P(),
            P(),
            P(),
            P(),
            P(),
            P(),
            P(),
            P(),
            P(),
            P(),
            P(),
            P(),
            P(),
            P(),
            P(),
        ),
        check_vma=False,
    )
```

```python
import functools
import math

import jax
import jax.numpy as jnp
from jax import lax
from jax.experimental import pallas as pl
from jax.experimental.pallas import tpu as pltpu
from jax.sharding import PartitionSpec as P

HEADS = 12
epsilon = 1e-05
f32, bf16 = jnp.float32, jnp.bfloat16

ERFC_P = 0.35
ERFC_C = (
    0.19567911,
    0.22612264,
    0.02080242,
    0.63768037,
    -0.6386366,
    0.75239514,
    -0.19404308,
)


def nn(a, b):
    return lax.dot_general(a, b, (((1,), (0,)), ((), ())), preferred_element_type=f32)


def nt(a, b):
    return lax.dot_general(a, b, (((1,), (1,)), ((), ())), preferred_element_type=f32)


def tn(a, b):
    return lax.dot_general(a, b, (((0,), (0,)), ((), ())), preferred_element_type=f32)


def norm_parts(values):
    centered = values - jnp.mean(values, -1, keepdims=True)
    inverse = lax.rsqrt(jnp.mean(centered * centered, -1, keepdims=True) + epsilon)
    return centered * inverse, inverse


def norm_back(upstream, normed, inverse, gain):
    weighted = upstream * gain
    return inverse * (
        weighted
        - jnp.mean(weighted, -1, keepdims=True)
        - normed * jnp.mean(weighted * normed, -1, keepdims=True)
    )


def gelu_parts(x):
    e = jnp.exp(-0.5 * x * x)
    t = 1.0 / (1.0 + (ERFC_P * math.sqrt(0.5)) * jnp.abs(x))
    acc = jnp.full_like(t, 0.5 * ERFC_C[-1])
    for c in ERFC_C[-2::-1]:
        acc = acc * t + 0.5 * c
    tail = acc * t * e
    phi = jnp.where(x >= 0, 1.0 - tail, tail)
    return x * phi, phi + x * (e * (1.0 / math.sqrt(2.0 * math.pi)))


def one_hot(wanted, live, rows, pad, sent, devices, offset):
    row = lax.broadcasted_iota(jnp.int32, (1, rows), 1)
    shift = pad.bit_length() - 1
    turn = lax.shift_right_logical(row, shift) - offset
    turn = jnp.where(turn < 0, turn + devices, turn)
    inside = jnp.bitwise_and(row, pad - 1)
    arrival = jnp.where(inside < sent, inside * devices + turn, -1)
    return ((wanted == arrival) & live).astype(bf16)


def spread(pad, sent, rows, padded):
    to = lax.broadcasted_iota(jnp.int32, (padded, 1), 0)
    shift = pad.bit_length() - 1
    inside = jnp.bitwise_and(to, pad - 1)
    source = jnp.where(inside < sent, lax.shift_right_logical(to, shift) * sent + inside, -1)
    return (source == lax.broadcasted_iota(jnp.int32, (1, rows), 1)).astype(bf16)


def image_encode(
    pad, sent, x_ref, box_ref, wi_ref, wb_ref, bi_ref, gr_ref, betar_ref, pre_ref, enc_ref
):
    pre = nn(x_ref[...], wi_ref[...]) + tn(box_ref[...], wb_ref[...]) + bi_ref[...]
    pre_ref[...] = pre
    normed, _ = norm_parts(pre)
    encoded = (normed * gr_ref[...] + betar_ref[...]).astype(bf16)
    enc_ref[...] = nn(spread(pad, sent, x_ref.shape[0], enc_ref.shape[0]), encoded).astype(bf16)


def attention_forward(
    pad, sent, devices,
    captions, counts, offset,
    enc_ref, text_ref,
    wq_ref, wk_ref, wv_ref, wo_ref, bq_ref, bv_ref, bo_ref, g_ref, beta_ref,
    h_ref, q_ref, k_ref, v_ref, p_ref, c_ref, mixed_ref, n_ref,
):
    s = pl.program_id(0)
    text_len = text_ref.shape[0]
    rows, width = h_ref.shape
    hd = width // HEADS
    start = jnp.int32(0)
    for i in range(captions.shape[0]):
        start = start + jnp.where(s > i, counts[i], 0)
    slot = lax.broadcasted_iota(jnp.int32, (rows - text_len, 1), 0)
    taken = one_hot(
        slot + start, slot < counts[s], enc_ref.shape[0], pad, sent, devices, offset[0]
    )
    h_ref[:text_len, :] = text_ref[...]
    h_ref[text_len:, :] = nn(taken, enc_ref[...]).astype(bf16)
    h = h_ref[...]
    q = (nn(h, wq_ref[...]) + bq_ref[...]).astype(bf16)
    k = nn(h, wk_ref[...]).astype(bf16)
    v = (nn(h, wv_ref[...]) + bv_ref[...]).astype(bf16)
    q_ref[...] = q
    k_ref[...] = k
    v_ref[...] = v
    row = lax.broadcasted_iota(jnp.int32, (rows, 1), 0)
    live = (row < captions[s]) | ((row >= text_len) & (row < text_len + counts[s]))
    lane = lax.broadcasted_iota(jnp.int32, (1, 2 * hd), 1)
    masks = [(lane < hd).astype(bf16), (lane >= hd).astype(bf16)]
    scaled = q * jnp.asarray(hd**-0.5, bf16)
    for pair in range(HEADS // 2):
        cols = slice(pair * 2 * hd, (pair + 1) * 2 * hd)
        context = None
        for j in range(2):
            scores = nt(k[:, cols], scaled[:, cols] * masks[j])
            scores = jnp.where(live, scores, -1e30)
            top = jnp.max(scores, 0, keepdims=True)
            e = jnp.exp(scores - top)
            p = (e * (1.0 / jnp.sum(e, 0, keepdims=True))).astype(bf16)
            p_ref[0, 2 * pair + j] = p
            part = tn(p, v[:, cols] * masks[j])
            context = part if context is None else context + part
        c_ref[:, cols] = context.astype(bf16)
    mixed = h.astype(f32) + nn(c_ref[...], wo_ref[...]) + bo_ref[...]
    mixed_ref[...] = mixed
    normed, _ = norm_parts(mixed)
    n_ref[...] = (normed * g_ref[...] + beta_ref[...]).astype(bf16)


def image_backward(
    pad, sent, core_ref,
    x_ref, box_ref, wi_ref, pre_ref, back_ref, gr_ref, sums_ref, attn_sums_ref, bu_ref,
    gp_ref, gx_ref, away_ref, kept_ref, acc_ref,
):
    rows, feat = x_ref.shape
    width = pre_ref.shape[1]
    grad = tn(spread(pad, sent, rows, back_ref.shape[0]), back_ref[...])
    normed, inverse = norm_parts(pre_ref[...])
    gp = norm_back(grad, normed, inverse, gr_ref[...]).astype(bf16)
    gp_ref[...] = gp
    acc_ref[:feat, :] = tn(x_ref[...], gp)
    acc_ref[feat:, :] = jnp.zeros((acc_ref.shape[0] - feat, width), f32)
    acc_ref[feat : feat + box_ref.shape[0], :] = nn(box_ref[...], gp)
    at = feat + 8
    acc_ref[at : at + 1, :] = jnp.sum(gp.astype(f32), 0, keepdims=True)
    acc_ref[at + 1 : at + 2, :] = jnp.sum(grad * normed, 0, keepdims=True)
    acc_ref[at + 2 : at + 3, :] = jnp.sum(grad, 0, keepdims=True)
    acc_ref[at + 8 : at + 16, :] = sums_ref[...]
    acc_ref[at + 16 : at + 24, :] = attn_sums_ref[...]
    acc_ref[at + 24 : at + 24 + bu_ref.shape[0], :] = bu_ref[...]
    core = core_ref[0]
    pairs, chunk, _ = away_ref.shape
    for i in range(pairs):
        first = pl.multiple_of((2 * i + 1 - core) * chunk, 8)
        away_ref[i] = acc_ref[pl.ds(first, chunk), :].astype(bf16)
        first = pl.multiple_of((2 * i + core) * chunk, 8)
        kept_ref[i] = acc_ref[pl.ds(first, chunk), :].astype(bf16)
    gx_ref[...] = nt(gp, wi_ref[...]).astype(bf16)


def feed_forward(
    captions, counts, n_ref, mixed_ref, cot_ref, wd_ref, *refs,
):
    blocks = len(refs) - 17
    up_refs = refs[:blocks]
    wu_ref = refs[-1]

    @pl.when(pl.program_id(0) == 0)
    def _():
        for j in range(blocks):
            wu_ref[j] = up_refs[j][...].astype(f32).reshape(wu_ref.shape[1:]).astype(bf16)

    feed_forward_rows(captions, counts, n_ref, mixed_ref, cot_ref, wu_ref, wd_ref, *refs[blocks:-1])


def feed_forward_rows(
    captions, counts, n_ref, mixed_ref, cot_ref, wu_ref, wd_ref, wo_ref, bu_ref, bd_ref, g1_ref, g2_ref, beta2_ref,
    out_ref, act_ref, gdo_ref, gg_ref, gm_ref, ga_ref, gc_ref, sums_ref, bu_sum_ref, d_ref,
):
    s = pl.program_id(0)
    n1 = n_ref[...]
    rows, width = n1.shape
    ff = act_ref.shape[1]
    step = width
    per = wd_ref.shape[0] * step // ff

    def down_rows(j):
        return wd_ref[j // step * per : (j // step + 1) * per].reshape(step, width)

    @pl.when(s == 0)
    def _():
        sums_ref[...] = jnp.zeros_like(sums_ref)
        bu_sum_ref[...] = jnp.zeros_like(bu_sum_ref)

    second = n1.astype(f32) + bd_ref[...]
    for j in range(0, ff, step):
        cols = slice(j, j + step)
        gate = nn(n1, wu_ref[j // step]) + bu_ref[cols]
        act, d = gelu_parts(gate)
        act = act.astype(bf16)
        act_ref[:, cols] = act
        d_ref[:, cols] = d
        second = second + nn(act, down_rows(j))
    normed, inverse = norm_parts(second)
    text_len = rows // 2
    row = lax.broadcasted_iota(jnp.int32, (rows, 1), 0)
    live = (row < captions[s]) | ((row >= text_len) & (row < text_len + counts[s]))
    live = live.astype(f32)
    out_ref[...] = ((normed * g2_ref[...] + beta2_ref[...]) * live).astype(bf16)
    up = cot_ref[...].astype(f32) * live

    def add(i, value):
        sums_ref[i : i + 1, :] += jnp.sum(value, 0, keepdims=True)

    add(0, up * normed)
    add(1, up)
    gsi = norm_back(up, normed, inverse, g2_ref[...])
    gdo = gsi.astype(bf16)
    gdo_ref[...] = gdo
    add(2, gdo.astype(f32))
    first = gsi
    for j in range(0, ff, step):
        cols = slice(j, j + step)
        gg = (nt(gdo, down_rows(j)) * d_ref[:, cols]).astype(bf16)
        gg_ref[:, cols] = gg
        bu_sum_ref[:, cols] += jnp.sum(gg.astype(f32), 0, keepdims=True)
        first = first + nt(gg, wu_ref[j // step])
    normed, inverse = norm_parts(mixed_ref[...])
    add(3, first * normed)
    add(4, first)
    gm = norm_back(first, normed, inverse, g1_ref[...])
    gm_ref[...] = gm
    ga = gm.astype(bf16)
    ga_ref[...] = ga
    add(5, ga.astype(f32))
    gc_ref[...] = nt(ga, wo_ref[...]).astype(bf16)


def attention_backward(
    pad, sent, devices,
    counts, offset,
    q_ref, k_ref, v_ref, p_ref, gc_ref, gm_ref, wq_ref, wk_ref, wv_ref,
    gq_ref, gk_ref, gv_ref, gt_ref, gs_ref, sums_ref, acc_ref,
):
    s = pl.program_id(0)
    rows, width = q_ref.shape
    hd = width // HEADS
    scale = hd**-0.5

    @pl.when(s == 0)
    def _():
        sums_ref[...] = jnp.zeros_like(sums_ref)

    lane = lax.broadcasted_iota(jnp.int32, (1, 2 * hd), 1)
    masks = [(lane < hd).astype(bf16), (lane >= hd).astype(bf16)]
    for pair in range(HEADS // 2):
        cols = slice(pair * 2 * hd, (pair + 1) * 2 * hd)
        gq = gk = gv = None
        for j in range(2):
            p = p_ref[0, 2 * pair + j]
            gc = gc_ref[:, cols] * masks[j]
            gp = nt(v_ref[:, cols], gc)
            part = nn(p, gc)
            gv = part if gv is None else gv + part
            pf = p.astype(f32)
            weighted = pf * gp
            gs = (weighted - pf * jnp.sum(weighted, 0, keepdims=True)).astype(bf16)
            part = tn(gs, k_ref[:, cols] * masks[j])
            gq = part if gq is None else gq + part
            part = nn(gs, q_ref[:, cols] * masks[j])
            gk = part if gk is None else gk + part
        gq_ref[:, cols] = (gq * scale).astype(bf16)
        gk_ref[:, cols] = (gk * scale).astype(bf16)
        gv_ref[:, cols] = gv.astype(bf16)
    gq, gk, gv = gq_ref[...], gk_ref[...], gv_ref[...]
    sums_ref[0:1, :] += jnp.sum(gq.astype(f32), 0, keepdims=True)
    sums_ref[1:2, :] += jnp.sum(gv.astype(f32), 0, keepdims=True)
    hidden = gm_ref[...] + nt(gq, wq_ref[...]) + nt(gk, wk_ref[...]) + nt(gv, wv_ref[...])
    text_len = gt_ref.shape[0]
    gt_ref[...] = hidden[:text_len].astype(bf16)
    start = jnp.int32(0)
    for i in range(counts.shape[0]):
        start = start + jnp.where(s > i, counts[i], 0)
    slot = lax.broadcasted_iota(jnp.int32, (rows - text_len, 1), 0)
    taken = one_hot(
        slot + start, slot < counts[s], acc_ref.shape[0], pad, sent, devices, offset[0]
    )
    part = tn(taken, hidden[text_len:].astype(bf16))

    @pl.when(s == 0)
    def _():
        acc_ref[...] = part

    @pl.when(s > 0)
    def _():
        acc_ref[...] += part

    @pl.when(s == pl.num_programs(0) - 1)
    def _():
        gs_ref[...] = acc_ref[...].astype(bf16)


def whole(shape):
    return pl.BlockSpec(shape, lambda s, *_: (0,) * len(shape), pipeline_mode=pl.Buffered(1))


def tile(shape):
    return pl.BlockSpec(shape, lambda s, *_: (s,) + (0,) * (len(shape) - 1))


def still(shape):
    return pl.BlockSpec(shape, lambda s, *_: (0,) * len(shape))


LIMIT = 60 * 1024 * 1024


def cost(flops, moved, exps=0):
    return pl.CostEstimate(flops=int(flops), bytes_accessed=int(moved), transcendentals=int(exps))


def run_image_encode(geometry, x, boxes, wi, wb, bi, gr, betar):
    pad, sent, devices = geometry
    rows, feat = x.shape
    d = wi.shape[1]
    operands = (x, boxes, wi, wb, bi, gr, betar)
    shapes = [jax.ShapeDtypeStruct((rows, d), f32), jax.ShapeDtypeStruct((pad * devices, d), bf16)]
    return pl.pallas_call(
        functools.partial(image_encode, pad, sent),
        out_shape=shapes,
        compiler_params=pltpu.CompilerParams(vmem_limit_bytes=LIMIT),
        cost_estimate=cost(2 * rows * d * feat, x.size * 2 + wi.size * 2 + rows * d * 6),
        name="image_encode",
    )(*operands)


def run_attention_forward(
    geometry, captions, counts, offset, enc, text, wq, wk, wv, wo, bq, bv, bo, g1, beta1
):
    seqs = captions.shape[0]
    text_rows, d = text.shape
    total = 2 * text_rows
    L = total // seqs
    row = tile((L, d))
    vec = whole((d,))
    mat = whole((d, d))
    shapes = (
        [jax.ShapeDtypeStruct((total, d), bf16)] * 4
        + [
            jax.ShapeDtypeStruct((seqs, HEADS, L, L), bf16),
            jax.ShapeDtypeStruct((total, d), bf16),
            jax.ShapeDtypeStruct((total, d), f32),
            jax.ShapeDtypeStruct((total, d), bf16),
        ]
    )
    return pl.pallas_call(
        functools.partial(attention_forward, *geometry),
        out_shape=shapes,
        grid_spec=pltpu.PrefetchScalarGridSpec(
            num_scalar_prefetch=3,
            grid=(seqs,),
            in_specs=[whole(enc.shape), tile((L // 2, d))] + [mat] * 4 + [vec] * 5,
            out_specs=[row] * 4 + [tile((1, HEADS, L, L))] + [row] * 3,
        ),
        compiler_params=pltpu.CompilerParams(
            dimension_semantics=("arbitrary",), vmem_limit_bytes=LIMIT
        ),
        cost_estimate=cost(
            2 * total * d * (4 * d + 2 * L * 4),
            total * d * 18 + seqs * HEADS * L * L * 2,
            seqs * HEADS * L * L,
        ),
        name="attention_forward",
    )(
        captions, counts, offset, enc, text,
        wq, wk, wv, wo, bq, bv, bo, g1, beta1,
    )


def run_image_backward(geometry, chunk, core, x, boxes, wi, pre, back, gr, sums, attn_sums, bu):
    pad, sent, devices = geometry
    rows, feat = x.shape
    d = pre.shape[1]
    half = jax.ShapeDtypeStruct((devices // 2, chunk, d), bf16)
    operands = (x, boxes, wi, pre, back, gr, sums, attn_sums, bu)
    return pl.pallas_call(
        functools.partial(image_backward, pad, sent),
        out_shape=[
            jax.ShapeDtypeStruct((rows, d), bf16),
            jax.ShapeDtypeStruct((rows, feat), bf16),
            half,
            half,
        ],
        grid_spec=pltpu.PrefetchScalarGridSpec(
            num_scalar_prefetch=1,
            grid=(1,),
            in_specs=[whole(o.shape) for o in operands],
            out_specs=[whole((rows, d)), whole((rows, feat)), whole(half.shape), whole(half.shape)],
            scratch_shapes=[pltpu.VMEM((devices * chunk, d), f32)],
        ),
        compiler_params=pltpu.CompilerParams(
            dimension_semantics=("arbitrary",), vmem_limit_bytes=LIMIT
        ),
        cost_estimate=cost(4 * rows * d * feat, x.size * 4 + wi.size * 2 + devices * chunk * d * 2),
        name="image_backward",
    )(core, *operands)


def join_kernel(core_ref, *refs):
    core = core_ref[0]
    out_ref = refs[-1]
    groups = list(zip(refs[:-1:2], refs[1:-1:2]))
    at = 0
    for i in range(groups[0][0].shape[0]):
        for first in (0, 1):
            for own_ref, came_ref in groups:
                own, came = own_ref[i].astype(f32), came_ref[i].astype(f32)
                rows = own.shape[0]
                out_ref[at : at + rows, :] = jnp.where(core == first, own, came)
                at += rows


def join_square(core, halves, index):
    width = halves[0].shape[2]
    per = width // (2 * sum(t.shape[1] for t in halves[::2]))
    return pl.pallas_call(
        join_kernel,
        out_shape=jax.ShapeDtypeStruct((width, width), f32),
        grid_spec=pltpu.PrefetchScalarGridSpec(
            num_scalar_prefetch=1,
            grid=(1,),
            in_specs=[
                pl.BlockSpec((per,) + t.shape[1:], lambda s, *_: (index, 0, 0)) for t in halves
            ],
            out_specs=pl.BlockSpec((width, width), lambda s, *_: (0, 0)),
        ),
        cost_estimate=cost(0, width * width * 8),
        name="join_square",
    )(core, *halves)


def join_image_kernel(feat, core_ref, *refs):
    out_ref, small_ref, acc_ref = refs[-3:]
    join_kernel(core_ref, *refs[:-3], acc_ref)
    out_ref[...] = acc_ref[:feat, :]
    small_ref[...] = acc_ref[feat : feat + small_ref.shape[0], :]


def join_image(core, halves, feat, small_rows):
    width = halves[0].shape[2]
    rows = sum(t.shape[0] * t.shape[1] for t in halves)
    return pl.pallas_call(
        functools.partial(join_image_kernel, feat),
        out_shape=[
            jax.ShapeDtypeStruct((feat, width), f32),
            jax.ShapeDtypeStruct((small_rows, width), f32),
        ],
        grid_spec=pltpu.PrefetchScalarGridSpec(
            num_scalar_prefetch=1,
            grid=(1,),
            in_specs=[whole(t.shape) for t in halves],
            out_specs=[whole((feat, width)), whole((small_rows, width))],
            scratch_shapes=[pltpu.VMEM((rows, width), f32)],
        ),
        compiler_params=pltpu.CompilerParams(vmem_limit_bytes=LIMIT),
        cost_estimate=cost(0, feat * width * 8),
        name="join_image",
    )(core, *halves)


def widen_ff_kernel(down_in, up_in, down_ref, up_ref):
    down_ref[...] = down_in[...].reshape(down_ref.shape).astype(f32)
    up_ref[...] = up_in[...].reshape(up_ref.shape).astype(f32)


def widen_ff(parts, width, blocks):
    devices, rows, _ = parts.shape
    per = devices // blocks
    return pl.pallas_call(
        widen_ff_kernel,
        out_shape=[
            jax.ShapeDtypeStruct((blocks * width, width), f32),
            jax.ShapeDtypeStruct((width, blocks * width), f32),
        ],
        grid=(blocks,),
        in_specs=[
            pl.BlockSpec((per, rows // 2, width), lambda t: (t, 0, 0)),
            pl.BlockSpec((per, rows // 2, width), lambda t: (t, 1, 0)),
        ],
        out_specs=[
            pl.BlockSpec((width, width), lambda t: (t, 0)),
            pl.BlockSpec((width, width), lambda t: (0, t)),
        ],
        cost_estimate=cost(0, parts.size * 6),
        name="widen_ff",
    )(parts, parts)


def run_feed_forward(captions, counts, n1, mixed, cot, weights, cut, wo, bu, bd, g1, g2, beta2):
    seqs = captions.shape[0]
    total, d = n1.shape
    devices = weights.shape[0]
    down = weights.shape[1] // 2
    ff = devices * down
    blocks = ff // d

    def part(rows, index):
        return pl.BlockSpec(
            (devices, rows, d), lambda s, *_: (0, index, 0), pipeline_mode=pl.Buffered(1)
        )

    if cut % 8 == 0:
        ups = [part(cut, blocks + j) for j in range(blocks)]
        up_weights = [weights] * blocks
    else:
        ups = [whole((d, d))] * blocks
        up_weights = [
            weights[:, down + j * cut : down + (j + 1) * cut].reshape(d, d) for j in range(blocks)
        ]

    L = total // seqs
    row = tile((L, d))
    wide = tile((L, ff))
    vec = whole((d,))
    shapes = [
        jax.ShapeDtypeStruct((total, d), bf16),
        jax.ShapeDtypeStruct((total, ff), bf16),
        jax.ShapeDtypeStruct((total, d), bf16),
        jax.ShapeDtypeStruct((total, ff), bf16),
        jax.ShapeDtypeStruct((total, d), f32),
        jax.ShapeDtypeStruct((total, d), bf16),
        jax.ShapeDtypeStruct((total, d), bf16),
        jax.ShapeDtypeStruct((8, d), f32),
        jax.ShapeDtypeStruct((1, ff), f32),
    ]
    return pl.pallas_call(
        feed_forward,
        out_shape=shapes,
        grid_spec=pltpu.PrefetchScalarGridSpec(
            num_scalar_prefetch=2,
            grid=(seqs,),
            in_specs=[row, row, row, part(down, 0)]
            + ups
            + [whole((d, d)), whole((ff,)), vec, vec, vec, vec],
            out_specs=[row, wide, row, wide, row, row, row, still((8, d)), still((1, ff))],
            scratch_shapes=[pltpu.VMEM((L, ff), f32), pltpu.VMEM((blocks, d, d), bf16)],
        ),
        compiler_params=pltpu.CompilerParams(
            dimension_semantics=("arbitrary",), vmem_limit_bytes=LIMIT
        ),
        cost_estimate=cost(2 * total * d * (4 * ff + d), total * (ff * 4 + d * 18) + d * ff * 4, total * ff),
        name="feed_forward",
    )(captions, counts, n1, mixed, cot, weights, *up_weights, wo, bu, bd, g1, g2, beta2)


def run_attention_backward(geometry, counts, offset, q, k, v, p, gc, gm, wq, wk, wv):
    seqs, _, L, _ = p.shape
    total, d = q.shape
    row = tile((L, d))
    half = tile((L // 2, d))
    mat = whole((d, d))
    received = geometry[0] * geometry[2]
    shapes = [jax.ShapeDtypeStruct((total, d), bf16)] * 3 + [
        jax.ShapeDtypeStruct((total // 2, d), bf16),
        jax.ShapeDtypeStruct((received, d), bf16),
        jax.ShapeDtypeStruct((8, d), f32),
    ]
    return pl.pallas_call(
        functools.partial(attention_backward, *geometry),
        out_shape=shapes,
        grid_spec=pltpu.PrefetchScalarGridSpec(
            num_scalar_prefetch=2,
            grid=(seqs,),
            in_specs=[row, row, row, tile((1, HEADS, L, L)), row, row, mat, mat, mat],
            out_specs=[row, row, row, half, still((received, d)), still((8, d))],
            scratch_shapes=[pltpu.VMEM((received, d), f32)],
        ),
        compiler_params=pltpu.CompilerParams(
            dimension_semantics=("arbitrary",), vmem_limit_bytes=LIMIT
        ),
        cost_estimate=cost(2 * total * d * (3 * d + 4 * L * 4), total * d * 20 + seqs * HEADS * L * L * 2),
        name="attention_backward",
    )(counts, offset, q, k, v, p, gc, gm, wq, wk, wv)


def weight_grad_kernel(lhs_of, rhs_of, core_ref, *refs):
    lhs_refs = refs[: max(lhs_of) + 1]
    rhs_refs = refs[len(lhs_refs) : len(lhs_refs) + max(rhs_of) + 1]
    away_ref, kept_ref, acc_ref = refs[-3:]
    step = pl.program_id(0)
    core = core_ref[0]
    pairs = away_ref.shape[0]
    kinds = {}
    for i, kind in enumerate(zip(lhs_of, rhs_of)):
        kinds.setdefault(kind, []).append(i)
    for (a, b), steps in kinds.items():

        @pl.when((step >= steps[0]) & (step <= steps[-1]))
        def _(a=a, b=b):
            value = tn(lhs_refs[a][...], rhs_refs[b][...]).astype(bf16)
            acc_ref[...] = value.reshape(acc_ref.shape)

    for i in range(pairs):
        away_ref[i] = acc_ref[2 * i + 1 - core]
        kept_ref[i] = acc_ref[2 * i + core]


def weight_grads(core, devices, lhs, rhs, lhs_of, rhs_of, lhs_maps, rhs_maps, out_width, name):
    steps = len(lhs_of)
    total = lhs[0].shape[0]
    width = out_width
    rows = steps * width // devices
    per = width // rows
    half = jax.ShapeDtypeStruct((devices // 2, rows, width), bf16)
    out = pl.BlockSpec((per // 2, rows, width), lambda s, *_: (s, 0, 0))
    specs = [pl.BlockSpec((total, width), m) for m in lhs_maps + rhs_maps]
    return pl.pallas_call(
        functools.partial(weight_grad_kernel, lhs_of, rhs_of),
        out_shape=[half, half],
        grid_spec=pltpu.PrefetchScalarGridSpec(
            num_scalar_prefetch=1,
            grid=(steps,),
            in_specs=specs,
            out_specs=[out, out],
            scratch_shapes=[pltpu.VMEM((per, rows, width), bf16)],
        ),
        compiler_params=pltpu.CompilerParams(
            dimension_semantics=("arbitrary",), vmem_limit_bytes=LIMIT
        ),
        cost_estimate=cost(2 * total * width * width * steps, steps * width * (total + width) * 2),
        name=name,
    )(core, *lhs, *rhs)


def axis_bits(name):
    size = lax.axis_size(name)
    bits = []
    step = 1
    while step < size:
        bits.append((name, step))
        step *= 2
    return bits


def bit_layout():
    return axis_bits("enc")[::-1] + axis_bits("dp")[::-1]


def my_bit(bit):
    return (lax.axis_index(bit[0]) // bit[1]) % 2


def swap_bit(tensor, bit):
    name, step = bit
    size = lax.axis_size(name)
    return lax.ppermute(tensor, name, [(i, i ^ step) for i in range(size)])


def stage_orders():
    dp_bits, enc_bits = axis_bits("dp"), axis_bits("enc")
    near, middle = dp_bits[:1], dp_bits[1:]
    half = len(middle) // 2
    return (
        near + middle + enc_bits,
        near + middle[half:] + middle[:half] + enc_bits,
    )


def add_low(kept, came):
    return (kept.astype(f32) + came.astype(f32)).astype(bf16)


class Scatter:
    def __init__(self, away, kept, order):
        self.order = list(order)
        self.layout = bit_layout()
        self.value = (away, kept)
        self.fresh = True

    def stage(self):
        bit = self.order.pop(0)
        axis = self.layout.index(bit)
        self.layout.remove(bit)
        if self.fresh:
            away, kept = self.value
            self.fresh = False
        else:
            mine = my_bit(bit)
            away, kept = [
                add_low(*[lax.dynamic_index_in_dim(t, i, axis, keepdims=False) for t in self.value])
                for i in (1 - mine, mine)
            ]
        shape = (2,) * len(self.layout) + kept.shape[-2:]
        self.value = (kept.reshape(shape), swap_bit(away, bit).reshape(shape))
        return away

    def total(self):
        return add_low(*self.value)

    def split(self, at, orders):
        parts = []
        for rows, order in zip((slice(None, at), slice(at, None)), orders):
            part = Scatter(*[t[..., rows, :] for t in self.value], ())
            part.order = [b for b in order if b in self.layout]
            part.layout = list(self.layout)
            part.fresh = False
            parts.append(part)
        return parts

    def merge(self, parts):
        self.value = tuple(jnp.concatenate(t, -2) for t in zip(*[p.value for p in parts]))
        self.layout = list(parts[0].layout)
        self.order = list(parts[0].order)


class Gather:
    def __init__(self, rows, order, layout=()):
        self.order = list(order)[::-1]
        self.layout = list(layout)
        self.value = rows

    def stage(self):
        bit = self.order.pop(0)
        sent = self.value
        came = swap_bit(sent, bit)
        self.layout = [b for b in bit_layout() if b in self.layout or b == bit]
        axis = self.layout.index(bit)
        shape = sent.shape[:axis] + (2,) + sent.shape[axis:]
        at = lax.broadcasted_iota(jnp.int32, shape, axis)
        self.value = jnp.where(
            at == my_bit(bit), jnp.expand_dims(sent, axis), jnp.expand_dims(came, axis)
        )
        return sent

    def rows(self):
        return self.value.reshape((-1,) + self.value.shape[-2:])

    def halves(self):
        (bit,) = self.order
        came = swap_bit(self.value, bit)
        shape = (-1,) + came.shape[-2:]
        return self.value.reshape(shape), came.reshape(shape)

    def split(self, at, orders):
        values = (self.value[..., :at, :], self.value[..., at:, :])
        return [
            Gather(value, [b for b in order if b not in self.layout], self.layout)
            for value, order in zip(values, orders)
        ]


def fence(movers, *values):
    leaves, tree = jax.tree.flatten(([m.value for m in movers], values))
    held, values = jax.tree.unflatten(tree, lax.optimization_barrier(leaves))
    for mover, value in zip(movers, held):
        mover.value = value
    return values


class Sum:
    def __init__(self, away, kept, orders):
        self.movers = [Scatter(away, kept, orders[0])]
        self.orders = orders
        self.at = 8 * (-(-away.shape[1] // 16))
        far = len(axis_bits("enc"))
        middle = len(orders[0]) - 1 - far
        self.steps = (
            [self.near]
            + [self.run] * middle
            + [self.far]
            + [self.run] * (far - 1)
            + [self.turn]
            + [self.run] * (far - 1)
            + [self.part]
            + [self.run] * (middle - 1)
        )

    @property
    def value(self):
        return [m.value for m in self.movers]

    @value.setter
    def value(self, values):
        for mover, value in zip(self.movers, values):
            mover.value = value

    def stage(self):
        self.steps.pop(0)()

    def run(self):
        for mover in self.movers:
            mover.stage()

    def near(self):
        self.run()
        self.whole = self.movers[0]
        self.movers = self.whole.split(self.at, self.orders)

    def far(self):
        self.whole.merge(self.movers)
        self.movers = [self.whole]
        self.run()

    def turn(self):
        self.movers = [Gather(self.whole.total(), axis_bits("enc"))]
        self.run()

    def part(self):
        self.movers = self.movers[0].split(self.at, self.orders)
        self.run()

    def halves(self):
        return [t for mover in self.movers for t in mover.halves()]


def body(
    text,
    region_feats,
    boxes,
    caption_count,
    region_count,
    region_offset,
    w_img,
    w_box,
    b_img,
    g_reg,
    beta_reg,
    w_query,
    b_query,
    w_key,
    w_value,
    b_value,
    w_out,
    b_out,
    g_one,
    beta_one,
    w_up,
    b_up,
    w_down,
    b_down,
    g_two,
    beta_two,
    cotangent,
):
    axes = ("enc", "dp")
    orders = stage_orders()
    model_width = text.shape[1]
    ff_blocks = w_up.shape[1] // model_width
    cut = w_query.shape[0]
    far = axis_bits("enc")

    middle = len(orders[0]) - 1 - len(far)
    core = (lax.axis_index("dp") % 2).astype(jnp.int32).reshape(1)

    up_blocks = w_up.reshape(cut, ff_blocks, model_width).transpose(1, 0, 2)
    ff_shard = jnp.concatenate([w_down, up_blocks.reshape(ff_blocks * cut, model_width)], 0)
    ff_weights = lax.all_gather(ff_shard, axes, axis=0)
    rows_up = cut
    img = Gather(w_img, far)
    attn = Gather(jnp.concatenate([w_query, w_key, w_value, w_out], 0), far)
    img.stage()
    fence([img, attn])
    while img.order:
        img.stage()
        attn.stage()
        fence([img, attn])
    img = img.split(w_img.shape[0] // 2, orders)
    attn.stage()
    for _ in range(middle):
        for part in img:
            part.stage()
        fence([*img, attn])
    attn = attn.split(2 * cut, orders)
    for part in (*img, *attn):
        part.stage()
    img_full = jnp.concatenate([t.rows() for t in img], 1).reshape(-1, model_width)
    device_count = lax.axis_size(axes)
    seq_count = caption_count.shape[0]
    sent_rows, feat = region_feats.shape
    per_peer = sent_rows // device_count
    pad = 8 * (-(-per_peer // 8))
    pad = 1 << (pad - 1).bit_length()
    box_count = boxes.shape[0]
    geometry = (pad, per_peer, device_count)
    pre_norm, encoded = run_image_encode(
        geometry, region_feats, boxes, img_full, w_box, b_img, g_reg, beta_reg
    )
    (encoded,) = fence(attn, encoded)
    received = lax.all_to_all(encoded, axes, split_axis=0, concat_axis=0, tiled=True)
    for _ in range(middle - 1):
        for part in attn:
            part.stage()
        (received,) = fence(attn, received)
    for part in attn:
        part.stage()
    query_full, key_full, value_full, out_full = [
        t.reshape(-1, model_width)
        for part in attn
        for t in (part.rows()[:, :cut], part.rows()[:, cut:])
    ]
    (
        hidden_in,
        queries,
        keys,
        values,
        probs,
        context,
        mixed,
        normed_one,
    ) = run_attention_forward(
        geometry,
        caption_count,
        region_count,
        region_offset,
        received,
        text,
        query_full,
        key_full,
        value_full,
        out_full,
        b_query,
        b_value,
        b_out,
        g_one,
        beta_one,
    )
    (
        output,
        activated,
        grad_down_out,
        grad_gate,
        grad_mixed,
        grad_attn,
        grad_context,
        sums,
        grad_b_up,
    ) = run_feed_forward(
        caption_count,
        region_count,
        normed_one,
        mixed,
        cotangent,
        ff_weights,
        rows_up,
        out_full,
        b_up,
        b_down,
        g_one,
        g_two,
        beta_two,
    )
    fixed = lambda s, *_: (0, 0)
    moving = lambda s, *_: (0, s)
    down_away, down_kept = weight_grads(
        core,
        device_count,
        [activated],
        [grad_down_out],
        [0] * ff_blocks,
        [0] * ff_blocks,
        [moving],
        [fixed],
        model_width,
        "grad_w_down",
    )
    up_away, up_kept = weight_grads(
        core,
        device_count,
        [normed_one],
        [grad_gate],
        [0] * ff_blocks,
        [0] * ff_blocks,
        [fixed],
        [moving],
        model_width,
        "grad_w_up",
    )
    down = Scatter(down_away, down_kept, orders[0])
    up = Scatter(up_away, up_kept, orders[1])
    down.stage()
    up.stage()
    (grad_context,) = fence([down, up], grad_context)
    down.stage()
    up.stage()
    grad_query, grad_keys, grad_values, grad_text, grad_slots, attn_sums = run_attention_backward(
        geometry,
        region_count,
        region_offset,
        queries,
        keys,
        values,
        probs,
        grad_context,
        grad_mixed,
        query_full,
        key_full,
        value_full,
    )
    grad_query, grad_keys, grad_values, grad_slots, attn_sums = fence(
        [down, up], grad_query, grad_keys, grad_values, grad_slots, attn_sums
    )
    back = lax.all_to_all(grad_slots, axes, split_axis=0, concat_axis=0, tiled=True)
    down.stage()
    up.stage()
    attn_away, attn_kept = weight_grads(
        core,
        device_count,
        [hidden_in, context],
        [grad_query, grad_keys, grad_values, grad_attn],
        [0, 0, 0, 1],
        [0, 1, 2, 3],
        [fixed] * 2,
        [fixed] * 4,
        model_width,
        "grad_w_attn",
    )
    attn = Sum(attn_away, attn_kept, orders)
    (back,) = fence([down, up, attn], back)
    while len(down.order) > len(far):
        down.stage()
        up.stage()
        fence([down, up])
    down.stage()
    up.stage()
    attn.stage()
    small_rows = 40
    chunk = 8 * (-(-(feat + small_rows) // (8 * device_count)))
    grad_pre, grad_feats, img_away, img_kept = run_image_backward(
        geometry,
        chunk,
        core,
        region_feats,
        boxes,
        img_full,
        pre_norm,
        back,
        g_reg,
        sums,
        attn_sums,
        grad_b_up.reshape(ff_blocks, model_width),
    )
    img = Sum(img_away, img_kept, orders)
    fence([down, up, attn, img])
    while down.order:
        down.stage()
        up.stage()
        if not down.order:
            attn.stage()
            img.stage()
        fence([down, up, attn, img])
    ff_shard = jnp.concatenate([down.total(), up.total()], 0)
    ff_all = lax.all_gather(ff_shard, axes, axis=0)
    while attn.steps:
        attn.stage()
        img.stage()
        if len(attn.steps) == 0:
            grad_w_down, grad_w_up = widen_ff(ff_all, model_width, ff_blocks)
            grad_w_down, grad_w_up = fence([attn, img], grad_w_down, grad_w_up)
        else:
            fence([attn, img])
    attn_halves = attn.halves()
    img.stage()
    fence([img], *attn_halves)
    img_halves = img.halves()
    grad_w_query, grad_w_key, grad_w_value, grad_w_out = [
        join_square(core, attn_halves, j) for j in range(4)
    ]
    grad_boxes = jnp.einsum("cd,rd->cr", w_box, grad_pre, preferred_element_type=f32).astype(bf16)
    grad_w_img, small = join_image(core, img_halves, feat, small_rows)
    grad_w_box = small[:box_count]
    grad_b_img, grad_g_reg, grad_beta_reg = [small[8 + i] for i in range(3)]
    grad_g_two, grad_beta_two, grad_b_down, grad_g_one, grad_beta_one, grad_b_out = [
        small[16 + i] for i in range(6)
    ]
    grad_b_query, grad_b_value = small[24], small[25]
    grad_b_up = small[32 : 32 + ff_blocks].reshape(-1)
    return (
        output,
        grad_text,
        grad_feats,
        grad_boxes,
        grad_w_img,
        grad_w_box,
        grad_b_img,
        grad_g_reg,
        grad_beta_reg,
        grad_w_query,
        grad_b_query,
        grad_w_key,
        grad_w_value,
        grad_b_value,
        grad_w_out,
        grad_b_out,
        grad_g_one,
        grad_beta_one,
        grad_w_up,
        grad_b_up,
        grad_w_down,
        grad_b_down,
        grad_g_two,
        grad_beta_two,
    )


def solution(mesh):
    return jax.shard_map(
        body,
        mesh=mesh,
        in_specs=(
            P(("enc", "dp"), None),
            P(("enc", "dp"), None),
            P(None, ("enc", "dp")),
            P(("enc", "dp")),
            P(("enc", "dp")),
            P(("enc", "dp")),
            P(("enc", "dp"), None),
            P(),
            P(),
            P(),
            P(),
            P(("enc", "dp"), None),
            P(),
            P(("enc", "dp"), None),
            P(("enc", "dp"), None),
            P(),
            P(("enc", "dp"), None),
            P(),
            P(),
            P(),
            P(("enc", "dp"), None),
            P(),
            P(("enc", "dp"), None),
            P(),
            P(),
            P(),
            P(("enc", "dp"), None),
        ),
        out_specs=(
            P(("enc", "dp"), None),
            P(("enc", "dp"), None),
            P(("enc", "dp"), None),
            P(None, ("enc", "dp")),
            P(),
            P(),
            P(),
            P(),
            P(),
            P(),
            P(),
            P(),
            P(),
            P(),
            P(),
            P(),
            P(),
            P(),
            P(),
            P(),
            P(),
            P(),
            P(),
            P(),
        ),
        check_vma=False,
    )
```

```python
import functools
import math

import jax
import jax.numpy as jnp
from jax import lax
from jax.experimental import pallas as pl
from jax.experimental.pallas import tpu as pltpu
from jax.sharding import PartitionSpec as P

HEADS = 12
epsilon = 1e-05
f32, bf16 = jnp.float32, jnp.bfloat16

ERFC_P = 0.35
ERFC_C = (
    0.19567911,
    0.22612264,
    0.02080242,
    0.63768037,
    -0.6386366,
    0.75239514,
    -0.19404308,
)


def nn(a, b):
    return lax.dot_general(a, b, (((1,), (0,)), ((), ())), preferred_element_type=f32)


def nt(a, b):
    return lax.dot_general(a, b, (((1,), (1,)), ((), ())), preferred_element_type=f32)


def tn(a, b):
    return lax.dot_general(a, b, (((0,), (0,)), ((), ())), preferred_element_type=f32)


def norm_parts(values):
    centered = values - jnp.mean(values, -1, keepdims=True)
    inverse = lax.rsqrt(jnp.mean(centered * centered, -1, keepdims=True) + epsilon)
    return centered * inverse, inverse


def norm_back(upstream, normed, inverse, gain):
    weighted = upstream * gain
    return inverse * (
        weighted
        - jnp.mean(weighted, -1, keepdims=True)
        - normed * jnp.mean(weighted * normed, -1, keepdims=True)
    )


def gelu_parts(x):
    e = jnp.exp(-0.5 * x * x)
    t = 1.0 / (1.0 + (ERFC_P * math.sqrt(0.5)) * jnp.abs(x))
    acc = jnp.full_like(t, 0.5 * ERFC_C[-1])
    for c in ERFC_C[-2::-1]:
        acc = acc * t + 0.5 * c
    tail = acc * t * e
    phi = jnp.where(x >= 0, 1.0 - tail, tail)
    return x * phi, phi + x * (e * (1.0 / math.sqrt(2.0 * math.pi)))


def one_hot(wanted, live, rows, pad, sent, devices, offset):
    row = lax.broadcasted_iota(jnp.int32, (1, rows), 1)
    shift = pad.bit_length() - 1
    turn = lax.shift_right_logical(row, shift) - offset
    turn = jnp.where(turn < 0, turn + devices, turn)
    inside = jnp.bitwise_and(row, pad - 1)
    arrival = jnp.where(inside < sent, inside * devices + turn, -1)
    return ((wanted == arrival) & live).astype(bf16)


def spread(pad, sent, rows, padded):
    to = lax.broadcasted_iota(jnp.int32, (padded, 1), 0)
    shift = pad.bit_length() - 1
    inside = jnp.bitwise_and(to, pad - 1)
    source = jnp.where(inside < sent, lax.shift_right_logical(to, shift) * sent + inside, -1)
    return (source == lax.broadcasted_iota(jnp.int32, (1, rows), 1)).astype(bf16)


def image_encode(
    pad, sent, x_ref, box_ref, wi_ref, wb_ref, bi_ref, gr_ref, betar_ref, pre_ref, enc_ref
):
    pre = nn(x_ref[...], wi_ref[...]) + tn(box_ref[...], wb_ref[...]) + bi_ref[...]
    pre_ref[...] = pre
    normed, _ = norm_parts(pre)
    encoded = (normed * gr_ref[...] + betar_ref[...]).astype(bf16)
    enc_ref[...] = nn(spread(pad, sent, x_ref.shape[0], enc_ref.shape[0]), encoded).astype(bf16)


def attention_forward(
    pad, sent, devices,
    captions, counts, offset,
    enc_ref, text_ref,
    wq_ref, wk_ref, wv_ref, wo_ref, bq_ref, bv_ref, bo_ref, g_ref, beta_ref,
    h_ref, q_ref, k_ref, v_ref, p_ref, c_ref, mixed_ref, n_ref,
):
    s = pl.program_id(0)
    text_len = text_ref.shape[0]
    rows, width = h_ref.shape
    hd = width // HEADS
    start = jnp.int32(0)
    for i in range(captions.shape[0]):
        start = start + jnp.where(s > i, counts[i], 0)
    slot = lax.broadcasted_iota(jnp.int32, (rows - text_len, 1), 0)
    taken = one_hot(
        slot + start, slot < counts[s], enc_ref.shape[0], pad, sent, devices, offset[0]
    )
    h_ref[:text_len, :] = text_ref[...]
    h_ref[text_len:, :] = nn(taken, enc_ref[...]).astype(bf16)
    h = h_ref[...]
    q = (nn(h, wq_ref[...]) + bq_ref[...]).astype(bf16)
    k = nn(h, wk_ref[...]).astype(bf16)
    v = (nn(h, wv_ref[...]) + bv_ref[...]).astype(bf16)
    q_ref[...] = q
    k_ref[...] = k
    v_ref[...] = v
    row = lax.broadcasted_iota(jnp.int32, (rows, 1), 0)
    live = (row < captions[s]) | ((row >= text_len) & (row < text_len + counts[s]))
    lane = lax.broadcasted_iota(jnp.int32, (1, 2 * hd), 1)
    masks = [(lane < hd).astype(bf16), (lane >= hd).astype(bf16)]
    scaled = q * jnp.asarray(hd**-0.5, bf16)
    for pair in range(HEADS // 2):
        cols = slice(pair * 2 * hd, (pair + 1) * 2 * hd)
        context = None
        for j in range(2):
            scores = nt(k[:, cols], scaled[:, cols] * masks[j])
            scores = jnp.where(live, scores, -1e30)
            top = jnp.max(scores, 0, keepdims=True)
            e = jnp.exp(scores - top)
            p = (e * (1.0 / jnp.sum(e, 0, keepdims=True))).astype(bf16)
            p_ref[0, 2 * pair + j] = p
            part = tn(p, v[:, cols] * masks[j])
            context = part if context is None else context + part
        c_ref[:, cols] = context.astype(bf16)
    mixed = h.astype(f32) + nn(c_ref[...], wo_ref[...]) + bo_ref[...]
    mixed_ref[...] = mixed
    normed, _ = norm_parts(mixed)
    n_ref[...] = (normed * g_ref[...] + beta_ref[...]).astype(bf16)


def image_backward(
    pad, sent, core_ref,
    x_ref, box_ref, wi_ref, pre_ref, back_ref, gr_ref, sums_ref, attn_sums_ref, bu_ref,
    gp_ref, gx_ref, *outs,
):
    *outs, acc_ref = outs
    rows, feat = x_ref.shape
    width = pre_ref.shape[1]
    grad = tn(spread(pad, sent, rows, back_ref.shape[0]), back_ref[...])
    normed, inverse = norm_parts(pre_ref[...])
    gp = norm_back(grad, normed, inverse, gr_ref[...]).astype(bf16)
    gp_ref[...] = gp
    acc_ref[:feat, :] = tn(x_ref[...], gp)
    acc_ref[feat:, :] = jnp.zeros((acc_ref.shape[0] - feat, width), f32)
    acc_ref[feat : feat + box_ref.shape[0], :] = nn(box_ref[...], gp)
    at = feat + 8
    acc_ref[at : at + 1, :] = jnp.sum(gp.astype(f32), 0, keepdims=True)
    acc_ref[at + 1 : at + 2, :] = jnp.sum(grad * normed, 0, keepdims=True)
    acc_ref[at + 2 : at + 3, :] = jnp.sum(grad, 0, keepdims=True)
    acc_ref[at + 8 : at + 16, :] = sums_ref[...]
    acc_ref[at + 16 : at + 24, :] = attn_sums_ref[...]
    acc_ref[at + 24 : at + 24 + bu_ref.shape[0], :] = bu_ref[...]
    core = core_ref[0]
    half = len(outs) // 2
    chunk = sum(ref.shape[1] for ref in outs[:half])
    for i in range(outs[0].shape[0]):
        for side in (0, 1):
            at = (2 * i + (1 - core if side == 0 else core)) * chunk
            for ref in outs[side * half : (side + 1) * half]:
                rows_here = ref.shape[1]
                ref[i] = acc_ref[pl.ds(pl.multiple_of(at, 8), rows_here), :].astype(bf16)
                at = at + rows_here
    gx_ref[...] = nt(gp, wi_ref[...]).astype(bf16)


def feed_forward(
    captions, counts, n_ref, mixed_ref, cot_ref, wd_ref, *refs,
):
    blocks = len(refs) - 17
    up_refs = refs[:blocks]
    wu_ref = refs[-1]

    @pl.when(pl.program_id(0) == 0)
    def _():
        for j in range(blocks):
            wu_ref[j] = up_refs[j][...].astype(f32).reshape(wu_ref.shape[1:]).astype(bf16)

    feed_forward_rows(captions, counts, n_ref, mixed_ref, cot_ref, wu_ref, wd_ref, *refs[blocks:-1])


def feed_forward_rows(
    captions, counts, n_ref, mixed_ref, cot_ref, wu_ref, wd_ref, wo_ref, bu_ref, bd_ref, g1_ref, g2_ref, beta2_ref,
    out_ref, act_ref, gdo_ref, gg_ref, gm_ref, ga_ref, gc_ref, sums_ref, bu_sum_ref, d_ref,
):
    s = pl.program_id(0)
    n1 = n_ref[...]
    rows, width = n1.shape
    ff = act_ref.shape[1]
    step = width
    per = wd_ref.shape[0] * step // ff

    def down_rows(j):
        return wd_ref[j // step * per : (j // step + 1) * per].reshape(step, width)

    @pl.when(s == 0)
    def _():
        sums_ref[...] = jnp.zeros_like(sums_ref)
        bu_sum_ref[...] = jnp.zeros_like(bu_sum_ref)

    second = n1.astype(f32) + bd_ref[...]
    for j in range(0, ff, step):
        cols = slice(j, j + step)
        gate = nn(n1, wu_ref[j // step]) + bu_ref[cols]
        act, d = gelu_parts(gate)
        act = act.astype(bf16)
        act_ref[:, cols] = act
        d_ref[:, cols] = d
        second = second + nn(act, down_rows(j))
    normed, inverse = norm_parts(second)
    text_len = rows // 2
    row = lax.broadcasted_iota(jnp.int32, (rows, 1), 0)
    live = (row < captions[s]) | ((row >= text_len) & (row < text_len + counts[s]))
    live = live.astype(f32)
    out_ref[...] = ((normed * g2_ref[...] + beta2_ref[...]) * live).astype(bf16)
    up = cot_ref[...].astype(f32) * live

    def add(i, value):
        sums_ref[i : i + 1, :] += jnp.sum(value, 0, keepdims=True)

    add(0, up * normed)
    add(1, up)
    gsi = norm_back(up, normed, inverse, g2_ref[...])
    gdo = gsi.astype(bf16)
    gdo_ref[...] = gdo
    add(2, gdo.astype(f32))
    first = gsi
    for j in range(0, ff, step):
        cols = slice(j, j + step)
        gg = (nt(gdo, down_rows(j)) * d_ref[:, cols]).astype(bf16)
        gg_ref[:, cols] = gg
        bu_sum_ref[:, cols] += jnp.sum(gg.astype(f32), 0, keepdims=True)
        first = first + nt(gg, wu_ref[j // step])
    normed, inverse = norm_parts(mixed_ref[...])
    add(3, first * normed)
    add(4, first)
    gm = norm_back(first, normed, inverse, g1_ref[...])
    gm_ref[...] = gm
    ga = gm.astype(bf16)
    ga_ref[...] = ga
    add(5, ga.astype(f32))
    gc_ref[...] = nt(ga, wo_ref[...]).astype(bf16)


def attention_backward(
    pad, sent, devices,
    counts, offset,
    q_ref, k_ref, v_ref, p_ref, gc_ref, gm_ref, wq_ref, wk_ref, wv_ref,
    gq_ref, gk_ref, gv_ref, gt_ref, gs_ref, sums_ref, acc_ref,
):
    s = pl.program_id(0)
    rows, width = q_ref.shape
    hd = width // HEADS
    scale = hd**-0.5

    @pl.when(s == 0)
    def _():
        sums_ref[...] = jnp.zeros_like(sums_ref)

    lane = lax.broadcasted_iota(jnp.int32, (1, 2 * hd), 1)
    masks = [(lane < hd).astype(bf16), (lane >= hd).astype(bf16)]
    for pair in range(HEADS // 2):
        cols = slice(pair * 2 * hd, (pair + 1) * 2 * hd)
        gq = gk = gv = None
        for j in range(2):
            p = p_ref[0, 2 * pair + j]
            gc = gc_ref[:, cols] * masks[j]
            gp = nt(v_ref[:, cols], gc)
            part = nn(p, gc)
            gv = part if gv is None else gv + part
            pf = p.astype(f32)
            weighted = pf * gp
            gs = (weighted - pf * jnp.sum(weighted, 0, keepdims=True)).astype(bf16)
            part = tn(gs, k_ref[:, cols] * masks[j])
            gq = part if gq is None else gq + part
            part = nn(gs, q_ref[:, cols] * masks[j])
            gk = part if gk is None else gk + part
        gq_ref[:, cols] = (gq * scale).astype(bf16)
        gk_ref[:, cols] = (gk * scale).astype(bf16)
        gv_ref[:, cols] = gv.astype(bf16)
    gq, gk, gv = gq_ref[...], gk_ref[...], gv_ref[...]
    sums_ref[0:1, :] += jnp.sum(gq.astype(f32), 0, keepdims=True)
    sums_ref[1:2, :] += jnp.sum(gv.astype(f32), 0, keepdims=True)
    hidden = gm_ref[...] + nt(gq, wq_ref[...]) + nt(gk, wk_ref[...]) + nt(gv, wv_ref[...])
    text_len = gt_ref.shape[0]
    gt_ref[...] = hidden[:text_len].astype(bf16)
    start = jnp.int32(0)
    for i in range(counts.shape[0]):
        start = start + jnp.where(s > i, counts[i], 0)
    slot = lax.broadcasted_iota(jnp.int32, (rows - text_len, 1), 0)
    taken = one_hot(
        slot + start, slot < counts[s], acc_ref.shape[0], pad, sent, devices, offset[0]
    )
    part = tn(taken, hidden[text_len:].astype(bf16))

    @pl.when(s == 0)
    def _():
        acc_ref[...] = part

    @pl.when(s > 0)
    def _():
        acc_ref[...] += part

    @pl.when(s == pl.num_programs(0) - 1)
    def _():
        gs_ref[...] = acc_ref[...].astype(bf16)


def whole(shape):
    return pl.BlockSpec(shape, lambda s, *_: (0,) * len(shape), pipeline_mode=pl.Buffered(1))


def tile(shape):
    return pl.BlockSpec(shape, lambda s, *_: (s,) + (0,) * (len(shape) - 1))


def still(shape):
    return pl.BlockSpec(shape, lambda s, *_: (0,) * len(shape))


LIMIT = 60 * 1024 * 1024


def cost(flops, moved, exps=0):
    return pl.CostEstimate(flops=int(flops), bytes_accessed=int(moved), transcendentals=int(exps))


def run_image_encode(geometry, x, boxes, wi, wb, bi, gr, betar):
    pad, sent, devices = geometry
    rows, feat = x.shape
    d = wi.shape[1]
    operands = (x, boxes, wi, wb, bi, gr, betar)
    shapes = [jax.ShapeDtypeStruct((rows, d), f32), jax.ShapeDtypeStruct((pad * devices, d), bf16)]
    return pl.pallas_call(
        functools.partial(image_encode, pad, sent),
        out_shape=shapes,
        compiler_params=pltpu.CompilerParams(vmem_limit_bytes=LIMIT),
        cost_estimate=cost(2 * rows * d * feat, x.size * 2 + wi.size * 2 + rows * d * 6),
        name="image_encode",
    )(*operands)


def run_attention_forward(
    geometry, captions, counts, offset, enc, text, wq, wk, wv, wo, bq, bv, bo, g1, beta1
):
    seqs = captions.shape[0]
    text_rows, d = text.shape
    total = 2 * text_rows
    L = total // seqs
    row = tile((L, d))
    vec = whole((d,))
    mat = whole((d, d))
    shapes = (
        [jax.ShapeDtypeStruct((total, d), bf16)] * 4
        + [
            jax.ShapeDtypeStruct((seqs, HEADS, L, L), bf16),
            jax.ShapeDtypeStruct((total, d), bf16),
            jax.ShapeDtypeStruct((total, d), f32),
            jax.ShapeDtypeStruct((total, d), bf16),
        ]
    )
    return pl.pallas_call(
        functools.partial(attention_forward, *geometry),
        out_shape=shapes,
        grid_spec=pltpu.PrefetchScalarGridSpec(
            num_scalar_prefetch=3,
            grid=(seqs,),
            in_specs=[whole(enc.shape), tile((L // 2, d))] + [mat] * 4 + [vec] * 5,
            out_specs=[row] * 4 + [tile((1, HEADS, L, L))] + [row] * 3,
        ),
        compiler_params=pltpu.CompilerParams(
            dimension_semantics=("arbitrary",), vmem_limit_bytes=LIMIT
        ),
        cost_estimate=cost(
            2 * total * d * (4 * d + 2 * L * 4),
            total * d * 18 + seqs * HEADS * L * L * 2,
            seqs * HEADS * L * L,
        ),
        name="attention_forward",
    )(
        captions, counts, offset, enc, text,
        wq, wk, wv, wo, bq, bv, bo, g1, beta1,
    )


def run_image_backward(geometry, chunk, core, x, boxes, wi, pre, back, gr, sums, attn_sums, bu):
    pad, sent, devices = geometry
    rows, feat = x.shape
    d = pre.shape[1]
    first = 8 * (-(-chunk // 16))
    parts = [
        jax.ShapeDtypeStruct((devices // 2, r, d), bf16) for r in (first, chunk - first) * 2
    ]
    operands = (x, boxes, wi, pre, back, gr, sums, attn_sums, bu)
    gp, gx, *out = pl.pallas_call(
        functools.partial(image_backward, pad, sent),
        out_shape=[
            jax.ShapeDtypeStruct((rows, d), bf16),
            jax.ShapeDtypeStruct((rows, feat), bf16),
            *parts,
        ],
        grid_spec=pltpu.PrefetchScalarGridSpec(
            num_scalar_prefetch=1,
            grid=(1,),
            in_specs=[whole(o.shape) for o in operands],
            out_specs=[whole((rows, d)), whole((rows, feat))] + [whole(p.shape) for p in parts],
            scratch_shapes=[pltpu.VMEM((devices * chunk, d), f32)],
        ),
        compiler_params=pltpu.CompilerParams(
            dimension_semantics=("arbitrary",), vmem_limit_bytes=LIMIT
        ),
        cost_estimate=cost(4 * rows * d * feat, x.size * 4 + wi.size * 2 + devices * chunk * d * 2),
        name="image_backward",
    )(core, *operands)
    return gp, gx, list(zip(out[:2], out[2:]))


def join_kernel(core_ref, *refs):
    core = core_ref[0]
    out_ref = refs[-1]
    groups = list(zip(refs[:-1:2], refs[1:-1:2]))
    at = 0
    for i in range(groups[0][0].shape[0]):
        for first in (0, 1):
            for own_ref, came_ref in groups:
                own, came = own_ref[i].astype(f32), came_ref[i].astype(f32)
                rows = own.shape[0]
                out_ref[at : at + rows, :] = jnp.where(core == first, own, came)
                at += rows


def join_blocks(core, halves, shape, step):
    pairs, rows, width = halves[0].shape
    per = width // (2 * rows)
    down, right = step
    block = pl.BlockSpec((per, rows, width), lambda s, *_: (s, 0, 0))
    return pl.pallas_call(
        join_kernel,
        out_shape=jax.ShapeDtypeStruct(shape, f32),
        grid_spec=pltpu.PrefetchScalarGridSpec(
            num_scalar_prefetch=1,
            grid=(pairs // per,),
            in_specs=[block, block],
            out_specs=pl.BlockSpec((width, width), lambda s, *_: (s * down, s * right)),
        ),
        cost_estimate=cost(0, pairs * rows * width * 12),
        name="join_blocks",
    )(core, *halves)


def widen_rest_kernel(attn_rows, img_rows, parts_ref, *outs):
    *squares, img_ref, small_ref = outs
    devices = parts_ref.shape[0]
    width = img_ref.shape[1]
    per = width // attn_rows
    feat = img_ref.shape[0]
    for j, out_ref in enumerate(squares):
        for i in range(per):
            value = parts_ref[j * per + i, :attn_rows, :]
            out_ref[i * attn_rows : (i + 1) * attn_rows, :] = value.astype(f32)
    for i in range(devices):
        value = parts_ref[i, attn_rows:, :].astype(f32)
        at = i * img_rows
        inside = min(max(feat - at, 0), img_rows)
        if inside:
            img_ref[at : at + inside, :] = value[:inside]
        last = min(feat + small_ref.shape[0] - at, img_rows)
        if last > inside:
            first = at + inside - feat
            small_ref[first : first + last - inside, :] = value[inside:last]


def widen_rest(parts, attn_rows, feat, small_rows):
    devices, rows, width = parts.shape
    shapes = [(width, width)] * 4 + [(feat, width), (small_rows, width)]
    return pl.pallas_call(
        functools.partial(widen_rest_kernel, attn_rows, rows - attn_rows),
        out_shape=[jax.ShapeDtypeStruct(t, f32) for t in shapes],
        compiler_params=pltpu.CompilerParams(vmem_limit_bytes=LIMIT),
        cost_estimate=cost(0, parts.size * 6),
        name="widen_rest",
    )(parts)


def run_feed_forward(captions, counts, n1, mixed, cot, weights, cut, wo, bu, bd, g1, g2, beta2):
    seqs = captions.shape[0]
    total, d = n1.shape
    devices = weights.shape[0]
    down = weights.shape[1] // 2
    ff = devices * down
    blocks = ff // d

    def part(rows, index):
        return pl.BlockSpec(
            (devices, rows, d), lambda s, *_: (0, index, 0), pipeline_mode=pl.Buffered(1)
        )

    if cut % 8 == 0:
        ups = [part(cut, blocks + j) for j in range(blocks)]
        up_weights = [weights] * blocks
    else:
        ups = [whole((d, d))] * blocks
        up_weights = [
            weights[:, down + j * cut : down + (j + 1) * cut].reshape(d, d) for j in range(blocks)
        ]

    L = total // seqs
    row = tile((L, d))
    wide = tile((L, ff))
    vec = whole((d,))
    shapes = [
        jax.ShapeDtypeStruct((total, d), bf16),
        jax.ShapeDtypeStruct((total, ff), bf16),
        jax.ShapeDtypeStruct((total, d), bf16),
        jax.ShapeDtypeStruct((total, ff), bf16),
        jax.ShapeDtypeStruct((total, d), f32),
        jax.ShapeDtypeStruct((total, d), bf16),
        jax.ShapeDtypeStruct((total, d), bf16),
        jax.ShapeDtypeStruct((8, d), f32),
        jax.ShapeDtypeStruct((1, ff), f32),
    ]
    return pl.pallas_call(
        feed_forward,
        out_shape=shapes,
        grid_spec=pltpu.PrefetchScalarGridSpec(
            num_scalar_prefetch=2,
            grid=(seqs,),
            in_specs=[row, row, row, part(down, 0)]
            + ups
            + [whole((d, d)), whole((ff,)), vec, vec, vec, vec],
            out_specs=[row, wide, row, wide, row, row, row, still((8, d)), still((1, ff))],
            scratch_shapes=[pltpu.VMEM((L, ff), f32), pltpu.VMEM((blocks, d, d), bf16)],
        ),
        compiler_params=pltpu.CompilerParams(
            dimension_semantics=("arbitrary",), vmem_limit_bytes=LIMIT
        ),
        cost_estimate=cost(2 * total * d * (4 * ff + d), total * (ff * 4 + d * 18) + d * ff * 4, total * ff),
        name="feed_forward",
    )(captions, counts, n1, mixed, cot, weights, *up_weights, wo, bu, bd, g1, g2, beta2)


def run_attention_backward(geometry, counts, offset, q, k, v, p, gc, gm, wq, wk, wv):
    seqs, _, L, _ = p.shape
    total, d = q.shape
    row = tile((L, d))
    half = tile((L // 2, d))
    mat = whole((d, d))
    received = geometry[0] * geometry[2]
    shapes = [jax.ShapeDtypeStruct((total, d), bf16)] * 3 + [
        jax.ShapeDtypeStruct((total // 2, d), bf16),
        jax.ShapeDtypeStruct((received, d), bf16),
        jax.ShapeDtypeStruct((8, d), f32),
    ]
    return pl.pallas_call(
        functools.partial(attention_backward, *geometry),
        out_shape=shapes,
        grid_spec=pltpu.PrefetchScalarGridSpec(
            num_scalar_prefetch=2,
            grid=(seqs,),
            in_specs=[row, row, row, tile((1, HEADS, L, L)), row, row, mat, mat, mat],
            out_specs=[row, row, row, half, still((received, d)), still((8, d))],
            scratch_shapes=[pltpu.VMEM((received, d), f32)],
        ),
        compiler_params=pltpu.CompilerParams(
            dimension_semantics=("arbitrary",), vmem_limit_bytes=LIMIT
        ),
        cost_estimate=cost(2 * total * d * (3 * d + 4 * L * 4), total * d * 20 + seqs * HEADS * L * L * 2),
        name="attention_backward",
    )(counts, offset, q, k, v, p, gc, gm, wq, wk, wv)


def weight_grad_kernel(lhs_of, rhs_of, groups, core_ref, *refs):
    lhs_refs = refs[: max(lhs_of) + 1]
    rhs_refs = refs[len(lhs_refs) : len(lhs_refs) + max(rhs_of) + 1]
    outs = refs[len(lhs_refs) + len(rhs_refs) : -1]
    acc_ref = refs[-1]
    step = pl.program_id(0)
    core = core_ref[0]
    kinds = {}
    for i, kind in enumerate(zip(lhs_of, rhs_of)):
        kinds.setdefault(kind, []).append(i)
    for (a, b), steps in kinds.items():

        @pl.when((step >= steps[0]) & (step <= steps[-1]))
        def _(a=a, b=b):
            value = tn(lhs_refs[a][...], rhs_refs[b][...]).astype(bf16)
            acc_ref[...] = value.reshape(acc_ref.shape)

    for i in range(outs[0].shape[0]):
        for side in (0, 1):
            at = 0
            for ref in outs[side * groups : (side + 1) * groups]:
                rows = ref.shape[1]
                ref[i] = acc_ref[2 * i + (1 - core if side == 0 else core), at : at + rows, :]
                at += rows


def weight_grads(core, devices, lhs, rhs, lhs_of, rhs_of, lhs_maps, rhs_maps, width, groups, name):
    steps = len(lhs_of)
    total = lhs[0].shape[0]
    rows = steps * width // devices
    per = width // rows
    outs = [rows // groups] * (2 * groups)
    specs = [pl.BlockSpec((total, width), m) for m in lhs_maps + rhs_maps]
    out = pl.pallas_call(
        functools.partial(weight_grad_kernel, lhs_of, rhs_of, groups),
        out_shape=[jax.ShapeDtypeStruct((devices // 2, r, width), bf16) for r in outs],
        grid_spec=pltpu.PrefetchScalarGridSpec(
            num_scalar_prefetch=1,
            grid=(steps,),
            in_specs=specs,
            out_specs=[pl.BlockSpec((per // 2, r, width), lambda s, *_: (s, 0, 0)) for r in outs],
            scratch_shapes=[pltpu.VMEM((per, rows, width), bf16)],
        ),
        compiler_params=pltpu.CompilerParams(
            dimension_semantics=("arbitrary",), vmem_limit_bytes=LIMIT
        ),
        cost_estimate=cost(2 * total * width * width * steps, steps * width * (total + width) * 2),
        name=name,
    )(core, *lhs, *rhs)
    return list(zip(out[:groups], out[groups:]))


def axis_bits(name):
    size = lax.axis_size(name)
    bits = []
    step = 1
    while step < size:
        bits.append((name, step))
        step *= 2
    return bits


def bit_layout():
    return axis_bits("enc")[::-1] + axis_bits("dp")[::-1]


def my_bit(bit):
    return (lax.axis_index(bit[0]) // bit[1]) % 2


def swap_bit(tensor, bit):
    name, step = bit
    size = lax.axis_size(name)
    return lax.ppermute(tensor, name, [(i, i ^ step) for i in range(size)])


def stage_orders():
    dp_bits, enc_bits = axis_bits("dp"), axis_bits("enc")
    near, middle = dp_bits[:1], dp_bits[1:]
    half = len(middle) // 2
    return (
        near + middle + enc_bits,
        near + middle[half:] + middle[:half] + enc_bits,
    )


def add_low(kept, came):
    return (kept.astype(f32) + came.astype(f32)).astype(bf16)


class Scatter:
    def __init__(self, away, kept, order):
        self.order = list(order)
        self.layout = bit_layout()
        self.value = (away, kept)
        self.fresh = True

    def stage(self):
        bit = self.order.pop(0)
        axis = self.layout.index(bit)
        self.layout.remove(bit)
        if self.fresh:
            away, kept = self.value
            self.fresh = False
        else:
            mine = my_bit(bit)
            away, kept = [
                add_low(*[lax.dynamic_index_in_dim(t, i, axis, keepdims=False) for t in self.value])
                for i in (1 - mine, mine)
            ]
        shape = (2,) * len(self.layout) + kept.shape[-2:]
        self.value = (kept.reshape(shape), swap_bit(away, bit).reshape(shape))
        return away

    def total(self):
        return add_low(*self.value)


class Gather:
    def __init__(self, rows, order, layout=()):
        self.order = list(order)[::-1]
        self.layout = list(layout)
        self.value = rows

    def stage(self):
        bit = self.order.pop(0)
        sent = self.value
        came = swap_bit(sent, bit)
        self.layout = [b for b in bit_layout() if b in self.layout or b == bit]
        axis = self.layout.index(bit)
        shape = sent.shape[:axis] + (2,) + sent.shape[axis:]
        at = lax.broadcasted_iota(jnp.int32, shape, axis)
        self.value = jnp.where(
            at == my_bit(bit), jnp.expand_dims(sent, axis), jnp.expand_dims(came, axis)
        )
        return sent

    def rows(self):
        return self.value.reshape((-1,) + self.value.shape[-2:])

    def halves(self):
        (bit,) = self.order
        came = swap_bit(self.value, bit)
        shape = (-1,) + came.shape[-2:]
        return self.value.reshape(shape), came.reshape(shape)

    def split(self, at, orders):
        values = (self.value[..., :at, :], self.value[..., at:, :])
        return [
            Gather(value, [b for b in order if b not in self.layout], self.layout)
            for value, order in zip(values, orders)
        ]


def fence(movers, *values):
    leaves, tree = jax.tree.flatten(([m.value for m in movers], values))
    held, values = jax.tree.unflatten(tree, lax.optimization_barrier(leaves))
    for mover, value in zip(movers, held):
        mover.value = value
    return values


class Sum:
    def __init__(self, parts, orders):
        far = len(axis_bits("enc"))
        self.movers = [Scatter(*part, order) for part, order in zip(parts, orders)]
        self.steps = [self.run] * (len(orders[0]) - far) + [self.merge] + [self.run] * (far - 1)

    @property
    def value(self):
        return [m.value for m in self.movers]

    @value.setter
    def value(self, values):
        for mover, value in zip(self.movers, values):
            mover.value = value

    def stage(self):
        if self.steps:
            self.steps.pop(0)()

    def run(self):
        for mover in self.movers:
            mover.stage()

    def merge(self):
        first = self.movers[0]
        first.value = tuple(jnp.concatenate(t, -2) for t in zip(*[m.value for m in self.movers]))
        self.movers = [first]
        self.run()

    def total(self):
        return self.movers[0].total()


def body(
    text,
    region_feats,
    boxes,
    caption_count,
    region_count,
    region_offset,
    w_img,
    w_box,
    b_img,
    g_reg,
    beta_reg,
    w_query,
    b_query,
    w_key,
    w_value,
    b_value,
    w_out,
    b_out,
    g_one,
    beta_one,
    w_up,
    b_up,
    w_down,
    b_down,
    g_two,
    beta_two,
    cotangent,
):
    axes = ("enc", "dp")
    orders = stage_orders()
    model_width = text.shape[1]
    ff_blocks = w_up.shape[1] // model_width
    cut = w_query.shape[0]
    far = axis_bits("enc")

    middle = len(orders[0]) - 1 - len(far)
    core = (lax.axis_index("dp") % 2).astype(jnp.int32).reshape(1)

    up_blocks = w_up.reshape(cut, ff_blocks, model_width).transpose(1, 0, 2)
    ff_shard = jnp.concatenate([w_down, up_blocks.reshape(ff_blocks * cut, model_width)], 0)
    rows_up = cut
    img = Gather(w_img, far)
    attn = Gather(jnp.concatenate([w_query, w_key, w_value, w_out], 0), far)
    img.stage()
    (ff_shard,) = fence([img, attn], ff_shard)
    ff_weights = lax.all_gather(ff_shard, axes, axis=0)
    while img.order:
        img.stage()
        attn.stage()
        fence([img, attn])
    img = img.split(w_img.shape[0] // 2, orders)
    attn.stage()
    for _ in range(middle):
        for part in img:
            part.stage()
        fence([*img, attn])
    attn = attn.split(2 * cut, orders)
    for part in (*img, *attn):
        part.stage()
    img_full = jnp.concatenate([t.rows() for t in img], 1).reshape(-1, model_width)
    device_count = lax.axis_size(axes)
    seq_count = caption_count.shape[0]
    sent_rows, feat = region_feats.shape
    per_peer = sent_rows // device_count
    pad = 8 * (-(-per_peer // 8))
    pad = 1 << (pad - 1).bit_length()
    box_count = boxes.shape[0]
    geometry = (pad, per_peer, device_count)
    pre_norm, encoded = run_image_encode(
        geometry, region_feats, boxes, img_full, w_box, b_img, g_reg, beta_reg
    )
    (encoded,) = fence(attn, encoded)
    received = lax.all_to_all(encoded, axes, split_axis=0, concat_axis=0, tiled=True)
    for _ in range(middle - 1):
        for part in attn:
            part.stage()
        (received,) = fence(attn, received)
    for part in attn:
        part.stage()
    query_full, key_full, value_full, out_full = [
        t.reshape(-1, model_width)
        for part in attn
        for t in (part.rows()[:, :cut], part.rows()[:, cut:])
    ]
    (
        hidden_in,
        queries,
        keys,
        values,
        probs,
        context,
        mixed,
        normed_one,
    ) = run_attention_forward(
        geometry,
        caption_count,
        region_count,
        region_offset,
        received,
        text,
        query_full,
        key_full,
        value_full,
        out_full,
        b_query,
        b_value,
        b_out,
        g_one,
        beta_one,
    )
    (
        output,
        activated,
        grad_down_out,
        grad_gate,
        grad_mixed,
        grad_attn,
        grad_context,
        sums,
        grad_b_up,
    ) = run_feed_forward(
        caption_count,
        region_count,
        normed_one,
        mixed,
        cotangent,
        ff_weights,
        rows_up,
        out_full,
        b_up,
        b_down,
        g_one,
        g_two,
        beta_two,
    )
    fixed = lambda s, *_: (0, 0)
    moving = lambda s, *_: (0, s)
    (down,) = weight_grads(
        core,
        device_count,
        [activated],
        [grad_down_out],
        [0] * ff_blocks,
        [0] * ff_blocks,
        [moving],
        [fixed],
        model_width,
        1,
        "grad_w_down",
    )
    (up,) = weight_grads(
        core,
        device_count,
        [normed_one],
        [grad_gate],
        [0] * ff_blocks,
        [0] * ff_blocks,
        [fixed],
        [moving],
        model_width,
        1,
        "grad_w_up",
    )
    ff = Sum([down, up], orders)
    ff.stage()
    (grad_context,) = fence([ff], grad_context)
    ff.stage()
    grad_query, grad_keys, grad_values, grad_text, grad_slots, attn_sums = run_attention_backward(
        geometry,
        region_count,
        region_offset,
        queries,
        keys,
        values,
        probs,
        grad_context,
        grad_mixed,
        query_full,
        key_full,
        value_full,
    )
    grad_query, grad_keys, grad_values, grad_slots, attn_sums = fence(
        [ff], grad_query, grad_keys, grad_values, grad_slots, attn_sums
    )
    back = lax.all_to_all(grad_slots, axes, split_axis=0, concat_axis=0, tiled=True)
    ff.stage()
    attn_parts = weight_grads(
        core,
        device_count,
        [hidden_in, context],
        [grad_query, grad_keys, grad_values, grad_attn],
        [0, 0, 0, 1],
        [0, 1, 2, 3],
        [fixed] * 2,
        [fixed] * 4,
        model_width,
        2,
        "grad_w_attn",
    )
    attn = Sum(attn_parts, orders)
    (back,) = fence([ff, attn], back)
    while len(ff.steps) > len(far):
        ff.stage()
        fence([ff])
    ff.stage()
    attn.stage()
    small_rows = 40
    chunk = 8 * (-(-(feat + small_rows) // (8 * device_count)))
    grad_pre, grad_feats, img_parts = run_image_backward(
        geometry,
        chunk,
        core,
        region_feats,
        boxes,
        img_full,
        pre_norm,
        back,
        g_reg,
        sums,
        attn_sums,
        grad_b_up.reshape(ff_blocks, model_width),
    )
    img = Sum(img_parts, orders)
    fence([ff, attn, img])
    while ff.steps:
        ff.stage()
        if not ff.steps:
            attn.stage()
            img.stage()
        fence([ff, attn, img])
    ff = Gather(ff.total(), far)
    ff.stage()
    while img.steps:
        attn.stage()
        img.stage()
        fence([attn, img, ff])
    rest = jnp.concatenate([attn.total(), img.total()], 0)
    rest_all = lax.all_gather(rest, axes, axis=0)
    fence([ff], rest)
    while ff.order:
        ff.stage()
        fence([ff])
    down, up = ff.split(w_down.shape[0], orders)
    while len(down.order) > 1:
        down.stage()
        up.stage()
        fence([down, up])
    down_halves, up_halves = down.halves(), up.halves()
    grad_w_down = join_blocks(
        core, down_halves, (ff_blocks * model_width, model_width), (1, 0)
    )
    grad_w_up = join_blocks(core, up_halves, (model_width, ff_blocks * model_width), (0, 1))
    grad_boxes = jnp.einsum("cd,rd->cr", w_box, grad_pre, preferred_element_type=f32).astype(bf16)
    grad_w_query, grad_w_key, grad_w_value, grad_w_out, grad_w_img, small = widen_rest(
        rest_all, 4 * cut, feat, small_rows
    )
    grad_w_box = small[:box_count]
    grad_b_img, grad_g_reg, grad_beta_reg = [small[8 + i] for i in range(3)]
    grad_g_two, grad_beta_two, grad_b_down, grad_g_one, grad_beta_one, grad_b_out = [
        small[16 + i] for i in range(6)
    ]
    grad_b_query, grad_b_value = small[24], small[25]
    grad_b_up = small[32 : 32 + ff_blocks].reshape(-1)
    return (
        output,
        grad_text,
        grad_feats,
        grad_boxes,
        grad_w_img,
        grad_w_box,
        grad_b_img,
        grad_g_reg,
        grad_beta_reg,
        grad_w_query,
        grad_b_query,
        grad_w_key,
        grad_w_value,
        grad_b_value,
        grad_w_out,
        grad_b_out,
        grad_g_one,
        grad_beta_one,
        grad_w_up,
        grad_b_up,
        grad_w_down,
        grad_b_down,
        grad_g_two,
        grad_beta_two,
    )


def solution(mesh):
    return jax.shard_map(
        body,
        mesh=mesh,
        in_specs=(
            P(("enc", "dp"), None),
            P(("enc", "dp"), None),
            P(None, ("enc", "dp")),
            P(("enc", "dp")),
            P(("enc", "dp")),
            P(("enc", "dp")),
            P(("enc", "dp"), None),
            P(),
            P(),
            P(),
            P(),
            P(("enc", "dp"), None),
            P(),
            P(("enc", "dp"), None),
            P(("enc", "dp"), None),
            P(),
            P(("enc", "dp"), None),
            P(),
            P(),
            P(),
            P(("enc", "dp"), None),
            P(),
            P(("enc", "dp"), None),
            P(),
            P(),
            P(),
            P(("enc", "dp"), None),
        ),
        out_specs=(
            P(("enc", "dp"), None),
            P(("enc", "dp"), None),
            P(("enc", "dp"), None),
            P(None, ("enc", "dp")),
            P(),
            P(),
            P(),
            P(),
            P(),
            P(),
            P(),
            P(),
            P(),
            P(),
            P(),
            P(),
            P(),
            P(),
            P(),
            P(),
            P(),
            P(),
            P(),
            P(),
        ),
        check_vma=False,
    )
```

```python
import functools
import math

import jax
import jax.numpy as jnp
from jax import lax
from jax.experimental import pallas as pl
from jax.experimental.pallas import tpu as pltpu
from jax.sharding import PartitionSpec as P

HEADS = 12
epsilon = 1e-05
f32, bf16 = jnp.float32, jnp.bfloat16

ERFC_P = 0.35
ERFC_C = (
    0.19567911,
    0.22612264,
    0.02080242,
    0.63768037,
    -0.6386366,
    0.75239514,
    -0.19404308,
)


def nn(a, b):
    return lax.dot_general(a, b, (((1,), (0,)), ((), ())), preferred_element_type=f32)


def nt(a, b):
    return lax.dot_general(a, b, (((1,), (1,)), ((), ())), preferred_element_type=f32)


def tn(a, b):
    return lax.dot_general(a, b, (((0,), (0,)), ((), ())), preferred_element_type=f32)


def norm_parts(values):
    centered = values - jnp.mean(values, -1, keepdims=True)
    inverse = lax.rsqrt(jnp.mean(centered * centered, -1, keepdims=True) + epsilon)
    return centered * inverse, inverse


def norm_back(upstream, normed, inverse, gain):
    weighted = upstream * gain
    return inverse * (
        weighted
        - jnp.mean(weighted, -1, keepdims=True)
        - normed * jnp.mean(weighted * normed, -1, keepdims=True)
    )


def gelu_parts(x):
    e = jnp.exp(-0.5 * x * x)
    t = 1.0 / (1.0 + (ERFC_P * math.sqrt(0.5)) * jnp.abs(x))
    acc = jnp.full_like(t, 0.5 * ERFC_C[-1])
    for c in ERFC_C[-2::-1]:
        acc = acc * t + 0.5 * c
    tail = acc * t * e
    phi = jnp.where(x >= 0, 1.0 - tail, tail)
    return x * phi, phi + x * (e * (1.0 / math.sqrt(2.0 * math.pi)))


def one_hot(wanted, live, rows, pad, sent, devices, offset):
    row = lax.broadcasted_iota(jnp.int32, (1, rows), 1)
    shift = pad.bit_length() - 1
    turn = lax.shift_right_logical(row, shift) - offset
    turn = jnp.where(turn < 0, turn + devices, turn)
    inside = jnp.bitwise_and(row, pad - 1)
    arrival = jnp.where(inside < sent, inside * devices + turn, -1)
    return ((wanted == arrival) & live).astype(bf16)


def spread(pad, sent, rows, padded):
    to = lax.broadcasted_iota(jnp.int32, (padded, 1), 0)
    shift = pad.bit_length() - 1
    inside = jnp.bitwise_and(to, pad - 1)
    source = jnp.where(inside < sent, lax.shift_right_logical(to, shift) * sent + inside, -1)
    return (source == lax.broadcasted_iota(jnp.int32, (1, rows), 1)).astype(bf16)


def image_encode(
    pad, sent, core_ref,
    x_ref, box_ref, wb_ref, bi_ref, gr_ref, betar_ref, *refs,
):
    *halves, pre_ref, enc_ref, wi_ref = refs
    core = core_ref[0]
    at = 0
    for own_ref, came_ref in zip(halves[::2], halves[1::2]):
        pairs, rows, _ = own_ref.shape
        for i in range(pairs):
            wi_ref[2 * i + core, at : at + rows, :] = own_ref[i]
            wi_ref[2 * i + 1 - core, at : at + rows, :] = came_ref[i]
        at += rows
    weight = wi_ref[...].reshape(x_ref.shape[1], wi_ref.shape[2])
    pre = nn(x_ref[...], weight) + tn(box_ref[...], wb_ref[...]) + bi_ref[...]
    pre_ref[...] = pre
    normed, _ = norm_parts(pre)
    encoded = (normed * gr_ref[...] + betar_ref[...]).astype(bf16)
    enc_ref[...] = nn(spread(pad, sent, x_ref.shape[0], enc_ref.shape[0]), encoded).astype(bf16)


def attention_forward(
    pad, sent, devices,
    captions, counts, offset,
    enc_ref, text_ref,
    wq_ref, wk_ref, wv_ref, wo_ref, bq_ref, bv_ref, bo_ref, g_ref, beta_ref,
    h_ref, q_ref, k_ref, v_ref, p_ref, c_ref, mixed_ref, n_ref,
):
    s = pl.program_id(0)
    text_len = text_ref.shape[0]
    rows, width = h_ref.shape
    hd = width // HEADS
    start = jnp.int32(0)
    for i in range(captions.shape[0]):
        start = start + jnp.where(s > i, counts[i], 0)
    slot = lax.broadcasted_iota(jnp.int32, (rows - text_len, 1), 0)
    taken = one_hot(
        slot + start, slot < counts[s], enc_ref.shape[0], pad, sent, devices, offset[0]
    )
    h_ref[:text_len, :] = text_ref[...]
    h_ref[text_len:, :] = nn(taken, enc_ref[...]).astype(bf16)
    h = h_ref[...]
    q = (nn(h, wq_ref[...]) + bq_ref[...]).astype(bf16)
    k = nn(h, wk_ref[...]).astype(bf16)
    v = (nn(h, wv_ref[...]) + bv_ref[...]).astype(bf16)
    q_ref[...] = q
    k_ref[...] = k
    v_ref[...] = v
    row = lax.broadcasted_iota(jnp.int32, (rows, 1), 0)
    live = (row < captions[s]) | ((row >= text_len) & (row < text_len + counts[s]))
    lane = lax.broadcasted_iota(jnp.int32, (1, 2 * hd), 1)
    masks = [(lane < hd).astype(bf16), (lane >= hd).astype(bf16)]
    scaled = q * jnp.asarray(hd**-0.5, bf16)
    for pair in range(HEADS // 2):
        cols = slice(pair * 2 * hd, (pair + 1) * 2 * hd)
        context = None
        for j in range(2):
            scores = nt(k[:, cols], scaled[:, cols] * masks[j])
            scores = jnp.where(live, scores, -1e30)
            top = jnp.max(scores, 0, keepdims=True)
            e = jnp.exp(scores - top)
            p = (e * (1.0 / jnp.sum(e, 0, keepdims=True))).astype(bf16)
            p_ref[0, 2 * pair + j] = p
            part = tn(p, v[:, cols] * masks[j])
            context = part if context is None else context + part
        c_ref[:, cols] = context.astype(bf16)
    mixed = h.astype(f32) + nn(c_ref[...], wo_ref[...]) + bo_ref[...]
    mixed_ref[...] = mixed
    normed, _ = norm_parts(mixed)
    n_ref[...] = (normed * g_ref[...] + beta_ref[...]).astype(bf16)


def image_backward(
    pad, sent, core_ref,
    x_ref, box_ref, wi_ref, pre_ref, back_ref, gr_ref, sums_ref, attn_sums_ref, bu_ref,
    gp_ref, gx_ref, *outs,
):
    *outs, acc_ref = outs
    rows, feat = x_ref.shape
    width = pre_ref.shape[1]
    grad = tn(spread(pad, sent, rows, back_ref.shape[0]), back_ref[...])
    normed, inverse = norm_parts(pre_ref[...])
    gp = norm_back(grad, normed, inverse, gr_ref[...]).astype(bf16)
    gp_ref[...] = gp
    acc_ref[:feat, :] = tn(x_ref[...], gp)
    acc_ref[feat:, :] = jnp.zeros((acc_ref.shape[0] - feat, width), f32)
    acc_ref[feat : feat + box_ref.shape[0], :] = nn(box_ref[...], gp)
    at = feat + 8
    acc_ref[at : at + 1, :] = jnp.sum(gp.astype(f32), 0, keepdims=True)
    acc_ref[at + 1 : at + 2, :] = jnp.sum(grad * normed, 0, keepdims=True)
    acc_ref[at + 2 : at + 3, :] = jnp.sum(grad, 0, keepdims=True)
    acc_ref[at + 8 : at + 16, :] = sums_ref[...]
    acc_ref[at + 16 : at + 24, :] = attn_sums_ref[...]
    acc_ref[at + 24 : at + 24 + bu_ref.shape[0], :] = bu_ref[...]
    core = core_ref[0]
    half = len(outs) // 2
    chunk = sum(ref.shape[1] for ref in outs[:half])
    for i in range(outs[0].shape[0]):
        for side in (0, 1):
            at = (2 * i + (1 - core if side == 0 else core)) * chunk
            for ref in outs[side * half : (side + 1) * half]:
                rows_here = ref.shape[1]
                ref[i] = acc_ref[pl.ds(pl.multiple_of(at, 8), rows_here), :].astype(bf16)
                at = at + rows_here
    gx_ref[...] = nt(gp, wi_ref[...]).astype(bf16)


def feed_forward(
    captions, counts, n_ref, mixed_ref, cot_ref, wd_ref, *refs,
):
    blocks = len(refs) - 17
    up_refs = refs[:blocks]
    wu_ref = refs[-1]

    @pl.when(pl.program_id(0) == 0)
    def _():
        for j in range(blocks):
            wu_ref[j] = up_refs[j][...].astype(f32).reshape(wu_ref.shape[1:]).astype(bf16)

    feed_forward_rows(captions, counts, n_ref, mixed_ref, cot_ref, wu_ref, wd_ref, *refs[blocks:-1])


def feed_forward_rows(
    captions, counts, n_ref, mixed_ref, cot_ref, wu_ref, wd_ref, wo_ref, bu_ref, bd_ref, g1_ref, g2_ref, beta2_ref,
    out_ref, act_ref, gdo_ref, gg_ref, gm_ref, ga_ref, gc_ref, sums_ref, bu_sum_ref, d_ref,
):
    s = pl.program_id(0)
    n1 = n_ref[...]
    rows, width = n1.shape
    ff = act_ref.shape[1]
    step = width
    per = wd_ref.shape[0] * step // ff

    def down_rows(j):
        return wd_ref[j // step * per : (j // step + 1) * per].reshape(step, width)

    @pl.when(s == 0)
    def _():
        sums_ref[...] = jnp.zeros_like(sums_ref)
        bu_sum_ref[...] = jnp.zeros_like(bu_sum_ref)

    second = n1.astype(f32) + bd_ref[...]
    for j in range(0, ff, step):
        cols = slice(j, j + step)
        gate = nn(n1, wu_ref[j // step]) + bu_ref[cols]
        act, d = gelu_parts(gate)
        act = act.astype(bf16)
        act_ref[:, cols] = act
        d_ref[:, cols] = d
        second = second + nn(act, down_rows(j))
    normed, inverse = norm_parts(second)
    text_len = rows // 2
    row = lax.broadcasted_iota(jnp.int32, (rows, 1), 0)
    live = (row < captions[s]) | ((row >= text_len) & (row < text_len + counts[s]))
    live = live.astype(f32)
    out_ref[...] = ((normed * g2_ref[...] + beta2_ref[...]) * live).astype(bf16)
    up = cot_ref[...].astype(f32) * live

    def add(i, value):
        sums_ref[i : i + 1, :] += jnp.sum(value, 0, keepdims=True)

    add(0, up * normed)
    add(1, up)
    gsi = norm_back(up, normed, inverse, g2_ref[...])
    gdo = gsi.astype(bf16)
    gdo_ref[...] = gdo
    add(2, gdo.astype(f32))
    first = gsi
    for j in range(0, ff, step):
        cols = slice(j, j + step)
        gg = (nt(gdo, down_rows(j)) * d_ref[:, cols]).astype(bf16)
        gg_ref[:, cols] = gg
        bu_sum_ref[:, cols] += jnp.sum(gg.astype(f32), 0, keepdims=True)
        first = first + nt(gg, wu_ref[j // step])
    normed, inverse = norm_parts(mixed_ref[...])
    add(3, first * normed)
    add(4, first)
    gm = norm_back(first, normed, inverse, g1_ref[...])
    gm_ref[...] = gm
    ga = gm.astype(bf16)
    ga_ref[...] = ga
    add(5, ga.astype(f32))
    gc_ref[...] = nt(ga, wo_ref[...]).astype(bf16)


def attention_backward(
    pad, sent, devices,
    counts, offset,
    q_ref, k_ref, v_ref, p_ref, gc_ref, gm_ref, wq_ref, wk_ref, wv_ref,
    gq_ref, gk_ref, gv_ref, gt_ref, gs_ref, sums_ref, acc_ref,
):
    s = pl.program_id(0)
    rows, width = q_ref.shape
    hd = width // HEADS
    scale = hd**-0.5

    @pl.when(s == 0)
    def _():
        sums_ref[...] = jnp.zeros_like(sums_ref)

    lane = lax.broadcasted_iota(jnp.int32, (1, 2 * hd), 1)
    masks = [(lane < hd).astype(bf16), (lane >= hd).astype(bf16)]
    for pair in range(HEADS // 2):
        cols = slice(pair * 2 * hd, (pair + 1) * 2 * hd)
        gq = gk = gv = None
        for j in range(2):
            p = p_ref[0, 2 * pair + j]
            gc = gc_ref[:, cols] * masks[j]
            gp = nt(v_ref[:, cols], gc)
            part = nn(p, gc)
            gv = part if gv is None else gv + part
            pf = p.astype(f32)
            weighted = pf * gp
            gs = (weighted - pf * jnp.sum(weighted, 0, keepdims=True)).astype(bf16)
            part = tn(gs, k_ref[:, cols] * masks[j])
            gq = part if gq is None else gq + part
            part = nn(gs, q_ref[:, cols] * masks[j])
            gk = part if gk is None else gk + part
        gq_ref[:, cols] = (gq * scale).astype(bf16)
        gk_ref[:, cols] = (gk * scale).astype(bf16)
        gv_ref[:, cols] = gv.astype(bf16)
    gq, gk, gv = gq_ref[...], gk_ref[...], gv_ref[...]
    sums_ref[0:1, :] += jnp.sum(gq.astype(f32), 0, keepdims=True)
    sums_ref[1:2, :] += jnp.sum(gv.astype(f32), 0, keepdims=True)
    hidden = gm_ref[...] + nt(gq, wq_ref[...]) + nt(gk, wk_ref[...]) + nt(gv, wv_ref[...])
    text_len = gt_ref.shape[0]
    gt_ref[...] = hidden[:text_len].astype(bf16)
    start = jnp.int32(0)
    for i in range(counts.shape[0]):
        start = start + jnp.where(s > i, counts[i], 0)
    slot = lax.broadcasted_iota(jnp.int32, (rows - text_len, 1), 0)
    taken = one_hot(
        slot + start, slot < counts[s], acc_ref.shape[0], pad, sent, devices, offset[0]
    )
    part = tn(taken, hidden[text_len:].astype(bf16))

    @pl.when(s == 0)
    def _():
        acc_ref[...] = part

    @pl.when(s > 0)
    def _():
        acc_ref[...] += part

    @pl.when(s == pl.num_programs(0) - 1)
    def _():
        gs_ref[...] = acc_ref[...].astype(bf16)


def whole(shape):
    return pl.BlockSpec(shape, lambda s, *_: (0,) * len(shape), pipeline_mode=pl.Buffered(1))


def tile(shape):
    return pl.BlockSpec(shape, lambda s, *_: (s,) + (0,) * (len(shape) - 1))


def still(shape):
    return pl.BlockSpec(shape, lambda s, *_: (0,) * len(shape))


LIMIT = 60 * 1024 * 1024


def cost(flops, moved, exps=0):
    return pl.CostEstimate(flops=int(flops), bytes_accessed=int(moved), transcendentals=int(exps))


def run_image_encode(geometry, core, x, boxes, halves, wb, bi, gr, betar):
    pad, sent, devices = geometry
    rows, feat = x.shape
    d = wb.shape[1]
    operands = (x, boxes, wb, bi, gr, betar, *halves)
    shapes = [
        jax.ShapeDtypeStruct((rows, d), f32),
        jax.ShapeDtypeStruct((pad * devices, d), bf16),
        jax.ShapeDtypeStruct((devices, feat // devices, d), bf16),
    ]
    return pl.pallas_call(
        functools.partial(image_encode, pad, sent),
        out_shape=shapes,
        grid_spec=pltpu.PrefetchScalarGridSpec(
            num_scalar_prefetch=1,
            grid=(1,),
            in_specs=[whole(t.shape) for t in operands],
            out_specs=[whole(t.shape) for t in shapes],
        ),
        compiler_params=pltpu.CompilerParams(vmem_limit_bytes=LIMIT),
        cost_estimate=cost(2 * rows * d * feat, x.size * 2 + feat * d * 4 + rows * d * 6),
        name="image_encode",
    )(core, *operands)


def run_attention_forward(
    geometry, captions, counts, offset, enc, text, wq, wk, wv, wo, bq, bv, bo, g1, beta1
):
    seqs = captions.shape[0]
    text_rows, d = text.shape
    total = 2 * text_rows
    L = total // seqs
    row = tile((L, d))
    vec = whole((d,))
    mat = whole((d, d))
    shapes = (
        [jax.ShapeDtypeStruct((total, d), bf16)] * 4
        + [
            jax.ShapeDtypeStruct((seqs, HEADS, L, L), bf16),
            jax.ShapeDtypeStruct((total, d), bf16),
            jax.ShapeDtypeStruct((total, d), f32),
            jax.ShapeDtypeStruct((total, d), bf16),
        ]
    )
    return pl.pallas_call(
        functools.partial(attention_forward, *geometry),
        out_shape=shapes,
        grid_spec=pltpu.PrefetchScalarGridSpec(
            num_scalar_prefetch=3,
            grid=(seqs,),
            in_specs=[whole(enc.shape), tile((L // 2, d))] + [mat] * 4 + [vec] * 5,
            out_specs=[row] * 4 + [tile((1, HEADS, L, L))] + [row] * 3,
        ),
        compiler_params=pltpu.CompilerParams(
            dimension_semantics=("arbitrary",), vmem_limit_bytes=LIMIT
        ),
        cost_estimate=cost(
            2 * total * d * (4 * d + 2 * L * 4),
            total * d * 18 + seqs * HEADS * L * L * 2,
            seqs * HEADS * L * L,
        ),
        name="attention_forward",
    )(
        captions, counts, offset, enc, text,
        wq, wk, wv, wo, bq, bv, bo, g1, beta1,
    )


def run_image_backward(geometry, chunk, core, x, boxes, wi, pre, back, gr, sums, attn_sums, bu):
    pad, sent, devices = geometry
    rows, feat = x.shape
    d = pre.shape[1]
    first = 8 * (-(-chunk // 16))
    parts = [
        jax.ShapeDtypeStruct((devices // 2, r, d), bf16) for r in (first, chunk - first) * 2
    ]
    operands = (x, boxes, wi, pre, back, gr, sums, attn_sums, bu)
    gp, gx, *out = pl.pallas_call(
        functools.partial(image_backward, pad, sent),
        out_shape=[
            jax.ShapeDtypeStruct((rows, d), bf16),
            jax.ShapeDtypeStruct((rows, feat), bf16),
            *parts,
        ],
        grid_spec=pltpu.PrefetchScalarGridSpec(
            num_scalar_prefetch=1,
            grid=(1,),
            in_specs=[whole(o.shape) for o in operands],
            out_specs=[whole((rows, d)), whole((rows, feat))] + [whole(p.shape) for p in parts],
            scratch_shapes=[pltpu.VMEM((devices * chunk, d), f32)],
        ),
        compiler_params=pltpu.CompilerParams(
            dimension_semantics=("arbitrary",), vmem_limit_bytes=LIMIT
        ),
        cost_estimate=cost(4 * rows * d * feat, x.size * 4 + wi.size * 2 + devices * chunk * d * 2),
        name="image_backward",
    )(core, *operands)
    return gp, gx, list(zip(out[:2], out[2:]))


def join_kernel(core_ref, *refs):
    core = core_ref[0]
    out_ref = refs[-1]
    groups = list(zip(refs[:-1:2], refs[1:-1:2]))
    at = 0
    for i in range(groups[0][0].shape[0]):
        for first in (0, 1):
            for own_ref, came_ref in groups:
                own, came = own_ref[i].astype(f32), came_ref[i].astype(f32)
                rows = own.shape[0]
                out_ref[at : at + rows, :] = jnp.where(core == first, own, came)
                at += rows


def join_blocks(core, halves, shape, step):
    pairs, rows, width = halves[0].shape
    per = width // (2 * rows)
    down, right = step
    block = pl.BlockSpec((per, rows, width), lambda s, *_: (s, 0, 0))
    return pl.pallas_call(
        join_kernel,
        out_shape=jax.ShapeDtypeStruct(shape, f32),
        grid_spec=pltpu.PrefetchScalarGridSpec(
            num_scalar_prefetch=1,
            grid=(pairs // per,),
            in_specs=[block, block],
            out_specs=pl.BlockSpec((width, width), lambda s, *_: (s * down, s * right)),
        ),
        cost_estimate=cost(0, pairs * rows * width * 12),
        name="join_blocks",
    )(core, *halves)


def widen_rest_kernel(
    attn_rows, feat, picks, parts_ref, *refs
):
    squares, refs = refs[:4], refs[4:]
    img_ref, box_ref, refs = refs[0], refs[1], refs[2:]
    vectors, long_ref, refs = refs[: len(picks)], refs[len(picks)], refs[len(picks) + 1 :]
    in_buf, square_buf, img_buf, in_sem, out_sem = refs
    devices, rows, width = in_buf.shape
    img_rows = rows - attn_rows
    per = devices // 4
    loads = [
        pltpu.make_async_copy(
            parts_ref.at[j * per : (j + 1) * per], in_buf.at[j * per : (j + 1) * per], in_sem.at[j]
        )
        for j in range(4)
    ]
    for copy in loads:
        copy.start()
    stores = []

    def store(source, target):
        copy = pltpu.make_async_copy(source, target, out_sem.at[len(stores)])
        copy.start()
        stores.append(copy)

    for j in range(4):
        loads[j].wait()
        for i in range(per):
            value = in_buf[j * per + i, :attn_rows, :].astype(f32)
            square_buf[j, i * attn_rows : (i + 1) * attn_rows, :] = value
        store(square_buf.at[j], squares[j])
        for i in range(j * per, (j + 1) * per):
            value = in_buf[i, attn_rows:, :].astype(f32)
            img_buf[i * img_rows : (i + 1) * img_rows, :] = value
        first, last = [min(t * per * img_rows, feat) for t in (j, j + 1)]
        if last > first:
            store(img_buf.at[first:last], img_ref.at[first:last])
    box_ref[...] = img_buf[feat : feat + box_ref.shape[0], :]
    for pick, ref in zip(picks, vectors):
        ref[...] = img_buf[feat + pick, :]
    for i in range(long_ref.shape[0] // width):
        long_ref[i * width : (i + 1) * width] = img_buf[feat + 32 + i, :]
    for copy in stores:
        copy.wait()


def widen_rest(parts, attn_rows, feat, boxes, long, picks):
    devices, rows, width = parts.shape
    shapes = [(width, width)] * 4 + [(feat, width), (boxes, width)]
    shapes += [(width,)] * len(picks) + [(long,)]
    return pl.pallas_call(
        functools.partial(widen_rest_kernel, attn_rows, feat, picks),
        out_shape=[jax.ShapeDtypeStruct(t, f32) for t in shapes],
        in_specs=[pl.BlockSpec(memory_space=pl.ANY)],
        out_specs=[pl.BlockSpec(memory_space=pl.ANY)] * 5
        + [pl.BlockSpec(memory_space=pltpu.VMEM)] * (len(picks) + 2),
        scratch_shapes=[
            pltpu.VMEM((devices, rows, width), bf16),
            pltpu.VMEM((4, width, width), f32),
            pltpu.VMEM((devices * (rows - attn_rows), width), f32),
            pltpu.SemaphoreType.DMA((4,)),
            pltpu.SemaphoreType.DMA((8,)),
        ],
        compiler_params=pltpu.CompilerParams(vmem_limit_bytes=LIMIT),
        cost_estimate=cost(0, parts.size * 6),
        name="widen_rest",
    )(parts)


def run_feed_forward(captions, counts, n1, mixed, cot, weights, cut, wo, bu, bd, g1, g2, beta2):
    seqs = captions.shape[0]
    total, d = n1.shape
    devices = weights.shape[0]
    down = weights.shape[1] // 2
    ff = devices * down
    blocks = ff // d

    def part(rows, index):
        return pl.BlockSpec(
            (devices, rows, d), lambda s, *_: (0, index, 0), pipeline_mode=pl.Buffered(1)
        )

    if cut % 8 == 0:
        ups = [part(cut, blocks + j) for j in range(blocks)]
        up_weights = [weights] * blocks
    else:
        ups = [whole((d, d))] * blocks
        up_weights = [
            weights[:, down + j * cut : down + (j + 1) * cut].reshape(d, d) for j in range(blocks)
        ]

    L = total // seqs
    row = tile((L, d))
    wide = tile((L, ff))
    vec = whole((d,))
    shapes = [
        jax.ShapeDtypeStruct((total, d), bf16),
        jax.ShapeDtypeStruct((total, ff), bf16),
        jax.ShapeDtypeStruct((total, d), bf16),
        jax.ShapeDtypeStruct((total, ff), bf16),
        jax.ShapeDtypeStruct((total, d), f32),
        jax.ShapeDtypeStruct((total, d), bf16),
        jax.ShapeDtypeStruct((total, d), bf16),
        jax.ShapeDtypeStruct((8, d), f32),
        jax.ShapeDtypeStruct((1, ff), f32),
    ]
    return pl.pallas_call(
        feed_forward,
        out_shape=shapes,
        grid_spec=pltpu.PrefetchScalarGridSpec(
            num_scalar_prefetch=2,
            grid=(seqs,),
            in_specs=[row, row, row, part(down, 0)]
            + ups
            + [whole((d, d)), whole((ff,)), vec, vec, vec, vec],
            out_specs=[row, wide, row, wide, row, row, row, still((8, d)), still((1, ff))],
            scratch_shapes=[pltpu.VMEM((L, ff), f32), pltpu.VMEM((blocks, d, d), bf16)],
        ),
        compiler_params=pltpu.CompilerParams(
            dimension_semantics=("arbitrary",), vmem_limit_bytes=LIMIT
        ),
        cost_estimate=cost(2 * total * d * (4 * ff + d), total * (ff * 4 + d * 18) + d * ff * 4, total * ff),
        name="feed_forward",
    )(captions, counts, n1, mixed, cot, weights, *up_weights, wo, bu, bd, g1, g2, beta2)


def run_attention_backward(geometry, counts, offset, q, k, v, p, gc, gm, wq, wk, wv):
    seqs, _, L, _ = p.shape
    total, d = q.shape
    row = tile((L, d))
    half = tile((L // 2, d))
    mat = whole((d, d))
    received = geometry[0] * geometry[2]
    shapes = [jax.ShapeDtypeStruct((total, d), bf16)] * 3 + [
        jax.ShapeDtypeStruct((total // 2, d), bf16),
        jax.ShapeDtypeStruct((received, d), bf16),
        jax.ShapeDtypeStruct((8, d), f32),
    ]
    return pl.pallas_call(
        functools.partial(attention_backward, *geometry),
        out_shape=shapes,
        grid_spec=pltpu.PrefetchScalarGridSpec(
            num_scalar_prefetch=2,
            grid=(seqs,),
            in_specs=[row, row, row, tile((1, HEADS, L, L)), row, row, mat, mat, mat],
            out_specs=[row, row, row, half, still((received, d)), still((8, d))],
            scratch_shapes=[pltpu.VMEM((received, d), f32)],
        ),
        compiler_params=pltpu.CompilerParams(
            dimension_semantics=("arbitrary",), vmem_limit_bytes=LIMIT
        ),
        cost_estimate=cost(2 * total * d * (3 * d + 4 * L * 4), total * d * 20 + seqs * HEADS * L * L * 2),
        name="attention_backward",
    )(counts, offset, q, k, v, p, gc, gm, wq, wk, wv)


def weight_grad_kernel(lhs_of, rhs_of, groups, core_ref, *refs):
    lhs_refs = refs[: max(lhs_of) + 1]
    rhs_refs = refs[len(lhs_refs) : len(lhs_refs) + max(rhs_of) + 1]
    outs = refs[len(lhs_refs) + len(rhs_refs) : -1]
    acc_ref = refs[-1]
    step = pl.program_id(0)
    core = core_ref[0]
    kinds = {}
    for i, kind in enumerate(zip(lhs_of, rhs_of)):
        kinds.setdefault(kind, []).append(i)
    for (a, b), steps in kinds.items():

        @pl.when((step >= steps[0]) & (step <= steps[-1]))
        def _(a=a, b=b):
            value = tn(lhs_refs[a][...], rhs_refs[b][...]).astype(bf16)
            acc_ref[...] = value.reshape(acc_ref.shape)

    for i in range(outs[0].shape[0]):
        for side in (0, 1):
            at = 0
            for ref in outs[side * groups : (side + 1) * groups]:
                rows = ref.shape[1]
                ref[i] = acc_ref[2 * i + (1 - core if side == 0 else core), at : at + rows, :]
                at += rows


def weight_grads(core, devices, lhs, rhs, lhs_of, rhs_of, lhs_maps, rhs_maps, width, groups, name):
    steps = len(lhs_of)
    total = lhs[0].shape[0]
    rows = steps * width // devices
    per = width // rows
    outs = [rows // groups] * (2 * groups)
    specs = [pl.BlockSpec((total, width), m) for m in lhs_maps + rhs_maps]
    out = pl.pallas_call(
        functools.partial(weight_grad_kernel, lhs_of, rhs_of, groups),
        out_shape=[jax.ShapeDtypeStruct((devices // 2, r, width), bf16) for r in outs],
        grid_spec=pltpu.PrefetchScalarGridSpec(
            num_scalar_prefetch=1,
            grid=(steps,),
            in_specs=specs,
            out_specs=[pl.BlockSpec((per // 2, r, width), lambda s, *_: (s, 0, 0)) for r in outs],
            scratch_shapes=[pltpu.VMEM((per, rows, width), bf16)],
        ),
        compiler_params=pltpu.CompilerParams(
            dimension_semantics=("arbitrary",), vmem_limit_bytes=LIMIT
        ),
        cost_estimate=cost(2 * total * width * width * steps, steps * width * (total + width) * 2),
        name=name,
    )(core, *lhs, *rhs)
    return list(zip(out[:groups], out[groups:]))


def axis_bits(name):
    size = lax.axis_size(name)
    bits = []
    step = 1
    while step < size:
        bits.append((name, step))
        step *= 2
    return bits


def bit_layout():
    return axis_bits("enc")[::-1] + axis_bits("dp")[::-1]


def my_bit(bit):
    return (lax.axis_index(bit[0]) // bit[1]) % 2


def swap_bit(tensor, bit):
    name, step = bit
    size = lax.axis_size(name)
    return lax.ppermute(tensor, name, [(i, i ^ step) for i in range(size)])


def stage_orders():
    dp_bits, enc_bits = axis_bits("dp"), axis_bits("enc")
    near, middle = dp_bits[:1], dp_bits[1:]
    half = len(middle) // 2
    return (
        near + middle + enc_bits,
        near + middle[half:] + middle[:half] + enc_bits,
    )


def add_low(kept, came):
    return (kept.astype(f32) + came.astype(f32)).astype(bf16)


class Scatter:
    def __init__(self, away, kept, order):
        self.order = list(order)
        self.layout = bit_layout()
        self.value = (away, kept)
        self.fresh = True

    def stage(self):
        bit = self.order.pop(0)
        axis = self.layout.index(bit)
        self.layout.remove(bit)
        if self.fresh:
            away, kept = self.value
            self.fresh = False
        else:
            mine = my_bit(bit)
            away, kept = [
                add_low(*[lax.dynamic_index_in_dim(t, i, axis, keepdims=False) for t in self.value])
                for i in (1 - mine, mine)
            ]
        shape = (2,) * len(self.layout) + kept.shape[-2:]
        self.value = (kept.reshape(shape), swap_bit(away, bit).reshape(shape))
        return away

    def total(self):
        return add_low(*self.value)


class Gather:
    def __init__(self, rows, order, layout=()):
        self.order = list(order)[::-1]
        self.layout = list(layout)
        self.value = rows

    def stage(self):
        bit = self.order.pop(0)
        sent = self.value
        came = swap_bit(sent, bit)
        self.layout = [b for b in bit_layout() if b in self.layout or b == bit]
        axis = self.layout.index(bit)
        shape = sent.shape[:axis] + (2,) + sent.shape[axis:]
        at = lax.broadcasted_iota(jnp.int32, shape, axis)
        self.value = jnp.where(
            at == my_bit(bit), jnp.expand_dims(sent, axis), jnp.expand_dims(came, axis)
        )
        return sent

    def rows(self):
        return self.value.reshape((-1,) + self.value.shape[-2:])

    def halves(self):
        (bit,) = self.order
        came = swap_bit(self.value, bit)
        shape = (-1,) + came.shape[-2:]
        return self.value.reshape(shape), came.reshape(shape)

    def split(self, at, orders):
        values = (self.value[..., :at, :], self.value[..., at:, :])
        return [
            Gather(value, [b for b in order if b not in self.layout], self.layout)
            for value, order in zip(values, orders)
        ]


def fence(movers, *values):
    leaves, tree = jax.tree.flatten(([m.value for m in movers], values))
    held, values = jax.tree.unflatten(tree, lax.optimization_barrier(leaves))
    for mover, value in zip(movers, held):
        mover.value = value
    return values


def in_turn(*movers):
    sent = []
    for mover in movers:
        fence([mover], sent)
        sent = mover.stage()


class Sum:
    def __init__(self, parts, orders):
        far = len(axis_bits("enc"))
        self.movers = [Scatter(*part, order) for part, order in zip(parts, orders)]
        self.steps = [self.run] * (len(orders[0]) - far) + [self.merge] + [self.run] * (far - 1)

    @property
    def value(self):
        return [m.value for m in self.movers]

    @value.setter
    def value(self, values):
        for mover, value in zip(self.movers, values):
            mover.value = value

    def stage(self):
        return self.steps.pop(0)() if self.steps else []

    def run(self):
        return [mover.stage() for mover in self.movers]

    def merge(self):
        first = self.movers[0]
        first.value = tuple(jnp.concatenate(t, -2) for t in zip(*[m.value for m in self.movers]))
        self.movers = [first]
        return self.run()

    def total(self):
        return self.movers[0].total()


def body(
    text,
    region_feats,
    boxes,
    caption_count,
    region_count,
    region_offset,
    w_img,
    w_box,
    b_img,
    g_reg,
    beta_reg,
    w_query,
    b_query,
    w_key,
    w_value,
    b_value,
    w_out,
    b_out,
    g_one,
    beta_one,
    w_up,
    b_up,
    w_down,
    b_down,
    g_two,
    beta_two,
    cotangent,
):
    axes = ("enc", "dp")
    orders = stage_orders()
    model_width = text.shape[1]
    ff_blocks = w_up.shape[1] // model_width
    cut = w_query.shape[0]
    far = axis_bits("enc")

    middle = len(orders[0]) - 1 - len(far)
    core = (lax.axis_index("dp") % 2).astype(jnp.int32).reshape(1)

    up_blocks = w_up.reshape(cut, ff_blocks, model_width).transpose(1, 0, 2)
    ff_shard = jnp.concatenate([w_down, up_blocks.reshape(ff_blocks * cut, model_width)], 0)
    rows_up = cut
    img = Gather(w_img, far)
    attn = Gather(jnp.concatenate([w_query, w_key, w_value, w_out], 0), far)
    img.stage()
    fence([img, attn])
    while img.order:
        img.stage()
        attn.stage()
        (ff_shard,) = fence([img, attn], ff_shard)
    ff_weights = lax.all_gather(ff_shard, axes, axis=0)
    img = img.split(w_img.shape[0] // 2, orders)
    attn.stage()
    for _ in range(middle):
        for part in img:
            part.stage()
        fence([*img, attn])
    attn = attn.split(2 * cut, orders)
    img_halves = [t for part in img for t in part.halves()]
    for part in attn:
        part.stage()
    device_count = lax.axis_size(axes)
    seq_count = caption_count.shape[0]
    sent_rows, feat = region_feats.shape
    per_peer = sent_rows // device_count
    pad = 8 * (-(-per_peer // 8))
    pad = 1 << (pad - 1).bit_length()
    box_count = boxes.shape[0]
    geometry = (pad, per_peer, device_count)
    pre_norm, encoded, img_full = run_image_encode(
        geometry, core, region_feats, boxes, img_halves, w_box, b_img, g_reg, beta_reg
    )
    img_full = img_full.reshape(feat, model_width)
    (encoded,) = fence(attn, encoded)
    received = lax.all_to_all(encoded, axes, split_axis=0, concat_axis=0, tiled=True)
    for _ in range(middle - 1):
        for part in attn:
            part.stage()
        (received,) = fence(attn, received)
    for part in attn:
        part.stage()
    query_full, key_full, value_full, out_full = [
        t.reshape(-1, model_width)
        for part in attn
        for t in (part.rows()[:, :cut], part.rows()[:, cut:])
    ]
    (
        hidden_in,
        queries,
        keys,
        values,
        probs,
        context,
        mixed,
        normed_one,
    ) = run_attention_forward(
        geometry,
        caption_count,
        region_count,
        region_offset,
        received,
        text,
        query_full,
        key_full,
        value_full,
        out_full,
        b_query,
        b_value,
        b_out,
        g_one,
        beta_one,
    )
    (
        output,
        activated,
        grad_down_out,
        grad_gate,
        grad_mixed,
        grad_attn,
        grad_context,
        sums,
        grad_b_up,
    ) = run_feed_forward(
        caption_count,
        region_count,
        normed_one,
        mixed,
        cotangent,
        ff_weights,
        rows_up,
        out_full,
        b_up,
        b_down,
        g_one,
        g_two,
        beta_two,
    )
    fixed = lambda s, *_: (0, 0)
    moving = lambda s, *_: (0, s)
    (down,) = weight_grads(
        core,
        device_count,
        [activated],
        [grad_down_out],
        [0] * ff_blocks,
        [0] * ff_blocks,
        [moving],
        [fixed],
        model_width,
        1,
        "grad_w_down",
    )
    (up,) = weight_grads(
        core,
        device_count,
        [normed_one],
        [grad_gate],
        [0] * ff_blocks,
        [0] * ff_blocks,
        [fixed],
        [moving],
        model_width,
        1,
        "grad_w_up",
    )
    ff = Sum([down, up], orders)
    ff.stage()
    sent = ff.stage()
    grad_context, _ = fence([], grad_context, sent)
    grad_query, grad_keys, grad_values, grad_text, grad_slots, attn_sums = run_attention_backward(
        geometry,
        region_count,
        region_offset,
        queries,
        keys,
        values,
        probs,
        grad_context,
        grad_mixed,
        query_full,
        key_full,
        value_full,
    )
    grad_query, grad_keys, grad_values, grad_slots, attn_sums = fence(
        [ff], grad_query, grad_keys, grad_values, grad_slots, attn_sums
    )
    back = lax.all_to_all(grad_slots, axes, split_axis=0, concat_axis=0, tiled=True)
    attn_parts = weight_grads(
        core,
        device_count,
        [hidden_in, context],
        [grad_query, grad_keys, grad_values, grad_attn],
        [0, 0, 0, 1],
        [0, 1, 2, 3],
        [fixed] * 2,
        [fixed] * 4,
        model_width,
        2,
        "grad_w_attn",
    )
    attn = Sum(attn_parts, orders)
    (back,) = fence([ff, attn], back)
    in_turn(ff, attn)
    small_rows = 40
    chunk = 8 * (-(-(feat + small_rows) // (8 * device_count)))
    grad_pre, grad_feats, img_parts = run_image_backward(
        geometry,
        chunk,
        core,
        region_feats,
        boxes,
        img_full,
        pre_norm,
        back,
        g_reg,
        sums,
        attn_sums,
        grad_b_up.reshape(ff_blocks, model_width),
    )
    img = Sum(img_parts, orders)
    fence([ff, attn, img])
    while ff.steps:
        in_turn(ff, attn, img)
        fence([ff, attn, img])
    while img.steps:
        in_turn(attn, img)
        fence([attn, img])
    ff = Gather(ff.total(), far)
    rest = jnp.concatenate([attn.total(), img.total()], 0)
    rest_all = lax.all_gather(rest, axes, axis=0)
    fence([ff], rest)
    while ff.order:
        ff.stage()
        fence([ff])
    down, up = ff.split(w_down.shape[0], orders)
    while len(down.order) > 1:
        down.stage()
        up.stage()
        fence([down, up])
    down_halves, up_halves = down.halves(), up.halves()
    grad_w_down = join_blocks(
        core, down_halves, (ff_blocks * model_width, model_width), (1, 0)
    )
    grad_w_up = join_blocks(core, up_halves, (model_width, ff_blocks * model_width), (0, 1))
    grad_boxes = jnp.einsum("cd,rd->cr", w_box, grad_pre, preferred_element_type=f32).astype(bf16)
    (
        grad_w_query,
        grad_w_key,
        grad_w_value,
        grad_w_out,
        grad_w_img,
        grad_w_box,
        grad_b_img,
        grad_g_reg,
        grad_beta_reg,
        grad_g_two,
        grad_beta_two,
        grad_b_down,
        grad_g_one,
        grad_beta_one,
        grad_b_out,
        grad_b_query,
        grad_b_value,
        grad_b_up,
    ) = widen_rest(
        rest_all,
        4 * cut,
        feat,
        box_count,
        b_up.shape[0],
        (8, 9, 10, 16, 17, 18, 19, 20, 21, 24, 25),
    )
    return (
        output,
        grad_text,
        grad_feats,
        grad_boxes,
        grad_w_img,
        grad_w_box,
        grad_b_img,
        grad_g_reg,
        grad_beta_reg,
        grad_w_query,
        grad_b_query,
        grad_w_key,
        grad_w_value,
        grad_b_value,
        grad_w_out,
        grad_b_out,
        grad_g_one,
        grad_beta_one,
        grad_w_up,
        grad_b_up,
        grad_w_down,
        grad_b_down,
        grad_g_two,
        grad_beta_two,
    )


def solution(mesh):
    return jax.shard_map(
        body,
        mesh=mesh,
        in_specs=(
            P(("enc", "dp"), None),
            P(("enc", "dp"), None),
            P(None, ("enc", "dp")),
            P(("enc", "dp")),
            P(("enc", "dp")),
            P(("enc", "dp")),
            P(("enc", "dp"), None),
            P(),
            P(),
            P(),
            P(),
            P(("enc", "dp"), None),
            P(),
            P(("enc", "dp"), None),
            P(("enc", "dp"), None),
            P(),
            P(("enc", "dp"), None),
            P(),
            P(),
            P(),
            P(("enc", "dp"), None),
            P(),
            P(("enc", "dp"), None),
            P(),
            P(),
            P(),
            P(("enc", "dp"), None),
        ),
        out_specs=(
            P(("enc", "dp"), None),
            P(("enc", "dp"), None),
            P(("enc", "dp"), None),
            P(None, ("enc", "dp")),
            P(),
            P(),
            P(),
            P(),
            P(),
            P(),
            P(),
            P(),
            P(),
            P(),
            P(),
            P(),
            P(),
            P(),
            P(),
            P(),
            P(),
            P(),
            P(),
            P(),
        ),
        check_vma=False,
    )
```

```python
import functools
import math

import jax
import jax.numpy as jnp
from jax import lax
from jax.experimental import pallas as pl
from jax.experimental.pallas import tpu as pltpu
from jax.sharding import PartitionSpec as P

HEADS = 12
epsilon = 1e-05
f32, bf16 = jnp.float32, jnp.bfloat16

ERFC_P = 0.35
ERFC_C = (
    0.19567911,
    0.22612264,
    0.02080242,
    0.63768037,
    -0.6386366,
    0.75239514,
    -0.19404308,
)


def nn(a, b):
    return lax.dot_general(a, b, (((1,), (0,)), ((), ())), preferred_element_type=f32)


def nt(a, b):
    return lax.dot_general(a, b, (((1,), (1,)), ((), ())), preferred_element_type=f32)


def tn(a, b):
    return lax.dot_general(a, b, (((0,), (0,)), ((), ())), preferred_element_type=f32)


def norm_parts(values):
    centered = values - jnp.mean(values, -1, keepdims=True)
    inverse = lax.rsqrt(jnp.mean(centered * centered, -1, keepdims=True) + epsilon)
    return centered * inverse, inverse


def norm_back(upstream, normed, inverse, gain):
    weighted = upstream * gain
    return inverse * (
        weighted
        - jnp.mean(weighted, -1, keepdims=True)
        - normed * jnp.mean(weighted * normed, -1, keepdims=True)
    )


def gelu_parts(x):
    e = jnp.exp(-0.5 * x * x)
    t = 1.0 / (1.0 + (ERFC_P * math.sqrt(0.5)) * jnp.abs(x))
    acc = jnp.full_like(t, 0.5 * ERFC_C[-1])
    for c in ERFC_C[-2::-1]:
        acc = acc * t + 0.5 * c
    tail = acc * t * e
    phi = jnp.where(x >= 0, 1.0 - tail, tail)
    return x * phi, phi + x * (e * (1.0 / math.sqrt(2.0 * math.pi)))


def one_hot(wanted, live, rows, pad, sent, devices, offset):
    row = lax.broadcasted_iota(jnp.int32, (1, rows), 1)
    shift = pad.bit_length() - 1
    turn = lax.shift_right_logical(row, shift) - offset
    turn = jnp.where(turn < 0, turn + devices, turn)
    inside = jnp.bitwise_and(row, pad - 1)
    arrival = jnp.where(inside < sent, inside * devices + turn, -1)
    return ((wanted == arrival) & live).astype(bf16)


def spread(pad, sent, rows, padded):
    to = lax.broadcasted_iota(jnp.int32, (padded, 1), 0)
    shift = pad.bit_length() - 1
    inside = jnp.bitwise_and(to, pad - 1)
    source = jnp.where(inside < sent, lax.shift_right_logical(to, shift) * sent + inside, -1)
    return (source == lax.broadcasted_iota(jnp.int32, (1, rows), 1)).astype(bf16)


def image_encode(
    pad, sent, core_ref,
    x_ref, box_ref, wb_ref, bi_ref, gr_ref, betar_ref, *refs,
):
    *halves, pre_ref, enc_ref, wi_ref = refs
    core = core_ref[0]
    at = 0
    for own_ref, came_ref in zip(halves[::2], halves[1::2]):
        pairs, rows, _ = own_ref.shape
        for i in range(pairs):
            wi_ref[2 * i + core, at : at + rows, :] = own_ref[i]
            wi_ref[2 * i + 1 - core, at : at + rows, :] = came_ref[i]
        at += rows
    weight = wi_ref[...].reshape(x_ref.shape[1], wi_ref.shape[2])
    pre = nn(x_ref[...], weight) + tn(box_ref[...], wb_ref[...]) + bi_ref[...]
    pre_ref[...] = pre
    normed, _ = norm_parts(pre)
    encoded = (normed * gr_ref[...] + betar_ref[...]).astype(bf16)
    enc_ref[...] = nn(spread(pad, sent, x_ref.shape[0], enc_ref.shape[0]), encoded).astype(bf16)


def attention_forward(
    pad, sent, devices,
    captions, counts, offset,
    enc_ref, text_ref,
    wq_ref, wk_ref, wv_ref, wo_ref, bq_ref, bv_ref, bo_ref, g_ref, beta_ref,
    h_ref, q_ref, k_ref, v_ref, p_ref, c_ref, mixed_ref, n_ref,
):
    s = pl.program_id(0)
    text_len = text_ref.shape[0]
    rows, width = h_ref.shape
    hd = width // HEADS
    start = jnp.int32(0)
    for i in range(captions.shape[0]):
        start = start + jnp.where(s > i, counts[i], 0)
    slot = lax.broadcasted_iota(jnp.int32, (rows - text_len, 1), 0)
    taken = one_hot(
        slot + start, slot < counts[s], enc_ref.shape[0], pad, sent, devices, offset[0]
    )
    h_ref[:text_len, :] = text_ref[...]
    h_ref[text_len:, :] = nn(taken, enc_ref[...]).astype(bf16)
    h = h_ref[...]
    q = (nn(h, wq_ref[...]) + bq_ref[...]).astype(bf16)
    k = nn(h, wk_ref[...]).astype(bf16)
    v = (nn(h, wv_ref[...]) + bv_ref[...]).astype(bf16)
    q_ref[...] = q
    k_ref[...] = k
    v_ref[...] = v
    row = lax.broadcasted_iota(jnp.int32, (rows, 1), 0)
    live = (row < captions[s]) | ((row >= text_len) & (row < text_len + counts[s]))
    lane = lax.broadcasted_iota(jnp.int32, (1, 2 * hd), 1)
    masks = [(lane < hd).astype(bf16), (lane >= hd).astype(bf16)]
    scaled = q * jnp.asarray(hd**-0.5, bf16)
    for pair in range(HEADS // 2):
        cols = slice(pair * 2 * hd, (pair + 1) * 2 * hd)
        context = None
        for j in range(2):
            scores = nt(k[:, cols], scaled[:, cols] * masks[j])
            scores = jnp.where(live, scores, -1e30)
            top = jnp.max(scores, 0, keepdims=True)
            e = jnp.exp(scores - top)
            p = (e * (1.0 / jnp.sum(e, 0, keepdims=True))).astype(bf16)
            p_ref[0, 2 * pair + j] = p
            part = tn(p, v[:, cols] * masks[j])
            context = part if context is None else context + part
        c_ref[:, cols] = context.astype(bf16)
    mixed = h.astype(f32) + nn(c_ref[...], wo_ref[...]) + bo_ref[...]
    mixed_ref[...] = mixed
    normed, _ = norm_parts(mixed)
    n_ref[...] = (normed * g_ref[...] + beta_ref[...]).astype(bf16)


def image_backward(
    pad, sent, core_ref,
    x_ref, box_ref, wi_ref, pre_ref, back_ref, gr_ref, sums_ref, attn_sums_ref, bu_ref,
    gp_ref, gx_ref, *outs,
):
    *outs, acc_ref = outs
    rows, feat = x_ref.shape
    width = pre_ref.shape[1]
    grad = tn(spread(pad, sent, rows, back_ref.shape[0]), back_ref[...])
    normed, inverse = norm_parts(pre_ref[...])
    gp = norm_back(grad, normed, inverse, gr_ref[...]).astype(bf16)
    gp_ref[...] = gp
    acc_ref[:feat, :] = tn(x_ref[...], gp)
    acc_ref[feat:, :] = jnp.zeros((acc_ref.shape[0] - feat, width), f32)
    acc_ref[feat : feat + box_ref.shape[0], :] = nn(box_ref[...], gp)
    at = feat + 8
    acc_ref[at : at + 1, :] = jnp.sum(gp.astype(f32), 0, keepdims=True)
    acc_ref[at + 1 : at + 2, :] = jnp.sum(grad * normed, 0, keepdims=True)
    acc_ref[at + 2 : at + 3, :] = jnp.sum(grad, 0, keepdims=True)
    acc_ref[at + 8 : at + 16, :] = sums_ref[...]
    acc_ref[at + 16 : at + 24, :] = attn_sums_ref[...]
    acc_ref[at + 24 : at + 24 + bu_ref.shape[0], :] = bu_ref[...]
    core = core_ref[0]
    half = len(outs) // 2
    chunk = sum(ref.shape[1] for ref in outs[:half])
    for i in range(outs[0].shape[0]):
        for side in (0, 1):
            at = (2 * i + (1 - core if side == 0 else core)) * chunk
            for ref in outs[side * half : (side + 1) * half]:
                rows_here = ref.shape[1]
                ref[i] = acc_ref[pl.ds(pl.multiple_of(at, 8), rows_here), :].astype(bf16)
                at = at + rows_here
    gx_ref[...] = nt(gp, wi_ref[...]).astype(bf16)


def feed_forward(
    captions, counts, n_ref, mixed_ref, cot_ref, wd_ref, *refs,
):
    blocks = len(refs) - 17
    up_refs = refs[:blocks]
    wu_ref = refs[-1]

    @pl.when(pl.program_id(0) == 0)
    def _():
        for j in range(blocks):
            wu_ref[j] = up_refs[j][...].astype(f32).reshape(wu_ref.shape[1:]).astype(bf16)

    feed_forward_rows(captions, counts, n_ref, mixed_ref, cot_ref, wu_ref, wd_ref, *refs[blocks:-1])


def feed_forward_rows(
    captions, counts, n_ref, mixed_ref, cot_ref, wu_ref, wd_ref, wo_ref, bu_ref, bd_ref, g1_ref, g2_ref, beta2_ref,
    out_ref, act_ref, gdo_ref, gg_ref, gm_ref, ga_ref, gc_ref, sums_ref, bu_sum_ref, d_ref,
):
    s = pl.program_id(0)
    n1 = n_ref[...]
    rows, width = n1.shape
    ff = act_ref.shape[1]
    step = width
    per = wd_ref.shape[0] * step // ff

    def down_rows(j):
        return wd_ref[j // step * per : (j // step + 1) * per].reshape(step, width)

    @pl.when(s == 0)
    def _():
        sums_ref[...] = jnp.zeros_like(sums_ref)
        bu_sum_ref[...] = jnp.zeros_like(bu_sum_ref)

    second = n1.astype(f32) + bd_ref[...]
    for j in range(0, ff, step):
        cols = slice(j, j + step)
        gate = nn(n1, wu_ref[j // step]) + bu_ref[cols]
        act, d = gelu_parts(gate)
        act = act.astype(bf16)
        act_ref[:, cols] = act
        d_ref[:, cols] = d
        second = second + nn(act, down_rows(j))
    normed, inverse = norm_parts(second)
    text_len = rows // 2
    row = lax.broadcasted_iota(jnp.int32, (rows, 1), 0)
    live = (row < captions[s]) | ((row >= text_len) & (row < text_len + counts[s]))
    live = live.astype(f32)
    out_ref[...] = ((normed * g2_ref[...] + beta2_ref[...]) * live).astype(bf16)
    up = cot_ref[...].astype(f32) * live

    def add(i, value):
        sums_ref[i : i + 1, :] += jnp.sum(value, 0, keepdims=True)

    add(0, up * normed)
    add(1, up)
    gsi = norm_back(up, normed, inverse, g2_ref[...])
    gdo = gsi.astype(bf16)
    gdo_ref[...] = gdo
    add(2, gdo.astype(f32))
    first = gsi
    for j in range(0, ff, step):
        cols = slice(j, j + step)
        gg = (nt(gdo, down_rows(j)) * d_ref[:, cols]).astype(bf16)
        gg_ref[:, cols] = gg
        bu_sum_ref[:, cols] += jnp.sum(gg.astype(f32), 0, keepdims=True)
        first = first + nt(gg, wu_ref[j // step])
    normed, inverse = norm_parts(mixed_ref[...])
    add(3, first * normed)
    add(4, first)
    gm = norm_back(first, normed, inverse, g1_ref[...])
    gm_ref[...] = gm
    ga = gm.astype(bf16)
    ga_ref[...] = ga
    add(5, ga.astype(f32))
    gc_ref[...] = nt(ga, wo_ref[...]).astype(bf16)


def attention_backward(
    pad, sent, devices,
    counts, offset,
    q_ref, k_ref, v_ref, p_ref, gc_ref, gm_ref, wq_ref, wk_ref, wv_ref,
    gq_ref, gk_ref, gv_ref, gt_ref, gs_ref, sums_ref, acc_ref,
):
    s = pl.program_id(0)
    rows, width = q_ref.shape
    hd = width // HEADS
    scale = hd**-0.5

    @pl.when(s == 0)
    def _():
        sums_ref[...] = jnp.zeros_like(sums_ref)

    lane = lax.broadcasted_iota(jnp.int32, (1, 2 * hd), 1)
    masks = [(lane < hd).astype(bf16), (lane >= hd).astype(bf16)]
    for pair in range(HEADS // 2):
        cols = slice(pair * 2 * hd, (pair + 1) * 2 * hd)
        gq = gk = gv = None
        for j in range(2):
            p = p_ref[0, 2 * pair + j]
            gc = gc_ref[:, cols] * masks[j]
            gp = nt(v_ref[:, cols], gc)
            part = nn(p, gc)
            gv = part if gv is None else gv + part
            pf = p.astype(f32)
            weighted = pf * gp
            gs = (weighted - pf * jnp.sum(weighted, 0, keepdims=True)).astype(bf16)
            part = tn(gs, k_ref[:, cols] * masks[j])
            gq = part if gq is None else gq + part
            part = nn(gs, q_ref[:, cols] * masks[j])
            gk = part if gk is None else gk + part
        gq_ref[:, cols] = (gq * scale).astype(bf16)
        gk_ref[:, cols] = (gk * scale).astype(bf16)
        gv_ref[:, cols] = gv.astype(bf16)
    gq, gk, gv = gq_ref[...], gk_ref[...], gv_ref[...]
    sums_ref[0:1, :] += jnp.sum(gq.astype(f32), 0, keepdims=True)
    sums_ref[1:2, :] += jnp.sum(gv.astype(f32), 0, keepdims=True)
    hidden = gm_ref[...] + nt(gq, wq_ref[...]) + nt(gk, wk_ref[...]) + nt(gv, wv_ref[...])
    text_len = gt_ref.shape[0]
    gt_ref[...] = hidden[:text_len].astype(bf16)
    start = jnp.int32(0)
    for i in range(counts.shape[0]):
        start = start + jnp.where(s > i, counts[i], 0)
    slot = lax.broadcasted_iota(jnp.int32, (rows - text_len, 1), 0)
    taken = one_hot(
        slot + start, slot < counts[s], acc_ref.shape[0], pad, sent, devices, offset[0]
    )
    part = tn(taken, hidden[text_len:].astype(bf16))

    @pl.when(s == 0)
    def _():
        acc_ref[...] = part

    @pl.when(s > 0)
    def _():
        acc_ref[...] += part

    @pl.when(s == pl.num_programs(0) - 1)
    def _():
        gs_ref[...] = acc_ref[...].astype(bf16)


def whole(shape):
    return pl.BlockSpec(shape, lambda s, *_: (0,) * len(shape), pipeline_mode=pl.Buffered(1))


def tile(shape):
    return pl.BlockSpec(shape, lambda s, *_: (s,) + (0,) * (len(shape) - 1))


def still(shape):
    return pl.BlockSpec(shape, lambda s, *_: (0,) * len(shape))


LIMIT = 60 * 1024 * 1024


def cost(flops, moved, exps=0):
    return pl.CostEstimate(flops=int(flops), bytes_accessed=int(moved), transcendentals=int(exps))


def run_image_encode(geometry, core, x, boxes, halves, wb, bi, gr, betar):
    pad, sent, devices = geometry
    rows, feat = x.shape
    d = wb.shape[1]
    operands = (x, boxes, wb, bi, gr, betar, *halves)
    shapes = [
        jax.ShapeDtypeStruct((rows, d), f32),
        jax.ShapeDtypeStruct((pad * devices, d), bf16),
        jax.ShapeDtypeStruct((devices, feat // devices, d), bf16),
    ]
    return pl.pallas_call(
        functools.partial(image_encode, pad, sent),
        out_shape=shapes,
        grid_spec=pltpu.PrefetchScalarGridSpec(
            num_scalar_prefetch=1,
            grid=(1,),
            in_specs=[whole(t.shape) for t in operands],
            out_specs=[whole(t.shape) for t in shapes],
        ),
        compiler_params=pltpu.CompilerParams(vmem_limit_bytes=LIMIT),
        cost_estimate=cost(2 * rows * d * feat, x.size * 2 + feat * d * 4 + rows * d * 6),
        name="image_encode",
    )(core, *operands)


def run_attention_forward(
    geometry, captions, counts, offset, enc, text, wq, wk, wv, wo, bq, bv, bo, g1, beta1
):
    seqs = captions.shape[0]
    text_rows, d = text.shape
    total = 2 * text_rows
    L = total // seqs
    row = tile((L, d))
    vec = whole((d,))
    mat = whole((d, d))
    shapes = (
        [jax.ShapeDtypeStruct((total, d), bf16)] * 4
        + [
            jax.ShapeDtypeStruct((seqs, HEADS, L, L), bf16),
            jax.ShapeDtypeStruct((total, d), bf16),
            jax.ShapeDtypeStruct((total, d), f32),
            jax.ShapeDtypeStruct((total, d), bf16),
        ]
    )
    return pl.pallas_call(
        functools.partial(attention_forward, *geometry),
        out_shape=shapes,
        grid_spec=pltpu.PrefetchScalarGridSpec(
            num_scalar_prefetch=3,
            grid=(seqs,),
            in_specs=[whole(enc.shape), tile((L // 2, d))] + [mat] * 4 + [vec] * 5,
            out_specs=[row] * 4 + [tile((1, HEADS, L, L))] + [row] * 3,
        ),
        compiler_params=pltpu.CompilerParams(
            dimension_semantics=("arbitrary",), vmem_limit_bytes=LIMIT
        ),
        cost_estimate=cost(
            2 * total * d * (4 * d + 2 * L * 4),
            total * d * 18 + seqs * HEADS * L * L * 2,
            seqs * HEADS * L * L,
        ),
        name="attention_forward",
    )(
        captions, counts, offset, enc, text,
        wq, wk, wv, wo, bq, bv, bo, g1, beta1,
    )


def run_image_backward(geometry, chunk, core, x, boxes, wi, pre, back, gr, sums, attn_sums, bu):
    pad, sent, devices = geometry
    rows, feat = x.shape
    d = pre.shape[1]
    first = 8 * (-(-chunk // 16))
    parts = [
        jax.ShapeDtypeStruct((devices // 2, r, d), bf16) for r in (first, chunk - first) * 2
    ]
    operands = (x, boxes, wi, pre, back, gr, sums, attn_sums, bu)
    gp, gx, *out = pl.pallas_call(
        functools.partial(image_backward, pad, sent),
        out_shape=[
            jax.ShapeDtypeStruct((rows, d), bf16),
            jax.ShapeDtypeStruct((rows, feat), bf16),
            *parts,
        ],
        grid_spec=pltpu.PrefetchScalarGridSpec(
            num_scalar_prefetch=1,
            grid=(1,),
            in_specs=[whole(o.shape) for o in operands],
            out_specs=[whole((rows, d)), whole((rows, feat))] + [whole(p.shape) for p in parts],
            scratch_shapes=[pltpu.VMEM((devices * chunk, d), f32)],
        ),
        compiler_params=pltpu.CompilerParams(
            dimension_semantics=("arbitrary",), vmem_limit_bytes=LIMIT
        ),
        cost_estimate=cost(4 * rows * d * feat, x.size * 4 + wi.size * 2 + devices * chunk * d * 2),
        name="image_backward",
    )(core, *operands)
    return gp, gx, list(zip(out[:2], out[2:]))


def join_kernel(core_ref, *refs):
    core = core_ref[0]
    out_ref = refs[-1]
    groups = list(zip(refs[:-1:2], refs[1:-1:2]))
    at = 0
    for i in range(groups[0][0].shape[0]):
        for first in (0, 1):
            for own_ref, came_ref in groups:
                own, came = own_ref[i].astype(f32), came_ref[i].astype(f32)
                rows = own.shape[0]
                out_ref[at : at + rows, :] = jnp.where(core == first, own, came)
                at += rows


def join_blocks(core, halves, shape, step):
    pairs, rows, width = halves[0].shape
    per = width // (2 * rows)
    down, right = step
    block = pl.BlockSpec((per, rows, width), lambda s, *_: (s, 0, 0))
    return pl.pallas_call(
        join_kernel,
        out_shape=jax.ShapeDtypeStruct(shape, f32),
        grid_spec=pltpu.PrefetchScalarGridSpec(
            num_scalar_prefetch=1,
            grid=(pairs // per,),
            in_specs=[block, block],
            out_specs=pl.BlockSpec((width, width), lambda s, *_: (s * down, s * right)),
        ),
        cost_estimate=cost(0, pairs * rows * width * 12),
        name="join_blocks",
    )(core, *halves)


def widen_rest_kernel(
    attn_rows, feat, picks, parts_ref, *refs
):
    squares, refs = refs[:4], refs[4:]
    img_ref, box_ref, refs = refs[0], refs[1], refs[2:]
    vectors, long_ref, refs = refs[: len(picks)], refs[len(picks)], refs[len(picks) + 1 :]
    in_buf, square_buf, img_buf, in_sem, out_sem = refs
    devices, rows, width = in_buf.shape
    img_rows = rows - attn_rows
    per = devices // 4
    loads = [
        pltpu.make_async_copy(
            parts_ref.at[j * per : (j + 1) * per], in_buf.at[j * per : (j + 1) * per], in_sem.at[j]
        )
        for j in range(4)
    ]
    for copy in loads:
        copy.start()
    stores = []

    def store(source, target):
        copy = pltpu.make_async_copy(source, target, out_sem.at[len(stores)])
        copy.start()
        stores.append(copy)

    for j in range(4):
        loads[j].wait()
        for i in range(per):
            value = in_buf[j * per + i, :attn_rows, :].astype(f32)
            square_buf[j, i * attn_rows : (i + 1) * attn_rows, :] = value
        store(square_buf.at[j], squares[j])
        for i in range(j * per, (j + 1) * per):
            value = in_buf[i, attn_rows:, :].astype(f32)
            img_buf[i * img_rows : (i + 1) * img_rows, :] = value
        first, last = [min(t * per * img_rows, feat) for t in (j, j + 1)]
        if last > first:
            store(img_buf.at[first:last], img_ref.at[first:last])
    box_ref[...] = img_buf[feat : feat + box_ref.shape[0], :]
    for pick, ref in zip(picks, vectors):
        ref[...] = img_buf[feat + pick, :]
    for i in range(long_ref.shape[0] // width):
        long_ref[i * width : (i + 1) * width] = img_buf[feat + 32 + i, :]
    for copy in stores:
        copy.wait()


def widen_rest(parts, attn_rows, feat, boxes, long, picks):
    devices, rows, width = parts.shape
    shapes = [(width, width)] * 4 + [(feat, width), (boxes, width)]
    shapes += [(width,)] * len(picks) + [(long,)]
    return pl.pallas_call(
        functools.partial(widen_rest_kernel, attn_rows, feat, picks),
        out_shape=[jax.ShapeDtypeStruct(t, f32) for t in shapes],
        in_specs=[pl.BlockSpec(memory_space=pl.ANY)],
        out_specs=[pl.BlockSpec(memory_space=pl.ANY)] * 5
        + [pl.BlockSpec(memory_space=pltpu.VMEM)] * (len(picks) + 2),
        scratch_shapes=[
            pltpu.VMEM((devices, rows, width), bf16),
            pltpu.VMEM((4, width, width), f32),
            pltpu.VMEM((devices * (rows - attn_rows), width), f32),
            pltpu.SemaphoreType.DMA((4,)),
            pltpu.SemaphoreType.DMA((8,)),
        ],
        compiler_params=pltpu.CompilerParams(vmem_limit_bytes=LIMIT),
        cost_estimate=cost(0, parts.size * 6),
        name="widen_rest",
    )(parts)


def run_feed_forward(captions, counts, n1, mixed, cot, weights, cut, wo, bu, bd, g1, g2, beta2):
    seqs = captions.shape[0]
    total, d = n1.shape
    devices = weights.shape[0]
    down = weights.shape[1] // 2
    ff = devices * down
    blocks = ff // d

    def part(rows, index):
        return pl.BlockSpec(
            (devices, rows, d), lambda s, *_: (0, index, 0), pipeline_mode=pl.Buffered(1)
        )

    if cut % 8 == 0:
        ups = [part(cut, blocks + j) for j in range(blocks)]
        up_weights = [weights] * blocks
    else:
        ups = [whole((d, d))] * blocks
        up_weights = [
            weights[:, down + j * cut : down + (j + 1) * cut].reshape(d, d) for j in range(blocks)
        ]

    L = total // seqs
    row = tile((L, d))
    wide = tile((L, ff))
    vec = whole((d,))
    shapes = [
        jax.ShapeDtypeStruct((total, d), bf16),
        jax.ShapeDtypeStruct((total, ff), bf16),
        jax.ShapeDtypeStruct((total, d), bf16),
        jax.ShapeDtypeStruct((total, ff), bf16),
        jax.ShapeDtypeStruct((total, d), f32),
        jax.ShapeDtypeStruct((total, d), bf16),
        jax.ShapeDtypeStruct((total, d), bf16),
        jax.ShapeDtypeStruct((8, d), f32),
        jax.ShapeDtypeStruct((1, ff), f32),
    ]
    return pl.pallas_call(
        feed_forward,
        out_shape=shapes,
        grid_spec=pltpu.PrefetchScalarGridSpec(
            num_scalar_prefetch=2,
            grid=(seqs,),
            in_specs=[row, row, row, part(down, 0)]
            + ups
            + [whole((d, d)), whole((ff,)), vec, vec, vec, vec],
            out_specs=[row, wide, row, wide, row, row, row, still((8, d)), still((1, ff))],
            scratch_shapes=[pltpu.VMEM((L, ff), f32), pltpu.VMEM((blocks, d, d), bf16)],
        ),
        compiler_params=pltpu.CompilerParams(
            dimension_semantics=("arbitrary",), vmem_limit_bytes=LIMIT
        ),
        cost_estimate=cost(2 * total * d * (4 * ff + d), total * (ff * 4 + d * 18) + d * ff * 4, total * ff),
        name="feed_forward",
    )(captions, counts, n1, mixed, cot, weights, *up_weights, wo, bu, bd, g1, g2, beta2)


def run_attention_backward(geometry, counts, offset, q, k, v, p, gc, gm, wq, wk, wv):
    seqs, _, L, _ = p.shape
    total, d = q.shape
    row = tile((L, d))
    half = tile((L // 2, d))
    mat = whole((d, d))
    received = geometry[0] * geometry[2]
    shapes = [jax.ShapeDtypeStruct((total, d), bf16)] * 3 + [
        jax.ShapeDtypeStruct((total // 2, d), bf16),
        jax.ShapeDtypeStruct((received, d), bf16),
        jax.ShapeDtypeStruct((8, d), f32),
    ]
    return pl.pallas_call(
        functools.partial(attention_backward, *geometry),
        out_shape=shapes,
        grid_spec=pltpu.PrefetchScalarGridSpec(
            num_scalar_prefetch=2,
            grid=(seqs,),
            in_specs=[row, row, row, tile((1, HEADS, L, L)), row, row, mat, mat, mat],
            out_specs=[row, row, row, half, still((received, d)), still((8, d))],
            scratch_shapes=[pltpu.VMEM((received, d), f32)],
        ),
        compiler_params=pltpu.CompilerParams(
            dimension_semantics=("arbitrary",), vmem_limit_bytes=LIMIT
        ),
        cost_estimate=cost(2 * total * d * (3 * d + 4 * L * 4), total * d * 20 + seqs * HEADS * L * L * 2),
        name="attention_backward",
    )(counts, offset, q, k, v, p, gc, gm, wq, wk, wv)


def weight_grad_kernel(lhs_of, rhs_of, groups, core_ref, *refs):
    lhs_refs = refs[: max(lhs_of) + 1]
    rhs_refs = refs[len(lhs_refs) : len(lhs_refs) + max(rhs_of) + 1]
    outs = refs[len(lhs_refs) + len(rhs_refs) : -1]
    acc_ref = refs[-1]
    step = pl.program_id(0)
    core = core_ref[0]
    kinds = {}
    for i, kind in enumerate(zip(lhs_of, rhs_of)):
        kinds.setdefault(kind, []).append(i)
    for (a, b), steps in kinds.items():

        @pl.when((step >= steps[0]) & (step <= steps[-1]))
        def _(a=a, b=b):
            value = tn(lhs_refs[a][...], rhs_refs[b][...]).astype(bf16)
            acc_ref[...] = value.reshape(acc_ref.shape)

    for i in range(outs[0].shape[0]):
        for side in (0, 1):
            at = 0
            for ref in outs[side * groups : (side + 1) * groups]:
                rows = ref.shape[1]
                ref[i] = acc_ref[2 * i + (1 - core if side == 0 else core), at : at + rows, :]
                at += rows


def weight_grads(core, devices, lhs, rhs, lhs_of, rhs_of, lhs_maps, rhs_maps, width, groups, name):
    steps = len(lhs_of)
    total = lhs[0].shape[0]
    rows = steps * width // devices
    per = width // rows
    outs = [rows // groups] * (2 * groups)
    specs = [pl.BlockSpec((total, width), m) for m in lhs_maps + rhs_maps]
    out = pl.pallas_call(
        functools.partial(weight_grad_kernel, lhs_of, rhs_of, groups),
        out_shape=[jax.ShapeDtypeStruct((devices // 2, r, width), bf16) for r in outs],
        grid_spec=pltpu.PrefetchScalarGridSpec(
            num_scalar_prefetch=1,
            grid=(steps,),
            in_specs=specs,
            out_specs=[pl.BlockSpec((per // 2, r, width), lambda s, *_: (s, 0, 0)) for r in outs],
            scratch_shapes=[pltpu.VMEM((per, rows, width), bf16)],
        ),
        compiler_params=pltpu.CompilerParams(
            dimension_semantics=("arbitrary",), vmem_limit_bytes=LIMIT
        ),
        cost_estimate=cost(2 * total * width * width * steps, steps * width * (total + width) * 2),
        name=name,
    )(core, *lhs, *rhs)
    return list(zip(out[:groups], out[groups:]))


def axis_bits(name):
    size = lax.axis_size(name)
    bits = []
    step = 1
    while step < size:
        bits.append((name, step))
        step *= 2
    return bits


def bit_layout():
    return axis_bits("enc")[::-1] + axis_bits("dp")[::-1]


def my_bit(bit):
    return (lax.axis_index(bit[0]) // bit[1]) % 2


def swap_bit(tensor, bit):
    name, step = bit
    size = lax.axis_size(name)
    return lax.ppermute(tensor, name, [(i, i ^ step) for i in range(size)])


def stage_orders():
    dp_bits, enc_bits = axis_bits("dp"), axis_bits("enc")
    near, middle = dp_bits[:1], dp_bits[1:]
    half = len(middle) // 2
    return (
        near + middle + enc_bits,
        near + middle[half:] + middle[:half] + enc_bits,
    )


def add_low(kept, came):
    return (kept.astype(f32) + came.astype(f32)).astype(bf16)


class Scatter:
    def __init__(self, away, kept, order):
        self.order = list(order)
        self.layout = bit_layout()
        self.value = (away, kept)
        self.fresh = True

    def stage(self):
        bit = self.order.pop(0)
        axis = self.layout.index(bit)
        self.layout.remove(bit)
        if self.fresh:
            away, kept = self.value
            self.fresh = False
        else:
            mine = my_bit(bit)
            away, kept = [
                add_low(*[lax.dynamic_index_in_dim(t, i, axis, keepdims=False) for t in self.value])
                for i in (1 - mine, mine)
            ]
        shape = (2,) * len(self.layout) + kept.shape[-2:]
        self.value = (kept.reshape(shape), swap_bit(away, bit).reshape(shape))
        return away

    def total(self):
        return add_low(*self.value)


class Gather:
    def __init__(self, rows, order, layout=()):
        self.order = list(order)[::-1]
        self.layout = list(layout)
        self.value = rows

    def stage(self):
        bit = self.order.pop(0)
        sent = self.value
        came = swap_bit(sent, bit)
        self.layout = [b for b in bit_layout() if b in self.layout or b == bit]
        axis = self.layout.index(bit)
        shape = sent.shape[:axis] + (2,) + sent.shape[axis:]
        at = lax.broadcasted_iota(jnp.int32, shape, axis)
        self.value = jnp.where(
            at == my_bit(bit), jnp.expand_dims(sent, axis), jnp.expand_dims(came, axis)
        )
        return sent

    def rows(self):
        return self.value.reshape((-1,) + self.value.shape[-2:])

    def halves(self):
        (bit,) = self.order
        came = swap_bit(self.value, bit)
        shape = (-1,) + came.shape[-2:]
        return self.value.reshape(shape), came.reshape(shape)

    def split(self, at, orders):
        values = (self.value[..., :at, :], self.value[..., at:, :])
        return [
            Gather(value, [b for b in order if b not in self.layout], self.layout)
            for value, order in zip(values, orders)
        ]


def fence(movers, *values):
    leaves, tree = jax.tree.flatten(([m.value for m in movers], values))
    held, values = jax.tree.unflatten(tree, lax.optimization_barrier(leaves))
    for mover, value in zip(movers, held):
        mover.value = value
    return values


def in_turn(*movers):
    sent = []
    for mover in movers:
        fence([mover], sent)
        sent = mover.stage()


class Sum:
    def __init__(self, parts, orders):
        far = len(axis_bits("enc"))
        self.movers = [Scatter(*part, order) for part, order in zip(parts, orders)]
        self.steps = [self.run] * (len(orders[0]) - far) + [self.merge] + [self.run] * (far - 1)

    @property
    def value(self):
        return [m.value for m in self.movers]

    @value.setter
    def value(self, values):
        for mover, value in zip(self.movers, values):
            mover.value = value

    def stage(self):
        return self.steps.pop(0)() if self.steps else []

    def run(self):
        return [mover.stage() for mover in self.movers]

    def merge(self):
        first = self.movers[0]
        first.value = tuple(jnp.concatenate(t, -2) for t in zip(*[m.value for m in self.movers]))
        self.movers = [first]
        return self.run()

    def total(self):
        return self.movers[0].total()


def body(
    text,
    region_feats,
    boxes,
    caption_count,
    region_count,
    region_offset,
    w_img,
    w_box,
    b_img,
    g_reg,
    beta_reg,
    w_query,
    b_query,
    w_key,
    w_value,
    b_value,
    w_out,
    b_out,
    g_one,
    beta_one,
    w_up,
    b_up,
    w_down,
    b_down,
    g_two,
    beta_two,
    cotangent,
):
    axes = ("enc", "dp")
    orders = stage_orders()
    model_width = text.shape[1]
    ff_blocks = w_up.shape[1] // model_width
    cut = w_query.shape[0]
    far = axis_bits("enc")

    middle = len(orders[0]) - 1 - len(far)
    core = (lax.axis_index("dp") % 2).astype(jnp.int32).reshape(1)

    up_blocks = w_up.reshape(cut, ff_blocks, model_width).transpose(1, 0, 2)
    ff_shard = jnp.concatenate([w_down, up_blocks.reshape(ff_blocks * cut, model_width)], 0)
    rows_up = cut
    img = Gather(w_img, far)
    attn = Gather(jnp.concatenate([w_query, w_key, w_value, w_out], 0), far)
    img.stage()
    (ff_shard,) = fence([img, attn], ff_shard)
    while img.order:
        img.stage()
        attn.stage()
        (ff_shard,) = fence([img, attn], ff_shard)
    ff_weights = lax.all_gather(ff_shard, axes, axis=0)
    img = img.split(w_img.shape[0] // 2, orders)
    attn.stage()
    for _ in range(middle):
        for part in img:
            part.stage()
        fence([*img, attn])
    attn = attn.split(2 * cut, orders)
    img_halves = [t for part in img for t in part.halves()]
    for part in attn:
        part.stage()
    device_count = lax.axis_size(axes)
    seq_count = caption_count.shape[0]
    sent_rows, feat = region_feats.shape
    per_peer = sent_rows // device_count
    pad = 8 * (-(-per_peer // 8))
    pad = 1 << (pad - 1).bit_length()
    box_count = boxes.shape[0]
    geometry = (pad, per_peer, device_count)
    pre_norm, encoded, img_full = run_image_encode(
        geometry, core, region_feats, boxes, img_halves, w_box, b_img, g_reg, beta_reg
    )
    img_full = img_full.reshape(feat, model_width)
    (encoded,) = fence(attn, encoded)
    received = lax.all_to_all(encoded, axes, split_axis=0, concat_axis=0, tiled=True)
    for _ in range(middle - 1):
        for part in attn:
            part.stage()
        (received,) = fence(attn, received)
    for part in attn:
        part.stage()
    query_full, key_full, value_full, out_full = [
        t.reshape(-1, model_width)
        for part in attn
        for t in (part.rows()[:, :cut], part.rows()[:, cut:])
    ]
    (
        hidden_in,
        queries,
        keys,
        values,
        probs,
        context,
        mixed,
        normed_one,
    ) = run_attention_forward(
        geometry,
        caption_count,
        region_count,
        region_offset,
        received,
        text,
        query_full,
        key_full,
        value_full,
        out_full,
        b_query,
        b_value,
        b_out,
        g_one,
        beta_one,
    )
    (
        output,
        activated,
        grad_down_out,
        grad_gate,
        grad_mixed,
        grad_attn,
        grad_context,
        sums,
        grad_b_up,
    ) = run_feed_forward(
        caption_count,
        region_count,
        normed_one,
        mixed,
        cotangent,
        ff_weights,
        rows_up,
        out_full,
        b_up,
        b_down,
        g_one,
        g_two,
        beta_two,
    )
    fixed = lambda s, *_: (0, 0)
    moving = lambda s, *_: (0, s)
    (down,) = weight_grads(
        core,
        device_count,
        [activated],
        [grad_down_out],
        [0] * ff_blocks,
        [0] * ff_blocks,
        [moving],
        [fixed],
        model_width,
        1,
        "grad_w_down",
    )
    (up,) = weight_grads(
        core,
        device_count,
        [normed_one],
        [grad_gate],
        [0] * ff_blocks,
        [0] * ff_blocks,
        [fixed],
        [moving],
        model_width,
        1,
        "grad_w_up",
    )
    ff = Sum([down, up], orders)
    ff.stage()
    sent = ff.stage()
    grad_context, _ = fence([], grad_context, sent)
    grad_query, grad_keys, grad_values, grad_text, grad_slots, attn_sums = run_attention_backward(
        geometry,
        region_count,
        region_offset,
        queries,
        keys,
        values,
        probs,
        grad_context,
        grad_mixed,
        query_full,
        key_full,
        value_full,
    )
    grad_query, grad_keys, grad_values, grad_slots, attn_sums = fence(
        [ff], grad_query, grad_keys, grad_values, grad_slots, attn_sums
    )
    back = lax.all_to_all(grad_slots, axes, split_axis=0, concat_axis=0, tiled=True)
    ff.stage()
    attn_parts = weight_grads(
        core,
        device_count,
        [hidden_in, context],
        [grad_query, grad_keys, grad_values, grad_attn],
        [0, 0, 0, 1],
        [0, 1, 2, 3],
        [fixed] * 2,
        [fixed] * 4,
        model_width,
        2,
        "grad_w_attn",
    )
    attn = Sum(attn_parts, orders)
    (back,) = fence([ff, attn], back)
    while len(ff.steps) > len(far):
        ff.stage()
        fence([ff])
    in_turn(ff, attn)
    small_rows = 40
    chunk = 8 * (-(-(feat + small_rows) // (8 * device_count)))
    grad_pre, grad_feats, img_parts = run_image_backward(
        geometry,
        chunk,
        core,
        region_feats,
        boxes,
        img_full,
        pre_norm,
        back,
        g_reg,
        sums,
        attn_sums,
        grad_b_up.reshape(ff_blocks, model_width),
    )
    img = Sum(img_parts, orders)
    fence([ff, attn, img])
    while ff.steps:
        if len(ff.steps) > 1:
            in_turn(ff)
        else:
            in_turn(ff, attn, img)
        fence([ff, attn, img])
    ff = Gather(ff.total(), far)
    in_turn(ff, img, attn)
    fence([attn, img, ff])
    while img.steps:
        in_turn(attn, img)
        fence([attn, img, ff])
    rest = jnp.concatenate([attn.total(), img.total()], 0)
    rest_all = lax.all_gather(rest, axes, axis=0)
    fence([ff], rest)
    while ff.order:
        ff.stage()
        fence([ff])
    down, up = ff.split(w_down.shape[0], orders)
    while len(down.order) > 1:
        down.stage()
        up.stage()
        fence([down, up])
    down_halves, up_halves = down.halves(), up.halves()
    grad_w_down = join_blocks(
        core, down_halves, (ff_blocks * model_width, model_width), (1, 0)
    )
    grad_w_up = join_blocks(core, up_halves, (model_width, ff_blocks * model_width), (0, 1))
    grad_boxes = jnp.einsum("cd,rd->cr", w_box, grad_pre, preferred_element_type=f32).astype(bf16)
    (
        grad_w_query,
        grad_w_key,
        grad_w_value,
        grad_w_out,
        grad_w_img,
        grad_w_box,
        grad_b_img,
        grad_g_reg,
        grad_beta_reg,
        grad_g_two,
        grad_beta_two,
        grad_b_down,
        grad_g_one,
        grad_beta_one,
        grad_b_out,
        grad_b_query,
        grad_b_value,
        grad_b_up,
    ) = widen_rest(
        rest_all,
        4 * cut,
        feat,
        box_count,
        b_up.shape[0],
        (8, 9, 10, 16, 17, 18, 19, 20, 21, 24, 25),
    )
    return (
        output,
        grad_text,
        grad_feats,
        grad_boxes,
        grad_w_img,
        grad_w_box,
        grad_b_img,
        grad_g_reg,
        grad_beta_reg,
        grad_w_query,
        grad_b_query,
        grad_w_key,
        grad_w_value,
        grad_b_value,
        grad_w_out,
        grad_b_out,
        grad_g_one,
        grad_beta_one,
        grad_w_up,
        grad_b_up,
        grad_w_down,
        grad_b_down,
        grad_g_two,
        grad_beta_two,
    )


def solution(mesh):
    return jax.shard_map(
        body,
        mesh=mesh,
        in_specs=(
            P(("enc", "dp"), None),
            P(("enc", "dp"), None),
            P(None, ("enc", "dp")),
            P(("enc", "dp")),
            P(("enc", "dp")),
            P(("enc", "dp")),
            P(("enc", "dp"), None),
            P(),
            P(),
            P(),
            P(),
            P(("enc", "dp"), None),
            P(),
            P(("enc", "dp"), None),
            P(("enc", "dp"), None),
            P(),
            P(("enc", "dp"), None),
            P(),
            P(),
            P(),
            P(("enc", "dp"), None),
            P(),
            P(("enc", "dp"), None),
            P(),
            P(),
            P(),
            P(("enc", "dp"), None),
        ),
        out_specs=(
            P(("enc", "dp"), None),
            P(("enc", "dp"), None),
            P(("enc", "dp"), None),
            P(None, ("enc", "dp")),
            P(),
            P(),
            P(),
            P(),
            P(),
            P(),
            P(),
            P(),
            P(),
            P(),
            P(),
            P(),
            P(),
            P(),
            P(),
            P(),
            P(),
            P(),
            P(),
            P(),
        ),
        check_vma=False,
    )
```

```python
import functools
import math

import jax
import jax.numpy as jnp
from jax import lax
from jax.experimental import pallas as pl
from jax.experimental.pallas import tpu as pltpu
from jax.sharding import PartitionSpec as P

HEADS = 12
epsilon = 1e-05
f32, bf16 = jnp.float32, jnp.bfloat16

ERFC_P = 0.35
ERFC_C = (
    0.19567911,
    0.22612264,
    0.02080242,
    0.63768037,
    -0.6386366,
    0.75239514,
    -0.19404308,
)


def nn(a, b):
    return lax.dot_general(a, b, (((1,), (0,)), ((), ())), preferred_element_type=f32)


def nt(a, b):
    return lax.dot_general(a, b, (((1,), (1,)), ((), ())), preferred_element_type=f32)


def tn(a, b):
    return lax.dot_general(a, b, (((0,), (0,)), ((), ())), preferred_element_type=f32)


def norm_parts(values):
    centered = values - jnp.mean(values, -1, keepdims=True)
    inverse = lax.rsqrt(jnp.mean(centered * centered, -1, keepdims=True) + epsilon)
    return centered * inverse, inverse


def norm_back(upstream, normed, inverse, gain):
    weighted = upstream * gain
    return inverse * (
        weighted
        - jnp.mean(weighted, -1, keepdims=True)
        - normed * jnp.mean(weighted * normed, -1, keepdims=True)
    )


def gelu_parts(x):
    e = jnp.exp(-0.5 * x * x)
    t = 1.0 / (1.0 + (ERFC_P * math.sqrt(0.5)) * jnp.abs(x))
    acc = jnp.full_like(t, 0.5 * ERFC_C[-1])
    for c in ERFC_C[-2::-1]:
        acc = acc * t + 0.5 * c
    tail = acc * t * e
    phi = jnp.where(x >= 0, 1.0 - tail, tail)
    return x * phi, phi + x * (e * (1.0 / math.sqrt(2.0 * math.pi)))


def one_hot(wanted, live, rows, pad, sent, devices, offset):
    row = lax.broadcasted_iota(jnp.int32, (1, rows), 1)
    shift = pad.bit_length() - 1
    turn = lax.shift_right_logical(row, shift) - offset
    turn = jnp.where(turn < 0, turn + devices, turn)
    inside = jnp.bitwise_and(row, pad - 1)
    arrival = jnp.where(inside < sent, inside * devices + turn, -1)
    return ((wanted == arrival) & live).astype(bf16)


def spread(pad, sent, rows, padded):
    to = lax.broadcasted_iota(jnp.int32, (padded, 1), 0)
    shift = pad.bit_length() - 1
    inside = jnp.bitwise_and(to, pad - 1)
    source = jnp.where(inside < sent, lax.shift_right_logical(to, shift) * sent + inside, -1)
    return (source == lax.broadcasted_iota(jnp.int32, (1, rows), 1)).astype(bf16)


def image_encode(
    pad, sent, core_ref,
    x_ref, box_ref, wb_ref, bi_ref, gr_ref, betar_ref, *refs,
):
    *halves, pre_ref, enc_ref, wi_ref = refs
    core = core_ref[0]
    at = 0
    for own_ref, came_ref in zip(halves[::2], halves[1::2]):
        pairs, rows, _ = own_ref.shape
        for i in range(pairs):
            wi_ref[2 * i + core, at : at + rows, :] = own_ref[i]
            wi_ref[2 * i + 1 - core, at : at + rows, :] = came_ref[i]
        at += rows
    weight = wi_ref[...].reshape(x_ref.shape[1], wi_ref.shape[2])
    pre = nn(x_ref[...], weight) + tn(box_ref[...], wb_ref[...]) + bi_ref[...]
    pre_ref[...] = pre
    normed, _ = norm_parts(pre)
    encoded = (normed * gr_ref[...] + betar_ref[...]).astype(bf16)
    enc_ref[...] = nn(spread(pad, sent, x_ref.shape[0], enc_ref.shape[0]), encoded).astype(bf16)


def attention_forward(
    pad, sent, devices,
    captions, counts, offset,
    enc_ref, text_ref,
    wq_ref, wk_ref, wv_ref, wo_ref, bq_ref, bv_ref, bo_ref, g_ref, beta_ref,
    h_ref, q_ref, k_ref, v_ref, p_ref, c_ref, mixed_ref, n_ref,
):
    s = pl.program_id(0)
    text_len = text_ref.shape[0]
    rows, width = h_ref.shape
    hd = width // HEADS
    start = jnp.int32(0)
    for i in range(captions.shape[0]):
        start = start + jnp.where(s > i, counts[i], 0)
    slot = lax.broadcasted_iota(jnp.int32, (rows - text_len, 1), 0)
    taken = one_hot(
        slot + start, slot < counts[s], enc_ref.shape[0], pad, sent, devices, offset[0]
    )
    h_ref[:text_len, :] = text_ref[...]
    h_ref[text_len:, :] = nn(taken, enc_ref[...]).astype(bf16)
    h = h_ref[...]
    q = (nn(h, wq_ref[...]) + bq_ref[...]).astype(bf16)
    k = nn(h, wk_ref[...]).astype(bf16)
    v = (nn(h, wv_ref[...]) + bv_ref[...]).astype(bf16)
    q_ref[...] = q
    k_ref[...] = k
    v_ref[...] = v
    row = lax.broadcasted_iota(jnp.int32, (rows, 1), 0)
    live = (row < captions[s]) | ((row >= text_len) & (row < text_len + counts[s]))
    lane = lax.broadcasted_iota(jnp.int32, (1, 2 * hd), 1)
    masks = [(lane < hd).astype(bf16), (lane >= hd).astype(bf16)]
    scaled = q * jnp.asarray(hd**-0.5, bf16)
    for pair in range(HEADS // 2):
        cols = slice(pair * 2 * hd, (pair + 1) * 2 * hd)
        context = None
        for j in range(2):
            scores = nt(k[:, cols], scaled[:, cols] * masks[j])
            scores = jnp.where(live, scores, -1e30)
            top = jnp.max(scores, 0, keepdims=True)
            e = jnp.exp(scores - top)
            p = (e * (1.0 / jnp.sum(e, 0, keepdims=True))).astype(bf16)
            p_ref[0, 2 * pair + j] = p
            part = tn(p, v[:, cols] * masks[j])
            context = part if context is None else context + part
        c_ref[:, cols] = context.astype(bf16)
    mixed = h.astype(f32) + nn(c_ref[...], wo_ref[...]) + bo_ref[...]
    mixed_ref[...] = mixed
    normed, _ = norm_parts(mixed)
    n_ref[...] = (normed * g_ref[...] + beta_ref[...]).astype(bf16)


def image_backward(
    pad, sent, core_ref,
    x_ref, box_ref, wi_ref, pre_ref, back_ref, gr_ref, sums_ref, attn_sums_ref, bu_ref,
    gp_ref, gx_ref, *outs,
):
    *outs, acc_ref = outs
    rows, feat = x_ref.shape
    width = pre_ref.shape[1]
    grad = tn(spread(pad, sent, rows, back_ref.shape[0]), back_ref[...])
    normed, inverse = norm_parts(pre_ref[...])
    gp = norm_back(grad, normed, inverse, gr_ref[...]).astype(bf16)
    gp_ref[...] = gp
    acc_ref[:feat, :] = tn(x_ref[...], gp)
    acc_ref[feat:, :] = jnp.zeros((acc_ref.shape[0] - feat, width), f32)
    acc_ref[feat : feat + box_ref.shape[0], :] = nn(box_ref[...], gp)
    at = feat + 8
    acc_ref[at : at + 1, :] = jnp.sum(gp.astype(f32), 0, keepdims=True)
    acc_ref[at + 1 : at + 2, :] = jnp.sum(grad * normed, 0, keepdims=True)
    acc_ref[at + 2 : at + 3, :] = jnp.sum(grad, 0, keepdims=True)
    acc_ref[at + 8 : at + 16, :] = sums_ref[...]
    acc_ref[at + 16 : at + 24, :] = attn_sums_ref[...]
    acc_ref[at + 24 : at + 24 + bu_ref.shape[0], :] = bu_ref[...]
    core = core_ref[0]
    half = len(outs) // 2
    chunk = sum(ref.shape[1] for ref in outs[:half])
    for i in range(outs[0].shape[0]):
        for side in (0, 1):
            at = (2 * i + (1 - core if side == 0 else core)) * chunk
            for ref in outs[side * half : (side + 1) * half]:
                rows_here = ref.shape[1]
                ref[i] = acc_ref[pl.ds(pl.multiple_of(at, 8), rows_here), :].astype(bf16)
                at = at + rows_here
    gx_ref[...] = nt(gp, wi_ref[...]).astype(bf16)


def feed_forward(
    captions, counts, n_ref, mixed_ref, cot_ref, wd_ref, *refs,
):
    blocks = len(refs) - 17
    up_refs = refs[:blocks]
    wu_ref = refs[-1]

    @pl.when(pl.program_id(0) == 0)
    def _():
        for j in range(blocks):
            wu_ref[j] = up_refs[j][...].astype(f32).reshape(wu_ref.shape[1:]).astype(bf16)

    feed_forward_rows(captions, counts, n_ref, mixed_ref, cot_ref, wu_ref, wd_ref, *refs[blocks:-1])


def feed_forward_rows(
    captions, counts, n_ref, mixed_ref, cot_ref, wu_ref, wd_ref, wo_ref, bu_ref, bd_ref, g1_ref, g2_ref, beta2_ref,
    out_ref, act_ref, gdo_ref, gg_ref, gm_ref, ga_ref, gc_ref, sums_ref, bu_sum_ref, d_ref,
):
    s = pl.program_id(0)
    n1 = n_ref[...]
    rows, width = n1.shape
    ff = act_ref.shape[1]
    step = width
    per = wd_ref.shape[0] * step // ff

    def down_rows(j):
        return wd_ref[j // step * per : (j // step + 1) * per].reshape(step, width)

    @pl.when(s == 0)
    def _():
        sums_ref[...] = jnp.zeros_like(sums_ref)
        bu_sum_ref[...] = jnp.zeros_like(bu_sum_ref)

    second = n1.astype(f32) + bd_ref[...]
    for j in range(0, ff, step):
        cols = slice(j, j + step)
        gate = nn(n1, wu_ref[j // step]) + bu_ref[cols]
        act, d = gelu_parts(gate)
        act = act.astype(bf16)
        act_ref[:, cols] = act
        d_ref[:, cols] = d
        second = second + nn(act, down_rows(j))
    normed, inverse = norm_parts(second)
    text_len = rows // 2
    row = lax.broadcasted_iota(jnp.int32, (rows, 1), 0)
    live = (row < captions[s]) | ((row >= text_len) & (row < text_len + counts[s]))
    live = live.astype(f32)
    out_ref[...] = ((normed * g2_ref[...] + beta2_ref[...]) * live).astype(bf16)
    up = cot_ref[...].astype(f32) * live

    def add(i, value):
        sums_ref[i : i + 1, :] += jnp.sum(value, 0, keepdims=True)

    add(0, up * normed)
    add(1, up)
    gsi = norm_back(up, normed, inverse, g2_ref[...])
    gdo = gsi.astype(bf16)
    gdo_ref[...] = gdo
    add(2, gdo.astype(f32))
    first = gsi
    for j in range(0, ff, step):
        cols = slice(j, j + step)
        gg = (nt(gdo, down_rows(j)) * d_ref[:, cols]).astype(bf16)
        gg_ref[:, cols] = gg
        bu_sum_ref[:, cols] += jnp.sum(gg.astype(f32), 0, keepdims=True)
        first = first + nt(gg, wu_ref[j // step])
    normed, inverse = norm_parts(mixed_ref[...])
    add(3, first * normed)
    add(4, first)
    gm = norm_back(first, normed, inverse, g1_ref[...])
    gm_ref[...] = gm
    ga = gm.astype(bf16)
    ga_ref[...] = ga
    add(5, ga.astype(f32))
    gc_ref[...] = nt(ga, wo_ref[...]).astype(bf16)


def attention_backward(
    pad, sent, devices,
    counts, offset,
    q_ref, k_ref, v_ref, p_ref, gc_ref, gm_ref, wq_ref, wk_ref, wv_ref,
    gq_ref, gk_ref, gv_ref, gt_ref, gs_ref, sums_ref, acc_ref,
):
    s = pl.program_id(0)
    rows, width = q_ref.shape
    hd = width // HEADS
    scale = hd**-0.5

    @pl.when(s == 0)
    def _():
        sums_ref[...] = jnp.zeros_like(sums_ref)

    lane = lax.broadcasted_iota(jnp.int32, (1, 2 * hd), 1)
    masks = [(lane < hd).astype(bf16), (lane >= hd).astype(bf16)]
    for pair in range(HEADS // 2):
        cols = slice(pair * 2 * hd, (pair + 1) * 2 * hd)
        gq = gk = gv = None
        for j in range(2):
            p = p_ref[0, 2 * pair + j]
            gc = gc_ref[:, cols] * masks[j]
            gp = nt(v_ref[:, cols], gc)
            part = nn(p, gc)
            gv = part if gv is None else gv + part
            pf = p.astype(f32)
            weighted = pf * gp
            gs = (weighted - pf * jnp.sum(weighted, 0, keepdims=True)).astype(bf16)
            part = tn(gs, k_ref[:, cols] * masks[j])
            gq = part if gq is None else gq + part
            part = nn(gs, q_ref[:, cols] * masks[j])
            gk = part if gk is None else gk + part
        gq_ref[:, cols] = (gq * scale).astype(bf16)
        gk_ref[:, cols] = (gk * scale).astype(bf16)
        gv_ref[:, cols] = gv.astype(bf16)
    gq, gk, gv = gq_ref[...], gk_ref[...], gv_ref[...]
    sums_ref[0:1, :] += jnp.sum(gq.astype(f32), 0, keepdims=True)
    sums_ref[1:2, :] += jnp.sum(gv.astype(f32), 0, keepdims=True)
    hidden = gm_ref[...] + nt(gq, wq_ref[...]) + nt(gk, wk_ref[...]) + nt(gv, wv_ref[...])
    text_len = gt_ref.shape[0]
    gt_ref[...] = hidden[:text_len].astype(bf16)
    start = jnp.int32(0)
    for i in range(counts.shape[0]):
        start = start + jnp.where(s > i, counts[i], 0)
    slot = lax.broadcasted_iota(jnp.int32, (rows - text_len, 1), 0)
    taken = one_hot(
        slot + start, slot < counts[s], acc_ref.shape[0], pad, sent, devices, offset[0]
    )
    part = tn(taken, hidden[text_len:].astype(bf16))

    @pl.when(s == 0)
    def _():
        acc_ref[...] = part

    @pl.when(s > 0)
    def _():
        acc_ref[...] += part

    @pl.when(s == pl.num_programs(0) - 1)
    def _():
        gs_ref[...] = acc_ref[...].astype(bf16)


def whole(shape):
    return pl.BlockSpec(shape, lambda s, *_: (0,) * len(shape), pipeline_mode=pl.Buffered(1))


def tile(shape):
    return pl.BlockSpec(shape, lambda s, *_: (s,) + (0,) * (len(shape) - 1))


def still(shape):
    return pl.BlockSpec(shape, lambda s, *_: (0,) * len(shape))


LIMIT = 60 * 1024 * 1024


def cost(flops, moved, exps=0):
    return pl.CostEstimate(flops=int(flops), bytes_accessed=int(moved), transcendentals=int(exps))


def run_image_encode(geometry, core, x, boxes, halves, wb, bi, gr, betar):
    pad, sent, devices = geometry
    rows, feat = x.shape
    d = wb.shape[1]
    operands = (x, boxes, wb, bi, gr, betar, *halves)
    shapes = [
        jax.ShapeDtypeStruct((rows, d), f32),
        jax.ShapeDtypeStruct((pad * devices, d), bf16),
        jax.ShapeDtypeStruct((devices, feat // devices, d), bf16),
    ]
    return pl.pallas_call(
        functools.partial(image_encode, pad, sent),
        out_shape=shapes,
        grid_spec=pltpu.PrefetchScalarGridSpec(
            num_scalar_prefetch=1,
            grid=(1,),
            in_specs=[whole(t.shape) for t in operands],
            out_specs=[whole(t.shape) for t in shapes],
        ),
        compiler_params=pltpu.CompilerParams(vmem_limit_bytes=LIMIT),
        cost_estimate=cost(2 * rows * d * feat, x.size * 2 + feat * d * 4 + rows * d * 6),
        name="image_encode",
    )(core, *operands)


def run_attention_forward(
    geometry, captions, counts, offset, enc, text, wq, wk, wv, wo, bq, bv, bo, g1, beta1
):
    seqs = captions.shape[0]
    text_rows, d = text.shape
    total = 2 * text_rows
    L = total // seqs
    row = tile((L, d))
    vec = whole((d,))
    mat = whole((d, d))
    shapes = (
        [jax.ShapeDtypeStruct((total, d), bf16)] * 4
        + [
            jax.ShapeDtypeStruct((seqs, HEADS, L, L), bf16),
            jax.ShapeDtypeStruct((total, d), bf16),
            jax.ShapeDtypeStruct((total, d), f32),
            jax.ShapeDtypeStruct((total, d), bf16),
        ]
    )
    return pl.pallas_call(
        functools.partial(attention_forward, *geometry),
        out_shape=shapes,
        grid_spec=pltpu.PrefetchScalarGridSpec(
            num_scalar_prefetch=3,
            grid=(seqs,),
            in_specs=[whole(enc.shape), tile((L // 2, d))] + [mat] * 4 + [vec] * 5,
            out_specs=[row] * 4 + [tile((1, HEADS, L, L))] + [row] * 3,
        ),
        compiler_params=pltpu.CompilerParams(
            dimension_semantics=("arbitrary",), vmem_limit_bytes=LIMIT
        ),
        cost_estimate=cost(
            2 * total * d * (4 * d + 2 * L * 4),
            total * d * 18 + seqs * HEADS * L * L * 2,
            seqs * HEADS * L * L,
        ),
        name="attention_forward",
    )(
        captions, counts, offset, enc, text,
        wq, wk, wv, wo, bq, bv, bo, g1, beta1,
    )


def run_image_backward(geometry, chunk, core, x, boxes, wi, pre, back, gr, sums, attn_sums, bu):
    pad, sent, devices = geometry
    rows, feat = x.shape
    d = pre.shape[1]
    first = 8 * (-(-chunk // 16))
    parts = [
        jax.ShapeDtypeStruct((devices // 2, r, d), bf16) for r in (first, chunk - first) * 2
    ]
    operands = (x, boxes, wi, pre, back, gr, sums, attn_sums, bu)
    gp, gx, *out = pl.pallas_call(
        functools.partial(image_backward, pad, sent),
        out_shape=[
            jax.ShapeDtypeStruct((rows, d), bf16),
            jax.ShapeDtypeStruct((rows, feat), bf16),
            *parts,
        ],
        grid_spec=pltpu.PrefetchScalarGridSpec(
            num_scalar_prefetch=1,
            grid=(1,),
            in_specs=[whole(o.shape) for o in operands],
            out_specs=[whole((rows, d)), whole((rows, feat))] + [whole(p.shape) for p in parts],
            scratch_shapes=[pltpu.VMEM((devices * chunk, d), f32)],
        ),
        compiler_params=pltpu.CompilerParams(
            dimension_semantics=("arbitrary",), vmem_limit_bytes=LIMIT
        ),
        cost_estimate=cost(4 * rows * d * feat, x.size * 4 + wi.size * 2 + devices * chunk * d * 2),
        name="image_backward",
    )(core, *operands)
    return gp, gx, list(zip(out[:2], out[2:]))


def join_kernel(core_ref, *refs):
    core = core_ref[0]
    out_ref = refs[-1]
    groups = list(zip(refs[:-1:2], refs[1:-1:2]))
    at = 0
    for i in range(groups[0][0].shape[0]):
        for first in (0, 1):
            for own_ref, came_ref in groups:
                own, came = own_ref[i].astype(f32), came_ref[i].astype(f32)
                rows = own.shape[0]
                out_ref[at : at + rows, :] = jnp.where(core == first, own, came)
                at += rows


def join_blocks(core, halves, shape, step):
    pairs, rows, width = halves[0].shape
    per = width // (2 * rows)
    down, right = step
    block = pl.BlockSpec((per, rows, width), lambda s, *_: (s, 0, 0))
    return pl.pallas_call(
        join_kernel,
        out_shape=jax.ShapeDtypeStruct(shape, f32),
        grid_spec=pltpu.PrefetchScalarGridSpec(
            num_scalar_prefetch=1,
            grid=(pairs // per,),
            in_specs=[block, block],
            out_specs=pl.BlockSpec((width, width), lambda s, *_: (s * down, s * right)),
        ),
        cost_estimate=cost(0, pairs * rows * width * 12),
        name="join_blocks",
    )(core, *halves)


def widen_rest_kernel(
    attn_rows, feat, picks, parts_ref, *refs
):
    squares, refs = refs[:4], refs[4:]
    img_ref, box_ref, refs = refs[0], refs[1], refs[2:]
    vectors, long_ref, refs = refs[: len(picks)], refs[len(picks)], refs[len(picks) + 1 :]
    in_buf, square_buf, img_buf, in_sem, out_sem = refs
    devices, rows, width = in_buf.shape
    img_rows = rows - attn_rows
    per = devices // 4
    loads = [
        pltpu.make_async_copy(
            parts_ref.at[j * per : (j + 1) * per], in_buf.at[j * per : (j + 1) * per], in_sem.at[j]
        )
        for j in range(4)
    ]
    for copy in loads:
        copy.start()
    stores = []

    def store(source, target):
        copy = pltpu.make_async_copy(source, target, out_sem.at[len(stores)])
        copy.start()
        stores.append(copy)

    for j in range(4):
        loads[j].wait()
        for i in range(per):
            value = in_buf[j * per + i, :attn_rows, :].astype(f32)
            square_buf[j, i * attn_rows : (i + 1) * attn_rows, :] = value
        store(square_buf.at[j], squares[j])
        for i in range(j * per, (j + 1) * per):
            value = in_buf[i, attn_rows:, :].astype(f32)
            img_buf[i * img_rows : (i + 1) * img_rows, :] = value
        first, last = [min(t * per * img_rows, feat) for t in (j, j + 1)]
        if last > first:
            store(img_buf.at[first:last], img_ref.at[first:last])
    box_ref[...] = img_buf[feat : feat + box_ref.shape[0], :]
    for pick, ref in zip(picks, vectors):
        ref[...] = img_buf[feat + pick, :]
    for i in range(long_ref.shape[0] // width):
        long_ref[i * width : (i + 1) * width] = img_buf[feat + 32 + i, :]
    for copy in stores:
        copy.wait()


def widen_rest(parts, attn_rows, feat, boxes, long, picks):
    devices, rows, width = parts.shape
    shapes = [(width, width)] * 4 + [(feat, width), (boxes, width)]
    shapes += [(width,)] * len(picks) + [(long,)]
    return pl.pallas_call(
        functools.partial(widen_rest_kernel, attn_rows, feat, picks),
        out_shape=[jax.ShapeDtypeStruct(t, f32) for t in shapes],
        in_specs=[pl.BlockSpec(memory_space=pl.ANY)],
        out_specs=[pl.BlockSpec(memory_space=pl.ANY)] * 5
        + [pl.BlockSpec(memory_space=pltpu.VMEM)] * (len(picks) + 2),
        scratch_shapes=[
            pltpu.VMEM((devices, rows, width), bf16),
            pltpu.VMEM((4, width, width), f32),
            pltpu.VMEM((devices * (rows - attn_rows), width), f32),
            pltpu.SemaphoreType.DMA((4,)),
            pltpu.SemaphoreType.DMA((8,)),
        ],
        compiler_params=pltpu.CompilerParams(vmem_limit_bytes=LIMIT),
        cost_estimate=cost(0, parts.size * 6),
        name="widen_rest",
    )(parts)


def run_feed_forward(captions, counts, n1, mixed, cot, weights, cut, wo, bu, bd, g1, g2, beta2):
    seqs = captions.shape[0]
    total, d = n1.shape
    devices = weights.shape[0]
    down = weights.shape[1] // 2
    ff = devices * down
    blocks = ff // d

    def part(rows, index):
        return pl.BlockSpec(
            (devices, rows, d), lambda s, *_: (0, index, 0), pipeline_mode=pl.Buffered(1)
        )

    if cut % 8 == 0:
        ups = [part(cut, blocks + j) for j in range(blocks)]
        up_weights = [weights] * blocks
    else:
        ups = [whole((d, d))] * blocks
        up_weights = [
            weights[:, down + j * cut : down + (j + 1) * cut].reshape(d, d) for j in range(blocks)
        ]

    L = total // seqs
    row = tile((L, d))
    wide = tile((L, ff))
    vec = whole((d,))
    shapes = [
        jax.ShapeDtypeStruct((total, d), bf16),
        jax.ShapeDtypeStruct((total, ff), bf16),
        jax.ShapeDtypeStruct((total, d), bf16),
        jax.ShapeDtypeStruct((total, ff), bf16),
        jax.ShapeDtypeStruct((total, d), f32),
        jax.ShapeDtypeStruct((total, d), bf16),
        jax.ShapeDtypeStruct((total, d), bf16),
        jax.ShapeDtypeStruct((8, d), f32),
        jax.ShapeDtypeStruct((1, ff), f32),
    ]
    return pl.pallas_call(
        feed_forward,
        out_shape=shapes,
        grid_spec=pltpu.PrefetchScalarGridSpec(
            num_scalar_prefetch=2,
            grid=(seqs,),
            in_specs=[row, row, row, part(down, 0)]
            + ups
            + [whole((d, d)), whole((ff,)), vec, vec, vec, vec],
            out_specs=[row, wide, row, wide, row, row, row, still((8, d)), still((1, ff))],
            scratch_shapes=[pltpu.VMEM((L, ff), f32), pltpu.VMEM((blocks, d, d), bf16)],
        ),
        compiler_params=pltpu.CompilerParams(
            dimension_semantics=("arbitrary",), vmem_limit_bytes=LIMIT
        ),
        cost_estimate=cost(2 * total * d * (4 * ff + d), total * (ff * 4 + d * 18) + d * ff * 4, total * ff),
        name="feed_forward",
    )(captions, counts, n1, mixed, cot, weights, *up_weights, wo, bu, bd, g1, g2, beta2)


def run_attention_backward(geometry, counts, offset, q, k, v, p, gc, gm, wq, wk, wv):
    seqs, _, L, _ = p.shape
    total, d = q.shape
    row = tile((L, d))
    half = tile((L // 2, d))
    mat = whole((d, d))
    received = geometry[0] * geometry[2]
    shapes = [jax.ShapeDtypeStruct((total, d), bf16)] * 3 + [
        jax.ShapeDtypeStruct((total // 2, d), bf16),
        jax.ShapeDtypeStruct((received, d), bf16),
        jax.ShapeDtypeStruct((8, d), f32),
    ]
    return pl.pallas_call(
        functools.partial(attention_backward, *geometry),
        out_shape=shapes,
        grid_spec=pltpu.PrefetchScalarGridSpec(
            num_scalar_prefetch=2,
            grid=(seqs,),
            in_specs=[row, row, row, tile((1, HEADS, L, L)), row, row, mat, mat, mat],
            out_specs=[row, row, row, half, still((received, d)), still((8, d))],
            scratch_shapes=[pltpu.VMEM((received, d), f32)],
        ),
        compiler_params=pltpu.CompilerParams(
            dimension_semantics=("arbitrary",), vmem_limit_bytes=LIMIT
        ),
        cost_estimate=cost(2 * total * d * (3 * d + 4 * L * 4), total * d * 20 + seqs * HEADS * L * L * 2),
        name="attention_backward",
    )(counts, offset, q, k, v, p, gc, gm, wq, wk, wv)


def weight_grad_kernel(lhs_of, rhs_of, groups, core_ref, *refs):
    lhs_refs = refs[: max(lhs_of) + 1]
    rhs_refs = refs[len(lhs_refs) : len(lhs_refs) + max(rhs_of) + 1]
    outs = refs[len(lhs_refs) + len(rhs_refs) : -1]
    acc_ref = refs[-1]
    step = pl.program_id(0)
    core = core_ref[0]
    kinds = {}
    for i, kind in enumerate(zip(lhs_of, rhs_of)):
        kinds.setdefault(kind, []).append(i)
    for (a, b), steps in kinds.items():

        @pl.when((step >= steps[0]) & (step <= steps[-1]))
        def _(a=a, b=b):
            value = tn(lhs_refs[a][...], rhs_refs[b][...]).astype(bf16)
            acc_ref[...] = value.reshape(acc_ref.shape)

    for i in range(outs[0].shape[0]):
        for side in (0, 1):
            at = 0
            for ref in outs[side * groups : (side + 1) * groups]:
                rows = ref.shape[1]
                ref[i] = acc_ref[2 * i + (1 - core if side == 0 else core), at : at + rows, :]
                at += rows


def weight_grads(core, devices, lhs, rhs, lhs_of, rhs_of, lhs_maps, rhs_maps, width, groups, name):
    steps = len(lhs_of)
    total = lhs[0].shape[0]
    rows = steps * width // devices
    per = width // rows
    outs = [rows // groups] * (2 * groups)
    specs = [pl.BlockSpec((total, width), m) for m in lhs_maps + rhs_maps]
    out = pl.pallas_call(
        functools.partial(weight_grad_kernel, lhs_of, rhs_of, groups),
        out_shape=[jax.ShapeDtypeStruct((devices // 2, r, width), bf16) for r in outs],
        grid_spec=pltpu.PrefetchScalarGridSpec(
            num_scalar_prefetch=1,
            grid=(steps,),
            in_specs=specs,
            out_specs=[pl.BlockSpec((per // 2, r, width), lambda s, *_: (s, 0, 0)) for r in outs],
            scratch_shapes=[pltpu.VMEM((per, rows, width), bf16)],
        ),
        compiler_params=pltpu.CompilerParams(
            dimension_semantics=("arbitrary",), vmem_limit_bytes=LIMIT
        ),
        cost_estimate=cost(2 * total * width * width * steps, steps * width * (total + width) * 2),
        name=name,
    )(core, *lhs, *rhs)
    return list(zip(out[:groups], out[groups:]))


def axis_bits(name):
    size = lax.axis_size(name)
    bits = []
    step = 1
    while step < size:
        bits.append((name, step))
        step *= 2
    return bits


def bit_layout():
    return axis_bits("enc")[::-1] + axis_bits("dp")[::-1]


def my_bit(bit):
    return (lax.axis_index(bit[0]) // bit[1]) % 2


def swap_bit(tensor, bit):
    name, step = bit
    size = lax.axis_size(name)
    return lax.ppermute(tensor, name, [(i, i ^ step) for i in range(size)])


def stage_orders():
    dp_bits, enc_bits = axis_bits("dp"), axis_bits("enc")
    near, middle = dp_bits[:1], dp_bits[1:]
    half = len(middle) // 2
    return (
        near + middle + enc_bits,
        near + middle[half:] + middle[:half] + enc_bits,
    )


def add_low(kept, came):
    return (kept.astype(f32) + came.astype(f32)).astype(bf16)


class Scatter:
    def __init__(self, away, kept, order):
        self.order = list(order)
        self.layout = bit_layout()
        self.value = (away, kept)
        self.fresh = True

    def stage(self):
        bit = self.order.pop(0)
        axis = self.layout.index(bit)
        self.layout.remove(bit)
        if self.fresh:
            away, kept = self.value
            self.fresh = False
        else:
            mine = my_bit(bit)
            away, kept = [
                add_low(*[lax.dynamic_index_in_dim(t, i, axis, keepdims=False) for t in self.value])
                for i in (1 - mine, mine)
            ]
        shape = (2,) * len(self.layout) + kept.shape[-2:]
        self.value = (kept.reshape(shape), swap_bit(away, bit).reshape(shape))
        return away

    def total(self):
        return add_low(*self.value)


class Gather:
    def __init__(self, rows, order, layout=()):
        self.order = list(order)[::-1]
        self.layout = list(layout)
        self.value = rows

    def stage(self):
        bit = self.order.pop(0)
        sent = self.value
        came = swap_bit(sent, bit)
        self.layout = [b for b in bit_layout() if b in self.layout or b == bit]
        axis = self.layout.index(bit)
        shape = sent.shape[:axis] + (2,) + sent.shape[axis:]
        at = lax.broadcasted_iota(jnp.int32, shape, axis)
        self.value = jnp.where(
            at == my_bit(bit), jnp.expand_dims(sent, axis), jnp.expand_dims(came, axis)
        )
        return sent

    def rows(self):
        return self.value.reshape((-1,) + self.value.shape[-2:])

    def halves(self):
        (bit,) = self.order
        came = swap_bit(self.value, bit)
        shape = (-1,) + came.shape[-2:]
        return self.value.reshape(shape), came.reshape(shape)

    def split(self, at, orders):
        values = (self.value[..., :at, :], self.value[..., at:, :])
        return [
            Gather(value, [b for b in order if b not in self.layout], self.layout)
            for value, order in zip(values, orders)
        ]


def fence(movers, *values):
    leaves, tree = jax.tree.flatten(([m.value for m in movers], values))
    held, values = jax.tree.unflatten(tree, lax.optimization_barrier(leaves))
    for mover, value in zip(movers, held):
        mover.value = value
    return values


def in_turn(*movers):
    sent = []
    for mover in movers:
        fence([mover], sent)
        sent = mover.stage()


class Sum:
    def __init__(self, parts, orders):
        far = len(axis_bits("enc"))
        self.movers = [Scatter(*part, order) for part, order in zip(parts, orders)]
        self.steps = [self.run] * (len(orders[0]) - far) + [self.merge] + [self.run] * (far - 1)

    @property
    def value(self):
        return [m.value for m in self.movers]

    @value.setter
    def value(self, values):
        for mover, value in zip(self.movers, values):
            mover.value = value

    def stage(self):
        return self.steps.pop(0)() if self.steps else []

    def run(self):
        return [mover.stage() for mover in self.movers]

    def merge(self):
        first = self.movers[0]
        first.value = tuple(jnp.concatenate(t, -2) for t in zip(*[m.value for m in self.movers]))
        self.movers = [first]
        return self.run()

    def total(self):
        return self.movers[0].total()


def body(
    text,
    region_feats,
    boxes,
    caption_count,
    region_count,
    region_offset,
    w_img,
    w_box,
    b_img,
    g_reg,
    beta_reg,
    w_query,
    b_query,
    w_key,
    w_value,
    b_value,
    w_out,
    b_out,
    g_one,
    beta_one,
    w_up,
    b_up,
    w_down,
    b_down,
    g_two,
    beta_two,
    cotangent,
):
    axes = ("enc", "dp")
    orders = stage_orders()
    model_width = text.shape[1]
    ff_blocks = w_up.shape[1] // model_width
    cut = w_query.shape[0]
    far = axis_bits("enc")

    middle = len(orders[0]) - 1 - len(far)
    core = (lax.axis_index("dp") % 2).astype(jnp.int32).reshape(1)

    up_blocks = w_up.reshape(cut, ff_blocks, model_width).transpose(1, 0, 2)
    ff_shard = jnp.concatenate([w_down, up_blocks.reshape(ff_blocks * cut, model_width)], 0)
    rows_up = cut
    img = Gather(w_img, far)
    attn = Gather(jnp.concatenate([w_query, w_key, w_value, w_out], 0), far)
    img.stage()
    (ff_shard,) = fence([img, attn], ff_shard)
    while img.order:
        img.stage()
        attn.stage()
        (ff_shard,) = fence([img, attn], ff_shard)
    ff_weights = lax.all_gather(ff_shard, axes, axis=0)
    img = img.split(w_img.shape[0] // 2, orders)
    attn.stage()
    for _ in range(middle):
        for part in img:
            part.stage()
        fence([*img, attn])
    attn = attn.split(2 * cut, orders)
    img_halves = fence(attn, *[t for part in img for t in part.halves()])
    for part in attn:
        part.stage()
    device_count = lax.axis_size(axes)
    seq_count = caption_count.shape[0]
    sent_rows, feat = region_feats.shape
    per_peer = sent_rows // device_count
    pad = 8 * (-(-per_peer // 8))
    pad = 1 << (pad - 1).bit_length()
    box_count = boxes.shape[0]
    geometry = (pad, per_peer, device_count)
    pre_norm, encoded, img_full = run_image_encode(
        geometry, core, region_feats, boxes, img_halves, w_box, b_img, g_reg, beta_reg
    )
    img_full = img_full.reshape(feat, model_width)
    (encoded,) = fence(attn, encoded)
    received = lax.all_to_all(encoded, axes, split_axis=0, concat_axis=0, tiled=True)
    for _ in range(middle - 1):
        for part in attn:
            part.stage()
        (received,) = fence(attn, received)
    for part in attn:
        part.stage()
    query_full, key_full, value_full, out_full = [
        t.reshape(-1, model_width)
        for part in attn
        for t in (part.rows()[:, :cut], part.rows()[:, cut:])
    ]
    (
        hidden_in,
        queries,
        keys,
        values,
        probs,
        context,
        mixed,
        normed_one,
    ) = run_attention_forward(
        geometry,
        caption_count,
        region_count,
        region_offset,
        received,
        text,
        query_full,
        key_full,
        value_full,
        out_full,
        b_query,
        b_value,
        b_out,
        g_one,
        beta_one,
    )
    (
        output,
        activated,
        grad_down_out,
        grad_gate,
        grad_mixed,
        grad_attn,
        grad_context,
        sums,
        grad_b_up,
    ) = run_feed_forward(
        caption_count,
        region_count,
        normed_one,
        mixed,
        cotangent,
        ff_weights,
        rows_up,
        out_full,
        b_up,
        b_down,
        g_one,
        g_two,
        beta_two,
    )
    fixed = lambda s, *_: (0, 0)
    moving = lambda s, *_: (0, s)
    (down,) = weight_grads(
        core,
        device_count,
        [activated],
        [grad_down_out],
        [0] * ff_blocks,
        [0] * ff_blocks,
        [moving],
        [fixed],
        model_width,
        1,
        "grad_w_down",
    )
    (up,) = weight_grads(
        core,
        device_count,
        [normed_one],
        [grad_gate],
        [0] * ff_blocks,
        [0] * ff_blocks,
        [fixed],
        [moving],
        model_width,
        1,
        "grad_w_up",
    )
    ff = Sum([down, up], orders)
    ff.stage()
    sent = ff.stage()
    grad_context, _ = fence([], grad_context, sent)
    grad_query, grad_keys, grad_values, grad_text, grad_slots, attn_sums = run_attention_backward(
        geometry,
        region_count,
        region_offset,
        queries,
        keys,
        values,
        probs,
        grad_context,
        grad_mixed,
        query_full,
        key_full,
        value_full,
    )
    grad_query, grad_keys, grad_values, grad_slots, attn_sums = fence(
        [ff], grad_query, grad_keys, grad_values, grad_slots, attn_sums
    )
    back = lax.all_to_all(grad_slots, axes, split_axis=0, concat_axis=0, tiled=True)
    ff.stage()
    attn_parts = weight_grads(
        core,
        device_count,
        [hidden_in, context],
        [grad_query, grad_keys, grad_values, grad_attn],
        [0, 0, 0, 1],
        [0, 1, 2, 3],
        [fixed] * 2,
        [fixed] * 4,
        model_width,
        2,
        "grad_w_attn",
    )
    attn = Sum(attn_parts, orders)
    (back,) = fence([ff, attn], back)
    while len(ff.steps) > len(far):
        ff.stage()
        fence([ff])
    in_turn(ff, attn)
    small_rows = 40
    chunk = 8 * (-(-(feat + small_rows) // (8 * device_count)))
    grad_pre, grad_feats, img_parts = run_image_backward(
        geometry,
        chunk,
        core,
        region_feats,
        boxes,
        img_full,
        pre_norm,
        back,
        g_reg,
        sums,
        attn_sums,
        grad_b_up.reshape(ff_blocks, model_width),
    )
    img = Sum(img_parts, orders)
    fence([ff, attn, img])
    while ff.steps:
        if len(ff.steps) > 1:
            in_turn(ff)
        else:
            in_turn(ff, attn, img)
        fence([ff, attn, img])
    ff = Gather(ff.total(), far)
    in_turn(ff, img, attn)
    fence([attn, img, ff])
    while img.steps:
        in_turn(attn, img)
        fence([attn, img, ff])
    rest = jnp.concatenate([attn.total(), img.total()], 0)
    rest_all = lax.all_gather(rest, axes, axis=0)
    fence([ff], rest)
    while ff.order:
        ff.stage()
        fence([ff])
    down, up = ff.split(w_down.shape[0], orders)
    while len(down.order) > 1:
        down.stage()
        up.stage()
        fence([down, up])
    down_halves, up_halves = down.halves(), up.halves()
    grad_w_down = join_blocks(
        core, down_halves, (ff_blocks * model_width, model_width), (1, 0)
    )
    grad_w_up = join_blocks(core, up_halves, (model_width, ff_blocks * model_width), (0, 1))
    grad_boxes = jnp.einsum("cd,rd->cr", w_box, grad_pre, preferred_element_type=f32).astype(bf16)
    (
        grad_w_query,
        grad_w_key,
        grad_w_value,
        grad_w_out,
        grad_w_img,
        grad_w_box,
        grad_b_img,
        grad_g_reg,
        grad_beta_reg,
        grad_g_two,
        grad_beta_two,
        grad_b_down,
        grad_g_one,
        grad_beta_one,
        grad_b_out,
        grad_b_query,
        grad_b_value,
        grad_b_up,
    ) = widen_rest(
        rest_all,
        4 * cut,
        feat,
        box_count,
        b_up.shape[0],
        (8, 9, 10, 16, 17, 18, 19, 20, 21, 24, 25),
    )
    return (
        output,
        grad_text,
        grad_feats,
        grad_boxes,
        grad_w_img,
        grad_w_box,
        grad_b_img,
        grad_g_reg,
        grad_beta_reg,
        grad_w_query,
        grad_b_query,
        grad_w_key,
        grad_w_value,
        grad_b_value,
        grad_w_out,
        grad_b_out,
        grad_g_one,
        grad_beta_one,
        grad_w_up,
        grad_b_up,
        grad_w_down,
        grad_b_down,
        grad_g_two,
        grad_beta_two,
    )


def solution(mesh):
    return jax.shard_map(
        body,
        mesh=mesh,
        in_specs=(
            P(("enc", "dp"), None),
            P(("enc", "dp"), None),
            P(None, ("enc", "dp")),
            P(("enc", "dp")),
            P(("enc", "dp")),
            P(("enc", "dp")),
            P(("enc", "dp"), None),
            P(),
            P(),
            P(),
            P(),
            P(("enc", "dp"), None),
            P(),
            P(("enc", "dp"), None),
            P(("enc", "dp"), None),
            P(),
            P(("enc", "dp"), None),
            P(),
            P(),
            P(),
            P(("enc", "dp"), None),
            P(),
            P(("enc", "dp"), None),
            P(),
            P(),
            P(),
            P(("enc", "dp"), None),
        ),
        out_specs=(
            P(("enc", "dp"), None),
            P(("enc", "dp"), None),
            P(("enc", "dp"), None),
            P(None, ("enc", "dp")),
            P(),
            P(),
            P(),
            P(),
            P(),
            P(),
            P(),
            P(),
            P(),
            P(),
            P(),
            P(),
            P(),
            P(),
            P(),
            P(),
            P(),
            P(),
            P(),
            P(),
        ),
        check_vma=False,
    )
```

```python
import functools
import math

import jax
import jax.numpy as jnp
from jax import lax
from jax.experimental import pallas as pl
from jax.experimental.pallas import tpu as pltpu
from jax.sharding import PartitionSpec as P

HEADS = 12
epsilon = 1e-05
f32, bf16 = jnp.float32, jnp.bfloat16

ERFC_P = 0.35
ERFC_C = (
    0.19567911,
    0.22612264,
    0.02080242,
    0.63768037,
    -0.6386366,
    0.75239514,
    -0.19404308,
)


def nn(a, b):
    return lax.dot_general(a, b, (((1,), (0,)), ((), ())), preferred_element_type=f32)


def nt(a, b):
    return lax.dot_general(a, b, (((1,), (1,)), ((), ())), preferred_element_type=f32)


def tn(a, b):
    return lax.dot_general(a, b, (((0,), (0,)), ((), ())), preferred_element_type=f32)


def norm_parts(values):
    centered = values - jnp.mean(values, -1, keepdims=True)
    inverse = lax.rsqrt(jnp.mean(centered * centered, -1, keepdims=True) + epsilon)
    return centered * inverse, inverse


def norm_back(upstream, normed, inverse, gain):
    weighted = upstream * gain
    return inverse * (
        weighted
        - jnp.mean(weighted, -1, keepdims=True)
        - normed * jnp.mean(weighted * normed, -1, keepdims=True)
    )


def gelu_parts(x):
    e = jnp.exp(-0.5 * x * x)
    t = 1.0 / (1.0 + (ERFC_P * math.sqrt(0.5)) * jnp.abs(x))
    acc = jnp.full_like(t, 0.5 * ERFC_C[-1])
    for c in ERFC_C[-2::-1]:
        acc = acc * t + 0.5 * c
    tail = acc * t * e
    phi = jnp.where(x >= 0, 1.0 - tail, tail)
    return x * phi, phi + x * (e * (1.0 / math.sqrt(2.0 * math.pi)))


def one_hot(wanted, live, rows, pad, sent, devices, offset):
    row = lax.broadcasted_iota(jnp.int32, (1, rows), 1)
    shift = pad.bit_length() - 1
    turn = lax.shift_right_logical(row, shift) - offset
    turn = jnp.where(turn < 0, turn + devices, turn)
    inside = jnp.bitwise_and(row, pad - 1)
    arrival = jnp.where(inside < sent, inside * devices + turn, -1)
    return ((wanted == arrival) & live).astype(bf16)


def spread(pad, sent, rows, padded):
    to = lax.broadcasted_iota(jnp.int32, (padded, 1), 0)
    shift = pad.bit_length() - 1
    inside = jnp.bitwise_and(to, pad - 1)
    source = jnp.where(inside < sent, lax.shift_right_logical(to, shift) * sent + inside, -1)
    return (source == lax.broadcasted_iota(jnp.int32, (1, rows), 1)).astype(bf16)


def image_encode(
    pad, sent, core_ref,
    x_ref, box_ref, wb_ref, bi_ref, gr_ref, betar_ref, *refs,
):
    *halves, pre_ref, enc_ref, wi_ref = refs
    core = core_ref[0]
    at = 0
    for own_ref, came_ref in zip(halves[::2], halves[1::2]):
        pairs, rows, _ = own_ref.shape
        for i in range(pairs):
            wi_ref[2 * i + core, at : at + rows, :] = own_ref[i]
            wi_ref[2 * i + 1 - core, at : at + rows, :] = came_ref[i]
        at += rows
    weight = wi_ref[...].reshape(x_ref.shape[1], wi_ref.shape[2])
    pre = nn(x_ref[...], weight) + tn(box_ref[...], wb_ref[...]) + bi_ref[...]
    pre_ref[...] = pre
    normed, _ = norm_parts(pre)
    encoded = (normed * gr_ref[...] + betar_ref[...]).astype(bf16)
    enc_ref[...] = nn(spread(pad, sent, x_ref.shape[0], enc_ref.shape[0]), encoded).astype(bf16)


def attention_forward(
    pad, sent, devices,
    captions, counts, offset,
    enc_ref, text_ref,
    wq_ref, wk_ref, wv_ref, wo_ref, bq_ref, bv_ref, bo_ref, g_ref, beta_ref,
    h_ref, q_ref, k_ref, v_ref, p_ref, c_ref, mixed_ref, n_ref,
):
    s = pl.program_id(0)
    text_len = text_ref.shape[0]
    rows, width = h_ref.shape
    hd = width // HEADS
    start = jnp.int32(0)
    for i in range(captions.shape[0]):
        start = start + jnp.where(s > i, counts[i], 0)
    slot = lax.broadcasted_iota(jnp.int32, (rows - text_len, 1), 0)
    taken = one_hot(
        slot + start, slot < counts[s], enc_ref.shape[0], pad, sent, devices, offset[0]
    )
    h_ref[:text_len, :] = text_ref[...]
    h_ref[text_len:, :] = nn(taken, enc_ref[...]).astype(bf16)
    h = h_ref[...]
    q = (nn(h, wq_ref[...]) + bq_ref[...]).astype(bf16)
    k = nn(h, wk_ref[...]).astype(bf16)
    v = (nn(h, wv_ref[...]) + bv_ref[...]).astype(bf16)
    q_ref[...] = q
    k_ref[...] = k
    v_ref[...] = v
    row = lax.broadcasted_iota(jnp.int32, (rows, 1), 0)
    live = (row < captions[s]) | ((row >= text_len) & (row < text_len + counts[s]))
    lane = lax.broadcasted_iota(jnp.int32, (1, 2 * hd), 1)
    masks = [(lane < hd).astype(bf16), (lane >= hd).astype(bf16)]
    scaled = q * jnp.asarray(hd**-0.5, bf16)
    for pair in range(HEADS // 2):
        cols = slice(pair * 2 * hd, (pair + 1) * 2 * hd)
        context = None
        for j in range(2):
            scores = nt(k[:, cols], scaled[:, cols] * masks[j])
            scores = jnp.where(live, scores, -1e30)
            top = jnp.max(scores, 0, keepdims=True)
            e = jnp.exp(scores - top)
            p = (e * (1.0 / jnp.sum(e, 0, keepdims=True))).astype(bf16)
            p_ref[0, 2 * pair + j] = p
            part = tn(p, v[:, cols] * masks[j])
            context = part if context is None else context + part
        c_ref[:, cols] = context.astype(bf16)
    mixed = h.astype(f32) + nn(c_ref[...], wo_ref[...]) + bo_ref[...]
    mixed_ref[...] = mixed
    normed, _ = norm_parts(mixed)
    n_ref[...] = (normed * g_ref[...] + beta_ref[...]).astype(bf16)


def image_backward(
    pad, sent, core_ref,
    x_ref, box_ref, pre_ref, back_ref, gr_ref, sums_ref, attn_sums_ref, bu_ref,
    gp_ref, *outs,
):
    *outs, acc_ref = outs
    rows, feat = x_ref.shape
    width = pre_ref.shape[1]
    grad = tn(spread(pad, sent, rows, back_ref.shape[0]), back_ref[...])
    normed, inverse = norm_parts(pre_ref[...])
    gp = norm_back(grad, normed, inverse, gr_ref[...]).astype(bf16)
    gp_ref[...] = gp
    acc_ref[:feat, :] = tn(x_ref[...], gp)
    acc_ref[feat:, :] = jnp.zeros((acc_ref.shape[0] - feat, width), f32)
    acc_ref[feat : feat + box_ref.shape[0], :] = nn(box_ref[...], gp)
    at = feat + 8
    acc_ref[at : at + 1, :] = jnp.sum(gp.astype(f32), 0, keepdims=True)
    acc_ref[at + 1 : at + 2, :] = jnp.sum(grad * normed, 0, keepdims=True)
    acc_ref[at + 2 : at + 3, :] = jnp.sum(grad, 0, keepdims=True)
    acc_ref[at + 8 : at + 16, :] = sums_ref[...]
    acc_ref[at + 16 : at + 24, :] = attn_sums_ref[...]
    acc_ref[at + 24 : at + 24 + bu_ref.shape[0], :] = bu_ref[...]
    core = core_ref[0]
    half = len(outs) // 2
    chunk = sum(ref.shape[1] for ref in outs[:half])
    for i in range(outs[0].shape[0]):
        for side in (0, 1):
            at = (2 * i + (1 - core if side == 0 else core)) * chunk
            for ref in outs[side * half : (side + 1) * half]:
                rows_here = ref.shape[1]
                ref[i] = acc_ref[pl.ds(pl.multiple_of(at, 8), rows_here), :].astype(bf16)
                at = at + rows_here


def feed_forward(
    captions, counts, n_ref, mixed_ref, cot_ref, wd_ref, *refs,
):
    blocks = len(refs) - 17
    up_refs = refs[:blocks]
    wu_ref = refs[-1]

    @pl.when(pl.program_id(0) == 0)
    def _():
        for j in range(blocks):
            wu_ref[j] = up_refs[j][...].astype(f32).reshape(wu_ref.shape[1:]).astype(bf16)

    feed_forward_rows(captions, counts, n_ref, mixed_ref, cot_ref, wu_ref, wd_ref, *refs[blocks:-1])


def feed_forward_rows(
    captions, counts, n_ref, mixed_ref, cot_ref, wu_ref, wd_ref, wo_ref, bu_ref, bd_ref, g1_ref, g2_ref, beta2_ref,
    out_ref, act_ref, gdo_ref, gg_ref, gm_ref, ga_ref, gc_ref, sums_ref, bu_sum_ref, d_ref,
):
    s = pl.program_id(0)
    n1 = n_ref[...]
    rows, width = n1.shape
    ff = act_ref.shape[1]
    step = width
    per = wd_ref.shape[0] * step // ff

    def down_rows(j):
        return wd_ref[j // step * per : (j // step + 1) * per].reshape(step, width)

    @pl.when(s == 0)
    def _():
        sums_ref[...] = jnp.zeros_like(sums_ref)
        bu_sum_ref[...] = jnp.zeros_like(bu_sum_ref)

    second = n1.astype(f32) + bd_ref[...]
    for j in range(0, ff, step):
        cols = slice(j, j + step)
        gate = nn(n1, wu_ref[j // step]) + bu_ref[cols]
        act, d = gelu_parts(gate)
        act = act.astype(bf16)
        act_ref[:, cols] = act
        d_ref[:, cols] = d
        second = second + nn(act, down_rows(j))
    normed, inverse = norm_parts(second)
    text_len = rows // 2
    row = lax.broadcasted_iota(jnp.int32, (rows, 1), 0)
    live = (row < captions[s]) | ((row >= text_len) & (row < text_len + counts[s]))
    live = live.astype(f32)
    out_ref[...] = ((normed * g2_ref[...] + beta2_ref[...]) * live).astype(bf16)
    up = cot_ref[...].astype(f32) * live

    def add(i, value):
        sums_ref[i : i + 1, :] += jnp.sum(value, 0, keepdims=True)

    add(0, up * normed)
    add(1, up)
    gsi = norm_back(up, normed, inverse, g2_ref[...])
    gdo = gsi.astype(bf16)
    gdo_ref[...] = gdo
    add(2, gdo.astype(f32))
    first = gsi
    for j in range(0, ff, step):
        cols = slice(j, j + step)
        gg = (nt(gdo, down_rows(j)) * d_ref[:, cols]).astype(bf16)
        gg_ref[:, cols] = gg
        at = j // step
        bu_sum_ref[at : at + 1, :] += jnp.sum(gg.astype(f32), 0, keepdims=True)
        first = first + nt(gg, wu_ref[j // step])
    normed, inverse = norm_parts(mixed_ref[...])
    add(3, first * normed)
    add(4, first)
    gm = norm_back(first, normed, inverse, g1_ref[...])
    gm_ref[...] = gm
    ga = gm.astype(bf16)
    ga_ref[...] = ga
    add(5, ga.astype(f32))
    gc_ref[...] = nt(ga, wo_ref[...]).astype(bf16)


def attention_backward(
    pad, sent, devices,
    counts, offset,
    q_ref, k_ref, v_ref, p_ref, gc_ref, gm_ref, wq_ref, wk_ref, wv_ref,
    gq_ref, gk_ref, gv_ref, gt_ref, gs_ref, sums_ref, acc_ref,
):
    s = pl.program_id(0)
    rows, width = q_ref.shape
    hd = width // HEADS
    scale = hd**-0.5

    @pl.when(s == 0)
    def _():
        sums_ref[...] = jnp.zeros_like(sums_ref)

    lane = lax.broadcasted_iota(jnp.int32, (1, 2 * hd), 1)
    masks = [(lane < hd).astype(bf16), (lane >= hd).astype(bf16)]
    for pair in range(HEADS // 2):
        cols = slice(pair * 2 * hd, (pair + 1) * 2 * hd)
        gq = gk = gv = None
        for j in range(2):
            p = p_ref[0, 2 * pair + j]
            gc = gc_ref[:, cols] * masks[j]
            gp = nt(v_ref[:, cols], gc)
            part = nn(p, gc)
            gv = part if gv is None else gv + part
            pf = p.astype(f32)
            weighted = pf * gp
            gs = (weighted - pf * jnp.sum(weighted, 0, keepdims=True)).astype(bf16)
            part = tn(gs, k_ref[:, cols] * masks[j])
            gq = part if gq is None else gq + part
            part = nn(gs, q_ref[:, cols] * masks[j])
            gk = part if gk is None else gk + part
        gq_ref[:, cols] = (gq * scale).astype(bf16)
        gk_ref[:, cols] = (gk * scale).astype(bf16)
        gv_ref[:, cols] = gv.astype(bf16)
    gq, gk, gv = gq_ref[...], gk_ref[...], gv_ref[...]
    sums_ref[0:1, :] += jnp.sum(gq.astype(f32), 0, keepdims=True)
    sums_ref[1:2, :] += jnp.sum(gv.astype(f32), 0, keepdims=True)
    hidden = gm_ref[...] + nt(gq, wq_ref[...]) + nt(gk, wk_ref[...]) + nt(gv, wv_ref[...])
    text_len = gt_ref.shape[0]
    gt_ref[...] = hidden[:text_len].astype(bf16)
    start = jnp.int32(0)
    for i in range(counts.shape[0]):
        start = start + jnp.where(s > i, counts[i], 0)
    slot = lax.broadcasted_iota(jnp.int32, (rows - text_len, 1), 0)
    taken = one_hot(
        slot + start, slot < counts[s], acc_ref.shape[0], pad, sent, devices, offset[0]
    )
    part = tn(taken, hidden[text_len:].astype(bf16))

    @pl.when(s == 0)
    def _():
        acc_ref[...] = part

    @pl.when(s > 0)
    def _():
        acc_ref[...] += part

    @pl.when(s == pl.num_programs(0) - 1)
    def _():
        gs_ref[...] = acc_ref[...].astype(bf16)


def whole(shape):
    return pl.BlockSpec(shape, lambda s, *_: (0,) * len(shape), pipeline_mode=pl.Buffered(1))


def tile(shape):
    return pl.BlockSpec(shape, lambda s, *_: (s,) + (0,) * (len(shape) - 1))


def still(shape):
    return pl.BlockSpec(shape, lambda s, *_: (0,) * len(shape))


LIMIT = 60 * 1024 * 1024


def cost(flops, moved, exps=0):
    return pl.CostEstimate(flops=int(flops), bytes_accessed=int(moved), transcendentals=int(exps))


def run_image_encode(geometry, core, x, boxes, halves, wb, bi, gr, betar):
    pad, sent, devices = geometry
    rows, feat = x.shape
    d = wb.shape[1]
    operands = (x, boxes, wb, bi, gr, betar, *halves)
    shapes = [
        jax.ShapeDtypeStruct((rows, d), f32),
        jax.ShapeDtypeStruct((pad * devices, d), bf16),
        jax.ShapeDtypeStruct((devices, feat // devices, d), bf16),
    ]
    return pl.pallas_call(
        functools.partial(image_encode, pad, sent),
        out_shape=shapes,
        grid_spec=pltpu.PrefetchScalarGridSpec(
            num_scalar_prefetch=1,
            grid=(1,),
            in_specs=[whole(t.shape) for t in operands],
            out_specs=[whole(t.shape) for t in shapes],
        ),
        compiler_params=pltpu.CompilerParams(vmem_limit_bytes=LIMIT),
        cost_estimate=cost(2 * rows * d * feat, x.size * 2 + feat * d * 4 + rows * d * 6),
        name="image_encode",
    )(core, *operands)


def run_attention_forward(
    geometry, captions, counts, offset, enc, text, wq, wk, wv, wo, bq, bv, bo, g1, beta1
):
    seqs = captions.shape[0]
    text_rows, d = text.shape
    total = 2 * text_rows
    L = total // seqs
    row = tile((L, d))
    vec = whole((d,))
    mat = whole((d, d))
    shapes = (
        [jax.ShapeDtypeStruct((total, d), bf16)] * 4
        + [
            jax.ShapeDtypeStruct((seqs, HEADS, L, L), bf16),
            jax.ShapeDtypeStruct((total, d), bf16),
            jax.ShapeDtypeStruct((total, d), f32),
            jax.ShapeDtypeStruct((total, d), bf16),
        ]
    )
    return pl.pallas_call(
        functools.partial(attention_forward, *geometry),
        out_shape=shapes,
        grid_spec=pltpu.PrefetchScalarGridSpec(
            num_scalar_prefetch=3,
            grid=(seqs,),
            in_specs=[whole(enc.shape), tile((L // 2, d))] + [mat] * 4 + [vec] * 5,
            out_specs=[row] * 4 + [tile((1, HEADS, L, L))] + [row] * 3,
        ),
        compiler_params=pltpu.CompilerParams(
            dimension_semantics=("arbitrary",), vmem_limit_bytes=LIMIT
        ),
        cost_estimate=cost(
            2 * total * d * (4 * d + 2 * L * 4),
            total * d * 18 + seqs * HEADS * L * L * 2,
            seqs * HEADS * L * L,
        ),
        name="attention_forward",
    )(
        captions, counts, offset, enc, text,
        wq, wk, wv, wo, bq, bv, bo, g1, beta1,
    )


def run_image_backward(geometry, chunk, core, x, boxes, pre, back, gr, sums, attn_sums, bu):
    pad, sent, devices = geometry
    rows, feat = x.shape
    d = pre.shape[1]
    first = 8 * (-(-chunk // 16))
    parts = [
        jax.ShapeDtypeStruct((devices // 2, r, d), bf16) for r in (first, chunk - first) * 2
    ]
    operands = (x, boxes, pre, back, gr, sums, attn_sums, bu)
    gp, *out = pl.pallas_call(
        functools.partial(image_backward, pad, sent),
        out_shape=[
            jax.ShapeDtypeStruct((rows, d), bf16),
            *parts,
        ],
        grid_spec=pltpu.PrefetchScalarGridSpec(
            num_scalar_prefetch=1,
            grid=(1,),
            in_specs=[whole(o.shape) for o in operands],
            out_specs=[whole((rows, d))] + [whole(p.shape) for p in parts],
            scratch_shapes=[pltpu.VMEM((devices * chunk, d), f32)],
        ),
        compiler_params=pltpu.CompilerParams(
            dimension_semantics=("arbitrary",), vmem_limit_bytes=LIMIT
        ),
        cost_estimate=cost(2 * rows * d * feat, x.size * 2 + devices * chunk * d * 2),
        name="image_backward",
    )(core, *operands)
    return gp, list(zip(out[:2], out[2:]))


def join_kernel(core_ref, *refs):
    core = core_ref[0]
    out_ref = refs[-1]
    groups = list(zip(refs[:-1:2], refs[1:-1:2]))
    at = 0
    for i in range(groups[0][0].shape[0]):
        for first in (0, 1):
            for own_ref, came_ref in groups:
                own, came = own_ref[i].astype(f32), came_ref[i].astype(f32)
                rows = own.shape[0]
                out_ref[at : at + rows, :] = jnp.where(core == first, own, came)
                at += rows


def join_blocks(core, halves, shape, step):
    pairs, rows, width = halves[0].shape
    per = width // (2 * rows)
    down, right = step
    block = pl.BlockSpec((per, rows, width), lambda s, *_: (s, 0, 0))
    return pl.pallas_call(
        join_kernel,
        out_shape=jax.ShapeDtypeStruct(shape, f32),
        grid_spec=pltpu.PrefetchScalarGridSpec(
            num_scalar_prefetch=1,
            grid=(pairs // per,),
            in_specs=[block, block],
            out_specs=pl.BlockSpec((width, width), lambda s, *_: (s * down, s * right)),
        ),
        cost_estimate=cost(0, pairs * rows * width * 12),
        name="join_blocks",
    )(core, *halves)


def widen_rest_kernel(
    attn_rows, feat, picks, parts_ref, *refs
):
    squares, refs = refs[:4], refs[4:]
    img_ref, box_ref, refs = refs[0], refs[1], refs[2:]
    vectors, long_ref, refs = refs[: len(picks)], refs[len(picks)], refs[len(picks) + 1 :]
    in_buf, square_buf, img_buf, in_sem, out_sem = refs
    devices, rows, width = in_buf.shape
    img_rows = rows - attn_rows
    per = devices // 4
    loads = [
        pltpu.make_async_copy(
            parts_ref.at[j * per : (j + 1) * per], in_buf.at[j * per : (j + 1) * per], in_sem.at[j]
        )
        for j in range(4)
    ]
    for copy in loads:
        copy.start()
    stores = []

    def store(source, target):
        copy = pltpu.make_async_copy(source, target, out_sem.at[len(stores)])
        copy.start()
        stores.append(copy)

    for j in range(4):
        loads[j].wait()
        for i in range(per):
            value = in_buf[j * per + i, :attn_rows, :].astype(f32)
            square_buf[j, i * attn_rows : (i + 1) * attn_rows, :] = value
        store(square_buf.at[j], squares[j])
        for i in range(j * per, (j + 1) * per):
            value = in_buf[i, attn_rows:, :].astype(f32)
            img_buf[i * img_rows : (i + 1) * img_rows, :] = value
        first, last = [min(t * per * img_rows, feat) for t in (j, j + 1)]
        if last > first:
            store(img_buf.at[first:last], img_ref.at[first:last])
    box_ref[...] = img_buf[feat : feat + box_ref.shape[0], :]
    for pick, ref in zip(picks, vectors):
        ref[...] = img_buf[feat + pick, :]
    for i in range(long_ref.shape[0] // width):
        long_ref[i * width : (i + 1) * width] = img_buf[feat + 32 + i, :]
    for copy in stores:
        copy.wait()


def widen_rest(parts, attn_rows, feat, boxes, long, picks):
    devices, rows, width = parts.shape
    shapes = [(width, width)] * 4 + [(feat, width), (boxes, width)]
    shapes += [(width,)] * len(picks) + [(long,)]
    return pl.pallas_call(
        functools.partial(widen_rest_kernel, attn_rows, feat, picks),
        out_shape=[jax.ShapeDtypeStruct(t, f32) for t in shapes],
        in_specs=[pl.BlockSpec(memory_space=pl.ANY)],
        out_specs=[pl.BlockSpec(memory_space=pl.ANY)] * 5
        + [pl.BlockSpec(memory_space=pltpu.VMEM)] * (len(picks) + 2),
        scratch_shapes=[
            pltpu.VMEM((devices, rows, width), bf16),
            pltpu.VMEM((4, width, width), f32),
            pltpu.VMEM((devices * (rows - attn_rows), width), f32),
            pltpu.SemaphoreType.DMA((4,)),
            pltpu.SemaphoreType.DMA((8,)),
        ],
        compiler_params=pltpu.CompilerParams(vmem_limit_bytes=LIMIT),
        cost_estimate=cost(0, parts.size * 6),
        name="widen_rest",
    )(parts)


def run_feed_forward(captions, counts, n1, mixed, cot, weights, cut, wo, bu, bd, g1, g2, beta2):
    seqs = captions.shape[0]
    total, d = n1.shape
    devices = weights.shape[0]
    down = weights.shape[1] // 2
    ff = devices * down
    blocks = ff // d

    def part(rows, index):
        return pl.BlockSpec(
            (devices, rows, d), lambda s, *_: (0, index, 0), pipeline_mode=pl.Buffered(1)
        )

    if cut % 8 == 0:
        ups = [part(cut, blocks + j) for j in range(blocks)]
        up_weights = [weights] * blocks
    else:
        ups = [whole((d, d))] * blocks
        up_weights = [
            weights[:, down + j * cut : down + (j + 1) * cut].reshape(d, d) for j in range(blocks)
        ]

    L = total // seqs
    row = tile((L, d))
    wide = tile((L, ff))
    vec = whole((d,))
    shapes = [
        jax.ShapeDtypeStruct((total, d), bf16),
        jax.ShapeDtypeStruct((total, ff), bf16),
        jax.ShapeDtypeStruct((total, d), bf16),
        jax.ShapeDtypeStruct((total, ff), bf16),
        jax.ShapeDtypeStruct((total, d), f32),
        jax.ShapeDtypeStruct((total, d), bf16),
        jax.ShapeDtypeStruct((total, d), bf16),
        jax.ShapeDtypeStruct((8, d), f32),
        jax.ShapeDtypeStruct((blocks, d), f32),
    ]
    return pl.pallas_call(
        feed_forward,
        out_shape=shapes,
        grid_spec=pltpu.PrefetchScalarGridSpec(
            num_scalar_prefetch=2,
            grid=(seqs,),
            in_specs=[row, row, row, part(down, 0)]
            + ups
            + [whole((d, d)), whole((ff,)), vec, vec, vec, vec],
            out_specs=[row, wide, row, wide, row, row, row, still((8, d)), still((blocks, d))],
            scratch_shapes=[pltpu.VMEM((L, ff), f32), pltpu.VMEM((blocks, d, d), bf16)],
        ),
        compiler_params=pltpu.CompilerParams(
            dimension_semantics=("arbitrary",), vmem_limit_bytes=LIMIT
        ),
        cost_estimate=cost(2 * total * d * (4 * ff + d), total * (ff * 4 + d * 18) + d * ff * 4, total * ff),
        name="feed_forward",
    )(captions, counts, n1, mixed, cot, weights, *up_weights, wo, bu, bd, g1, g2, beta2)


def run_attention_backward(geometry, counts, offset, q, k, v, p, gc, gm, wq, wk, wv):
    seqs, _, L, _ = p.shape
    total, d = q.shape
    row = tile((L, d))
    half = tile((L // 2, d))
    mat = whole((d, d))
    received = geometry[0] * geometry[2]
    shapes = [jax.ShapeDtypeStruct((total, d), bf16)] * 3 + [
        jax.ShapeDtypeStruct((total // 2, d), bf16),
        jax.ShapeDtypeStruct((received, d), bf16),
        jax.ShapeDtypeStruct((8, d), f32),
    ]
    return pl.pallas_call(
        functools.partial(attention_backward, *geometry),
        out_shape=shapes,
        grid_spec=pltpu.PrefetchScalarGridSpec(
            num_scalar_prefetch=2,
            grid=(seqs,),
            in_specs=[row, row, row, tile((1, HEADS, L, L)), row, row, mat, mat, mat],
            out_specs=[row, row, row, half, still((received, d)), still((8, d))],
            scratch_shapes=[pltpu.VMEM((received, d), f32)],
        ),
        compiler_params=pltpu.CompilerParams(
            dimension_semantics=("arbitrary",), vmem_limit_bytes=LIMIT
        ),
        cost_estimate=cost(2 * total * d * (3 * d + 4 * L * 4), total * d * 20 + seqs * HEADS * L * L * 2),
        name="attention_backward",
    )(counts, offset, q, k, v, p, gc, gm, wq, wk, wv)


def weight_grad_kernel(lhs_of, rhs_of, groups, core_ref, *refs):
    lhs_refs = refs[: max(lhs_of) + 1]
    rhs_refs = refs[len(lhs_refs) : len(lhs_refs) + max(rhs_of) + 1]
    outs = refs[len(lhs_refs) + len(rhs_refs) : -1]
    acc_ref = refs[-1]
    step = pl.program_id(0)
    core = core_ref[0]
    kinds = {}
    for i, kind in enumerate(zip(lhs_of, rhs_of)):
        kinds.setdefault(kind, []).append(i)
    for (a, b), steps in kinds.items():

        @pl.when((step >= steps[0]) & (step <= steps[-1]))
        def _(a=a, b=b):
            value = tn(lhs_refs[a][...], rhs_refs[b][...]).astype(bf16)
            acc_ref[...] = value.reshape(acc_ref.shape)

    for i in range(outs[0].shape[0]):
        for side in (0, 1):
            at = 0
            for ref in outs[side * groups : (side + 1) * groups]:
                rows = ref.shape[1]
                ref[i] = acc_ref[2 * i + (1 - core if side == 0 else core), at : at + rows, :]
                at += rows


def weight_grads(core, devices, lhs, rhs, lhs_of, rhs_of, lhs_maps, rhs_maps, width, groups, name):
    steps = len(lhs_of)
    total = lhs[0].shape[0]
    rows = steps * width // devices
    per = width // rows
    outs = [rows // groups] * (2 * groups)
    specs = [pl.BlockSpec((total, width), m) for m in lhs_maps + rhs_maps]
    out = pl.pallas_call(
        functools.partial(weight_grad_kernel, lhs_of, rhs_of, groups),
        out_shape=[jax.ShapeDtypeStruct((devices // 2, r, width), bf16) for r in outs],
        grid_spec=pltpu.PrefetchScalarGridSpec(
            num_scalar_prefetch=1,
            grid=(steps,),
            in_specs=specs,
            out_specs=[pl.BlockSpec((per // 2, r, width), lambda s, *_: (s, 0, 0)) for r in outs],
            scratch_shapes=[pltpu.VMEM((per, rows, width), bf16)],
        ),
        compiler_params=pltpu.CompilerParams(
            dimension_semantics=("arbitrary",), vmem_limit_bytes=LIMIT
        ),
        cost_estimate=cost(2 * total * width * width * steps, steps * width * (total + width) * 2),
        name=name,
    )(core, *lhs, *rhs)
    return list(zip(out[:groups], out[groups:]))


def axis_bits(name):
    size = lax.axis_size(name)
    bits = []
    step = 1
    while step < size:
        bits.append((name, step))
        step *= 2
    return bits


def bit_layout():
    return axis_bits("enc")[::-1] + axis_bits("dp")[::-1]


def my_bit(bit):
    return (lax.axis_index(bit[0]) // bit[1]) % 2


def swap_bit(tensor, bit):
    name, step = bit
    size = lax.axis_size(name)
    return lax.ppermute(tensor, name, [(i, i ^ step) for i in range(size)])


def stage_orders():
    dp_bits, enc_bits = axis_bits("dp"), axis_bits("enc")
    near, middle = dp_bits[:1], dp_bits[1:]
    half = len(middle) // 2
    return (
        near + middle + enc_bits,
        near + middle[half:] + middle[:half] + enc_bits,
    )


def add_low(kept, came):
    return (kept.astype(f32) + came.astype(f32)).astype(bf16)


class Scatter:
    def __init__(self, away, kept, order):
        self.order = list(order)
        self.layout = bit_layout()
        self.value = (away, kept)
        self.fresh = True

    def prepare(self):
        bit = self.order[0]
        axis = self.layout.index(bit)
        mine = my_bit(bit)
        self.value = tuple(
            add_low(*[lax.dynamic_index_in_dim(t, i, axis, keepdims=False) for t in self.value])
            for i in (1 - mine, mine)
        )
        self.fresh = True

    def stage(self):
        if not self.fresh:
            self.prepare()
        self.fresh = False
        bit = self.order.pop(0)
        self.layout.remove(bit)
        away, kept = self.value
        shape = (2,) * len(self.layout) + kept.shape[-2:]
        self.value = (kept.reshape(shape), swap_bit(away, bit).reshape(shape))
        return away

    def total(self):
        return add_low(*self.value)


class Gather:
    def __init__(self, rows, order, layout=()):
        self.order = list(order)[::-1]
        self.layout = list(layout)
        self.value = rows

    def stage(self):
        bit = self.order.pop(0)
        sent = self.value
        came = swap_bit(sent, bit)
        self.layout = [b for b in bit_layout() if b in self.layout or b == bit]
        axis = self.layout.index(bit)
        shape = sent.shape[:axis] + (2,) + sent.shape[axis:]
        at = lax.broadcasted_iota(jnp.int32, shape, axis)
        self.value = jnp.where(
            at == my_bit(bit), jnp.expand_dims(sent, axis), jnp.expand_dims(came, axis)
        )
        return sent

    def rows(self):
        return self.value.reshape((-1,) + self.value.shape[-2:])

    def halves(self):
        (bit,) = self.order
        came = swap_bit(self.value, bit)
        shape = (-1,) + came.shape[-2:]
        return self.value.reshape(shape), came.reshape(shape)

    def split(self, at, orders):
        values = (self.value[..., :at, :], self.value[..., at:, :])
        return [
            Gather(value, [b for b in order if b not in self.layout], self.layout)
            for value, order in zip(values, orders)
        ]


def fence(movers, *values):
    leaves, tree = jax.tree.flatten(([m.value for m in movers], values))
    held, values = jax.tree.unflatten(tree, lax.optimization_barrier(leaves))
    for mover, value in zip(movers, held):
        mover.value = value
    return values


def in_turn(*movers):
    sent = []
    for mover in movers:
        fence([mover], sent)
        sent = mover.stage()


class Sum:
    def __init__(self, parts, orders):
        far = len(axis_bits("enc"))
        self.movers = [Scatter(*part, order) for part, order in zip(parts, orders)]
        self.steps = [self.run] * (len(orders[0]) - far) + [self.merge] + [self.run] * (far - 1)

    @property
    def value(self):
        return [m.value for m in self.movers]

    @value.setter
    def value(self, values):
        for mover, value in zip(self.movers, values):
            mover.value = value

    def stage(self):
        return self.steps.pop(0)() if self.steps else []

    def run(self):
        return [mover.stage() for mover in self.movers]

    def prepare(self):
        for mover in self.movers:
            mover.prepare()

    def merge(self):
        first = self.movers[0]
        first.value = tuple(jnp.concatenate(t, -2) for t in zip(*[m.value for m in self.movers]))
        self.movers = [first]
        return self.run()

    def total(self):
        return self.movers[0].total()


def body(
    text,
    region_feats,
    boxes,
    caption_count,
    region_count,
    region_offset,
    w_img,
    w_box,
    b_img,
    g_reg,
    beta_reg,
    w_query,
    b_query,
    w_key,
    w_value,
    b_value,
    w_out,
    b_out,
    g_one,
    beta_one,
    w_up,
    b_up,
    w_down,
    b_down,
    g_two,
    beta_two,
    cotangent,
):
    axes = ("enc", "dp")
    orders = stage_orders()
    model_width = text.shape[1]
    ff_blocks = w_up.shape[1] // model_width
    cut = w_query.shape[0]
    far = axis_bits("enc")

    middle = len(orders[0]) - 1 - len(far)
    core = (lax.axis_index("dp") % 2).astype(jnp.int32).reshape(1)

    up_blocks = w_up.reshape(cut, ff_blocks, model_width).transpose(1, 0, 2)
    ff_shard = jnp.concatenate([w_down, up_blocks.reshape(ff_blocks * cut, model_width)], 0)
    rows_up = cut
    img = Gather(w_img, far)
    attn = Gather(jnp.concatenate([w_query, w_key, w_value, w_out], 0), far)
    img.stage()
    (ff_shard,) = fence([img, attn], ff_shard)
    while img.order:
        img.stage()
        attn.stage()
        (ff_shard,) = fence([img, attn], ff_shard)
    ff_weights = lax.all_gather(ff_shard, axes, axis=0)
    img = img.split(w_img.shape[0] // 2, orders)
    attn.stage()
    for _ in range(middle):
        for part in img:
            part.stage()
        fence([*img, attn])
    attn = attn.split(2 * cut, orders)
    img_halves = fence(attn, *[t for part in img for t in part.halves()])
    for part in attn:
        part.stage()
    device_count = lax.axis_size(axes)
    seq_count = caption_count.shape[0]
    sent_rows, feat = region_feats.shape
    per_peer = sent_rows // device_count
    pad = 8 * (-(-per_peer // 8))
    pad = 1 << (pad - 1).bit_length()
    box_count = boxes.shape[0]
    geometry = (pad, per_peer, device_count)
    pre_norm, encoded, img_full = run_image_encode(
        geometry, core, region_feats, boxes, img_halves, w_box, b_img, g_reg, beta_reg
    )
    img_full = img_full.reshape(feat, model_width)
    (encoded,) = fence(attn, encoded)
    received = lax.all_to_all(encoded, axes, split_axis=0, concat_axis=0, tiled=True)
    for _ in range(middle - 1):
        for part in attn:
            part.stage()
        (received,) = fence(attn, received)
    for part in attn:
        part.stage()
    query_full, key_full, value_full, out_full = [
        t.reshape(-1, model_width)
        for part in attn
        for t in (part.rows()[:, :cut], part.rows()[:, cut:])
    ]
    (
        hidden_in,
        queries,
        keys,
        values,
        probs,
        context,
        mixed,
        normed_one,
    ) = run_attention_forward(
        geometry,
        caption_count,
        region_count,
        region_offset,
        received,
        text,
        query_full,
        key_full,
        value_full,
        out_full,
        b_query,
        b_value,
        b_out,
        g_one,
        beta_one,
    )
    (
        output,
        activated,
        grad_down_out,
        grad_gate,
        grad_mixed,
        grad_attn,
        grad_context,
        sums,
        grad_b_up,
    ) = run_feed_forward(
        caption_count,
        region_count,
        normed_one,
        mixed,
        cotangent,
        ff_weights,
        rows_up,
        out_full,
        b_up,
        b_down,
        g_one,
        g_two,
        beta_two,
    )
    fixed = lambda s, *_: (0, 0)
    moving = lambda s, *_: (0, s)
    (down,) = weight_grads(
        core,
        device_count,
        [activated],
        [grad_down_out],
        [0] * ff_blocks,
        [0] * ff_blocks,
        [moving],
        [fixed],
        model_width,
        1,
        "grad_w_down",
    )
    (up,) = weight_grads(
        core,
        device_count,
        [normed_one],
        [grad_gate],
        [0] * ff_blocks,
        [0] * ff_blocks,
        [fixed],
        [moving],
        model_width,
        1,
        "grad_w_up",
    )
    ff = Sum([down, up], orders)
    ff.stage()
    sent = ff.stage()
    grad_context, _ = fence([], grad_context, sent)
    grad_query, grad_keys, grad_values, grad_text, grad_slots, attn_sums = run_attention_backward(
        geometry,
        region_count,
        region_offset,
        queries,
        keys,
        values,
        probs,
        grad_context,
        grad_mixed,
        query_full,
        key_full,
        value_full,
    )
    grad_query, grad_keys, grad_values, grad_slots, attn_sums = fence(
        [ff], grad_query, grad_keys, grad_values, grad_slots, attn_sums
    )
    back = lax.all_to_all(grad_slots, axes, split_axis=0, concat_axis=0, tiled=True)
    ff.stage()
    attn_parts = weight_grads(
        core,
        device_count,
        [hidden_in, context],
        [grad_query, grad_keys, grad_values, grad_attn],
        [0, 0, 0, 1],
        [0, 1, 2, 3],
        [fixed] * 2,
        [fixed] * 4,
        model_width,
        2,
        "grad_w_attn",
    )
    attn = Sum(attn_parts, orders)
    (back,) = fence([ff, attn], back)
    while len(ff.steps) > len(far):
        ff.stage()
        fence([ff])
    in_turn(ff, attn)
    attn.prepare()
    small_rows = 40
    chunk = 8 * (-(-(feat + small_rows) // (8 * device_count)))
    grad_pre, img_parts = run_image_backward(
        geometry,
        chunk,
        core,
        region_feats,
        boxes,
        pre_norm,
        back,
        g_reg,
        sums,
        attn_sums,
        grad_b_up,
    )
    img = Sum(img_parts, orders)
    img.stage()
    fence([ff, attn, img])
    while ff.steps:
        if len(ff.steps) > 1:
            in_turn(ff)
        else:
            in_turn(ff, attn)
            img.prepare()
        fence([ff, attn, img])
    ff = Gather(ff.total(), far)
    in_turn(ff, img, attn)
    fence([attn, img, ff])
    while img.steps:
        in_turn(attn, img)
        fence([attn, img, ff])
    rest = jnp.concatenate([attn.total(), img.total()], 0)
    rest_all = lax.all_gather(rest, axes, axis=0)
    _, grad_pre = fence([ff], rest, grad_pre)
    while ff.order:
        ff.stage()
        fence([ff])
    down, up = ff.split(w_down.shape[0], orders)
    while len(down.order) > 1:
        down.stage()
        up.stage()
        fence([down, up])
    down_halves, up_halves = down.halves(), up.halves()
    grad_w_down = join_blocks(
        core, down_halves, (ff_blocks * model_width, model_width), (1, 0)
    )
    grad_w_up = join_blocks(core, up_halves, (model_width, ff_blocks * model_width), (0, 1))
    grad_feats = jnp.einsum("rb,ab->ra", grad_pre, img_full, preferred_element_type=f32).astype(bf16)
    grad_boxes = jnp.einsum("cd,rd->cr", w_box, grad_pre, preferred_element_type=f32).astype(bf16)
    (
        grad_w_query,
        grad_w_key,
        grad_w_value,
        grad_w_out,
        grad_w_img,
        grad_w_box,
        grad_b_img,
        grad_g_reg,
        grad_beta_reg,
        grad_g_two,
        grad_beta_two,
        grad_b_down,
        grad_g_one,
        grad_beta_one,
        grad_b_out,
        grad_b_query,
        grad_b_value,
        grad_b_up,
    ) = widen_rest(
        rest_all,
        4 * cut,
        feat,
        box_count,
        b_up.shape[0],
        (8, 9, 10, 16, 17, 18, 19, 20, 21, 24, 25),
    )
    return (
        output,
        grad_text,
        grad_feats,
        grad_boxes,
        grad_w_img,
        grad_w_box,
        grad_b_img,
        grad_g_reg,
        grad_beta_reg,
        grad_w_query,
        grad_b_query,
        grad_w_key,
        grad_w_value,
        grad_b_value,
        grad_w_out,
        grad_b_out,
        grad_g_one,
        grad_beta_one,
        grad_w_up,
        grad_b_up,
        grad_w_down,
        grad_b_down,
        grad_g_two,
        grad_beta_two,
    )


def solution(mesh):
    return jax.shard_map(
        body,
        mesh=mesh,
        in_specs=(
            P(("enc", "dp"), None),
            P(("enc", "dp"), None),
            P(None, ("enc", "dp")),
            P(("enc", "dp")),
            P(("enc", "dp")),
            P(("enc", "dp")),
            P(("enc", "dp"), None),
            P(),
            P(),
            P(),
            P(),
            P(("enc", "dp"), None),
            P(),
            P(("enc", "dp"), None),
            P(("enc", "dp"), None),
            P(),
            P(("enc", "dp"), None),
            P(),
            P(),
            P(),
            P(("enc", "dp"), None),
            P(),
            P(("enc", "dp"), None),
            P(),
            P(),
            P(),
            P(("enc", "dp"), None),
        ),
        out_specs=(
            P(("enc", "dp"), None),
            P(("enc", "dp"), None),
            P(("enc", "dp"), None),
            P(None, ("enc", "dp")),
            P(),
            P(),
            P(),
            P(),
            P(),
            P(),
            P(),
            P(),
            P(),
            P(),
            P(),
            P(),
            P(),
            P(),
            P(),
            P(),
            P(),
            P(),
            P(),
            P(),
        ),
        check_vma=False,
    )
```

```python
import functools
import math

import jax
import jax.numpy as jnp
from jax import lax
from jax.experimental import pallas as pl
from jax.experimental.pallas import tpu as pltpu
from jax.sharding import PartitionSpec as P

HEADS = 12
epsilon = 1e-05
f32, bf16 = jnp.float32, jnp.bfloat16

ERFC_P = 0.35
ERFC_C = (
    0.19567911,
    0.22612264,
    0.02080242,
    0.63768037,
    -0.6386366,
    0.75239514,
    -0.19404308,
)


def nn(a, b):
    return lax.dot_general(a, b, (((1,), (0,)), ((), ())), preferred_element_type=f32)


def nt(a, b):
    return lax.dot_general(a, b, (((1,), (1,)), ((), ())), preferred_element_type=f32)


def tn(a, b):
    return lax.dot_general(a, b, (((0,), (0,)), ((), ())), preferred_element_type=f32)


def norm_parts(values):
    centered = values - jnp.mean(values, -1, keepdims=True)
    inverse = lax.rsqrt(jnp.mean(centered * centered, -1, keepdims=True) + epsilon)
    return centered * inverse, inverse


def norm_back(upstream, normed, inverse, gain):
    weighted = upstream * gain
    return inverse * (
        weighted
        - jnp.mean(weighted, -1, keepdims=True)
        - normed * jnp.mean(weighted * normed, -1, keepdims=True)
    )


def gelu_parts(x):
    e = jnp.exp(-0.5 * x * x)
    t = 1.0 / (1.0 + (ERFC_P * math.sqrt(0.5)) * jnp.abs(x))
    acc = jnp.full_like(t, 0.5 * ERFC_C[-1])
    for c in ERFC_C[-2::-1]:
        acc = acc * t + 0.5 * c
    tail = acc * t * e
    phi = jnp.where(x >= 0, 1.0 - tail, tail)
    return x * phi, phi + x * (e * (1.0 / math.sqrt(2.0 * math.pi)))


def one_hot(wanted, live, rows, pad, sent, devices, offset):
    row = lax.broadcasted_iota(jnp.int32, (1, rows), 1)
    shift = pad.bit_length() - 1
    turn = lax.shift_right_logical(row, shift) - offset
    turn = jnp.where(turn < 0, turn + devices, turn)
    inside = jnp.bitwise_and(row, pad - 1)
    arrival = jnp.where(inside < sent, inside * devices + turn, -1)
    return ((wanted == arrival) & live).astype(bf16)


def spread(pad, sent, rows, padded):
    to = lax.broadcasted_iota(jnp.int32, (padded, 1), 0)
    shift = pad.bit_length() - 1
    inside = jnp.bitwise_and(to, pad - 1)
    source = jnp.where(inside < sent, lax.shift_right_logical(to, shift) * sent + inside, -1)
    return (source == lax.broadcasted_iota(jnp.int32, (1, rows), 1)).astype(bf16)


def image_encode(
    pad, sent, core_ref,
    x_ref, box_ref, wb_ref, bi_ref, gr_ref, betar_ref, *refs,
):
    *halves, pre_ref, enc_ref, wi_ref = refs
    core = core_ref[0]
    at = 0
    for own_ref, came_ref in zip(halves[::2], halves[1::2]):
        pairs, rows, _ = own_ref.shape
        for i in range(pairs):
            wi_ref[2 * i + core, at : at + rows, :] = own_ref[i]
            wi_ref[2 * i + 1 - core, at : at + rows, :] = came_ref[i]
        at += rows
    weight = wi_ref[...].reshape(x_ref.shape[1], wi_ref.shape[2])
    pre = nn(x_ref[...], weight) + tn(box_ref[...], wb_ref[...]) + bi_ref[...]
    pre_ref[...] = pre
    normed, _ = norm_parts(pre)
    encoded = (normed * gr_ref[...] + betar_ref[...]).astype(bf16)
    enc_ref[...] = nn(spread(pad, sent, x_ref.shape[0], enc_ref.shape[0]), encoded).astype(bf16)


def attention_forward(
    pad, sent, devices,
    captions, counts, offset,
    enc_ref, text_ref,
    wq_ref, wk_ref, wv_ref, wo_ref, bq_ref, bv_ref, bo_ref, g_ref, beta_ref,
    h_ref, q_ref, k_ref, v_ref, p_ref, c_ref, mixed_ref, n_ref,
):
    s = pl.program_id(0)
    text_len = text_ref.shape[0]
    rows, width = h_ref.shape
    hd = width // HEADS
    start = jnp.int32(0)
    for i in range(captions.shape[0]):
        start = start + jnp.where(s > i, counts[i], 0)
    slot = lax.broadcasted_iota(jnp.int32, (rows - text_len, 1), 0)
    taken = one_hot(
        slot + start, slot < counts[s], enc_ref.shape[0], pad, sent, devices, offset[0]
    )
    h_ref[:text_len, :] = text_ref[...]
    h_ref[text_len:, :] = nn(taken, enc_ref[...]).astype(bf16)
    h = h_ref[...]
    q = (nn(h, wq_ref[...]) + bq_ref[...]).astype(bf16)
    k = nn(h, wk_ref[...]).astype(bf16)
    v = (nn(h, wv_ref[...]) + bv_ref[...]).astype(bf16)
    q_ref[...] = q
    k_ref[...] = k
    v_ref[...] = v
    row = lax.broadcasted_iota(jnp.int32, (rows, 1), 0)
    live = (row < captions[s]) | ((row >= text_len) & (row < text_len + counts[s]))
    lane = lax.broadcasted_iota(jnp.int32, (1, 2 * hd), 1)
    masks = [(lane < hd).astype(bf16), (lane >= hd).astype(bf16)]
    scaled = q * jnp.asarray(hd**-0.5, bf16)
    for pair in range(HEADS // 2):
        cols = slice(pair * 2 * hd, (pair + 1) * 2 * hd)
        context = None
        for j in range(2):
            scores = nt(k[:, cols], scaled[:, cols] * masks[j])
            scores = jnp.where(live, scores, -1e30)
            top = jnp.max(scores, 0, keepdims=True)
            e = jnp.exp(scores - top)
            p = (e * (1.0 / jnp.sum(e, 0, keepdims=True))).astype(bf16)
            p_ref[0, 2 * pair + j] = p
            part = tn(p, v[:, cols] * masks[j])
            context = part if context is None else context + part
        c_ref[:, cols] = context.astype(bf16)
    mixed = h.astype(f32) + nn(c_ref[...], wo_ref[...]) + bo_ref[...]
    mixed_ref[...] = mixed
    normed, _ = norm_parts(mixed)
    n_ref[...] = (normed * g_ref[...] + beta_ref[...]).astype(bf16)


def image_backward(
    pad, sent, core_ref,
    x_ref, box_ref, pre_ref, back_ref, gr_ref, sums_ref, attn_sums_ref, bu_ref,
    gp_ref, *outs,
):
    *outs, acc_ref = outs
    rows, feat = x_ref.shape
    width = pre_ref.shape[1]
    grad = tn(spread(pad, sent, rows, back_ref.shape[0]), back_ref[...])
    normed, inverse = norm_parts(pre_ref[...])
    gp = norm_back(grad, normed, inverse, gr_ref[...]).astype(bf16)
    gp_ref[...] = gp
    acc_ref[:feat, :] = tn(x_ref[...], gp)
    acc_ref[feat:, :] = jnp.zeros((acc_ref.shape[0] - feat, width), f32)
    acc_ref[feat : feat + box_ref.shape[0], :] = nn(box_ref[...], gp)
    at = feat + 8
    acc_ref[at : at + 1, :] = jnp.sum(gp.astype(f32), 0, keepdims=True)
    acc_ref[at + 1 : at + 2, :] = jnp.sum(grad * normed, 0, keepdims=True)
    acc_ref[at + 2 : at + 3, :] = jnp.sum(grad, 0, keepdims=True)
    acc_ref[at + 8 : at + 16, :] = sums_ref[...]
    acc_ref[at + 16 : at + 24, :] = attn_sums_ref[...]
    acc_ref[at + 24 : at + 24 + bu_ref.shape[0], :] = bu_ref[...]
    core = core_ref[0]
    half = len(outs) // 2
    chunk = sum(ref.shape[1] for ref in outs[:half])
    for i in range(outs[0].shape[0]):
        for side in (0, 1):
            at = (2 * i + (1 - core if side == 0 else core)) * chunk
            for ref in outs[side * half : (side + 1) * half]:
                rows_here = ref.shape[1]
                ref[i] = acc_ref[pl.ds(pl.multiple_of(at, 8), rows_here), :].astype(bf16)
                at = at + rows_here


def feed_forward(
    captions, counts, n_ref, mixed_ref, cot_ref, wd_ref, *refs,
):
    blocks = len(refs) - 17
    up_refs = refs[:blocks]
    wu_ref = refs[-1]

    @pl.when(pl.program_id(0) == 0)
    def _():
        for j in range(blocks):
            wu_ref[j] = up_refs[j][...].astype(f32).reshape(wu_ref.shape[1:]).astype(bf16)

    feed_forward_rows(captions, counts, n_ref, mixed_ref, cot_ref, wu_ref, wd_ref, *refs[blocks:-1])


def feed_forward_rows(
    captions, counts, n_ref, mixed_ref, cot_ref, wu_ref, wd_ref, wo_ref, bu_ref, bd_ref, g1_ref, g2_ref, beta2_ref,
    out_ref, act_ref, gdo_ref, gg_ref, gm_ref, ga_ref, gc_ref, sums_ref, bu_sum_ref, d_ref,
):
    s = pl.program_id(0)
    n1 = n_ref[...]
    rows, width = n1.shape
    ff = act_ref.shape[1]
    step = width
    per = wd_ref.shape[0] * step // ff

    def down_rows(j):
        return wd_ref[j // step * per : (j // step + 1) * per].reshape(step, width)

    @pl.when(s == 0)
    def _():
        sums_ref[...] = jnp.zeros_like(sums_ref)
        bu_sum_ref[...] = jnp.zeros_like(bu_sum_ref)

    second = n1.astype(f32) + bd_ref[...]
    for j in range(0, ff, step):
        cols = slice(j, j + step)
        gate = nn(n1, wu_ref[j // step]) + bu_ref[cols]
        act, d = gelu_parts(gate)
        act = act.astype(bf16)
        act_ref[:, cols] = act
        d_ref[:, cols] = d
        second = second + nn(act, down_rows(j))
    normed, inverse = norm_parts(second)
    text_len = rows // 2
    row = lax.broadcasted_iota(jnp.int32, (rows, 1), 0)
    live = (row < captions[s]) | ((row >= text_len) & (row < text_len + counts[s]))
    live = live.astype(f32)
    out_ref[...] = ((normed * g2_ref[...] + beta2_ref[...]) * live).astype(bf16)
    up = cot_ref[...].astype(f32) * live

    def add(i, value):
        sums_ref[i : i + 1, :] += jnp.sum(value, 0, keepdims=True)

    add(0, up * normed)
    add(1, up)
    gsi = norm_back(up, normed, inverse, g2_ref[...])
    gdo = gsi.astype(bf16)
    gdo_ref[...] = gdo
    add(2, gdo.astype(f32))
    first = gsi
    for j in range(0, ff, step):
        cols = slice(j, j + step)
        gg = (nt(gdo, down_rows(j)) * d_ref[:, cols]).astype(bf16)
        gg_ref[:, cols] = gg
        at = j // step
        bu_sum_ref[at : at + 1, :] += jnp.sum(gg.astype(f32), 0, keepdims=True)
        first = first + nt(gg, wu_ref[j // step])
    normed, inverse = norm_parts(mixed_ref[...])
    add(3, first * normed)
    add(4, first)
    gm = norm_back(first, normed, inverse, g1_ref[...])
    gm_ref[...] = gm
    ga = gm.astype(bf16)
    ga_ref[...] = ga
    add(5, ga.astype(f32))
    gc_ref[...] = nt(ga, wo_ref[...]).astype(bf16)


def attention_backward(
    pad, sent, devices,
    counts, offset,
    q_ref, k_ref, v_ref, p_ref, gc_ref, gm_ref, wq_ref, wk_ref, wv_ref,
    gq_ref, gk_ref, gv_ref, gt_ref, gs_ref, sums_ref, acc_ref,
):
    s = pl.program_id(0)
    rows, width = q_ref.shape
    hd = width // HEADS
    scale = hd**-0.5

    @pl.when(s == 0)
    def _():
        sums_ref[...] = jnp.zeros_like(sums_ref)

    lane = lax.broadcasted_iota(jnp.int32, (1, 2 * hd), 1)
    masks = [(lane < hd).astype(bf16), (lane >= hd).astype(bf16)]
    for pair in range(HEADS // 2):
        cols = slice(pair * 2 * hd, (pair + 1) * 2 * hd)
        gq = gk = gv = None
        for j in range(2):
            p = p_ref[0, 2 * pair + j]
            gc = gc_ref[:, cols] * masks[j]
            gp = nt(v_ref[:, cols], gc)
            part = nn(p, gc)
            gv = part if gv is None else gv + part
            pf = p.astype(f32)
            weighted = pf * gp
            gs = (weighted - pf * jnp.sum(weighted, 0, keepdims=True)).astype(bf16)
            part = tn(gs, k_ref[:, cols] * masks[j])
            gq = part if gq is None else gq + part
            part = nn(gs, q_ref[:, cols] * masks[j])
            gk = part if gk is None else gk + part
        gq_ref[:, cols] = (gq * scale).astype(bf16)
        gk_ref[:, cols] = (gk * scale).astype(bf16)
        gv_ref[:, cols] = gv.astype(bf16)
    gq, gk, gv = gq_ref[...], gk_ref[...], gv_ref[...]
    sums_ref[0:1, :] += jnp.sum(gq.astype(f32), 0, keepdims=True)
    sums_ref[1:2, :] += jnp.sum(gv.astype(f32), 0, keepdims=True)
    hidden = gm_ref[...] + nt(gq, wq_ref[...]) + nt(gk, wk_ref[...]) + nt(gv, wv_ref[...])
    text_len = gt_ref.shape[0]
    gt_ref[...] = hidden[:text_len].astype(bf16)
    start = jnp.int32(0)
    for i in range(counts.shape[0]):
        start = start + jnp.where(s > i, counts[i], 0)
    slot = lax.broadcasted_iota(jnp.int32, (rows - text_len, 1), 0)
    taken = one_hot(
        slot + start, slot < counts[s], acc_ref.shape[0], pad, sent, devices, offset[0]
    )
    part = tn(taken, hidden[text_len:].astype(bf16))

    @pl.when(s == 0)
    def _():
        acc_ref[...] = part

    @pl.when(s > 0)
    def _():
        acc_ref[...] += part

    @pl.when(s == pl.num_programs(0) - 1)
    def _():
        gs_ref[...] = acc_ref[...].astype(bf16)


def whole(shape):
    return pl.BlockSpec(shape, lambda s, *_: (0,) * len(shape), pipeline_mode=pl.Buffered(1))


def tile(shape):
    return pl.BlockSpec(shape, lambda s, *_: (s,) + (0,) * (len(shape) - 1))


def still(shape):
    return pl.BlockSpec(shape, lambda s, *_: (0,) * len(shape))


LIMIT = 60 * 1024 * 1024


def cost(flops, moved, exps=0):
    return pl.CostEstimate(flops=int(flops), bytes_accessed=int(moved), transcendentals=int(exps))


def run_image_encode(geometry, core, x, boxes, halves, wb, bi, gr, betar):
    pad, sent, devices = geometry
    rows, feat = x.shape
    d = wb.shape[1]
    operands = (x, boxes, wb, bi, gr, betar, *halves)
    shapes = [
        jax.ShapeDtypeStruct((rows, d), f32),
        jax.ShapeDtypeStruct((pad * devices, d), bf16),
        jax.ShapeDtypeStruct((devices, feat // devices, d), bf16),
    ]
    return pl.pallas_call(
        functools.partial(image_encode, pad, sent),
        out_shape=shapes,
        grid_spec=pltpu.PrefetchScalarGridSpec(
            num_scalar_prefetch=1,
            grid=(1,),
            in_specs=[whole(t.shape) for t in operands],
            out_specs=[whole(t.shape) for t in shapes],
        ),
        compiler_params=pltpu.CompilerParams(vmem_limit_bytes=LIMIT),
        cost_estimate=cost(2 * rows * d * feat, x.size * 2 + feat * d * 4 + rows * d * 6),
        name="image_encode",
    )(core, *operands)


def run_attention_forward(
    geometry, captions, counts, offset, enc, text, wq, wk, wv, wo, bq, bv, bo, g1, beta1
):
    seqs = captions.shape[0]
    text_rows, d = text.shape
    total = 2 * text_rows
    L = total // seqs
    row = tile((L, d))
    vec = whole((d,))
    mat = whole((d, d))
    shapes = (
        [jax.ShapeDtypeStruct((total, d), bf16)] * 4
        + [
            jax.ShapeDtypeStruct((seqs, HEADS, L, L), bf16),
            jax.ShapeDtypeStruct((total, d), bf16),
            jax.ShapeDtypeStruct((total, d), f32),
            jax.ShapeDtypeStruct((total, d), bf16),
        ]
    )
    return pl.pallas_call(
        functools.partial(attention_forward, *geometry),
        out_shape=shapes,
        grid_spec=pltpu.PrefetchScalarGridSpec(
            num_scalar_prefetch=3,
            grid=(seqs,),
            in_specs=[whole(enc.shape), tile((L // 2, d))] + [mat] * 4 + [vec] * 5,
            out_specs=[row] * 4 + [tile((1, HEADS, L, L))] + [row] * 3,
        ),
        compiler_params=pltpu.CompilerParams(
            dimension_semantics=("arbitrary",), vmem_limit_bytes=LIMIT
        ),
        cost_estimate=cost(
            2 * total * d * (4 * d + 2 * L * 4),
            total * d * 18 + seqs * HEADS * L * L * 2,
            seqs * HEADS * L * L,
        ),
        name="attention_forward",
    )(
        captions, counts, offset, enc, text,
        wq, wk, wv, wo, bq, bv, bo, g1, beta1,
    )


def run_image_backward(geometry, chunk, core, x, boxes, pre, back, gr, sums, attn_sums, bu):
    pad, sent, devices = geometry
    rows, feat = x.shape
    d = pre.shape[1]
    first = 8 * (-(-chunk // 16))
    parts = [
        jax.ShapeDtypeStruct((devices // 2, r, d), bf16) for r in (first, chunk - first) * 2
    ]
    operands = (x, boxes, pre, back, gr, sums, attn_sums, bu)
    gp, *out = pl.pallas_call(
        functools.partial(image_backward, pad, sent),
        out_shape=[
            jax.ShapeDtypeStruct((rows, d), bf16),
            *parts,
        ],
        grid_spec=pltpu.PrefetchScalarGridSpec(
            num_scalar_prefetch=1,
            grid=(1,),
            in_specs=[whole(o.shape) for o in operands],
            out_specs=[whole((rows, d))] + [whole(p.shape) for p in parts],
            scratch_shapes=[pltpu.VMEM((devices * chunk, d), f32)],
        ),
        compiler_params=pltpu.CompilerParams(
            dimension_semantics=("arbitrary",), vmem_limit_bytes=LIMIT
        ),
        cost_estimate=cost(2 * rows * d * feat, x.size * 2 + devices * chunk * d * 2),
        name="image_backward",
    )(core, *operands)
    return gp, list(zip(out[:2], out[2:]))


def join_kernel(core_ref, *refs):
    core = core_ref[0]
    out_ref = refs[-1]
    groups = list(zip(refs[:-1:2], refs[1:-1:2]))
    at = 0
    for i in range(groups[0][0].shape[0]):
        for first in (0, 1):
            for own_ref, came_ref in groups:
                own, came = own_ref[i].astype(f32), came_ref[i].astype(f32)
                rows = own.shape[0]
                out_ref[at : at + rows, :] = jnp.where(core == first, own, came)
                at += rows


def join_blocks(core, halves, shape, step):
    pairs, rows, width = halves[0].shape
    per = width // (2 * rows)
    down, right = step
    block = pl.BlockSpec((per, rows, width), lambda s, *_: (s, 0, 0))
    return pl.pallas_call(
        join_kernel,
        out_shape=jax.ShapeDtypeStruct(shape, f32),
        grid_spec=pltpu.PrefetchScalarGridSpec(
            num_scalar_prefetch=1,
            grid=(pairs // per,),
            in_specs=[block, block],
            out_specs=pl.BlockSpec((width, width), lambda s, *_: (s * down, s * right)),
        ),
        cost_estimate=cost(0, pairs * rows * width * 12),
        name="join_blocks",
    )(core, *halves)


def widen_rest_kernel(
    attn_rows, feat, picks, parts_ref, *refs
):
    squares, refs = refs[:4], refs[4:]
    img_ref, box_ref, refs = refs[0], refs[1], refs[2:]
    vectors, long_ref, refs = refs[: len(picks)], refs[len(picks)], refs[len(picks) + 1 :]
    in_buf, square_buf, img_buf, in_sem, out_sem = refs
    devices, rows, width = in_buf.shape
    img_rows = rows - attn_rows
    per = devices // 4
    loads = [
        pltpu.make_async_copy(
            parts_ref.at[j * per : (j + 1) * per], in_buf.at[j * per : (j + 1) * per], in_sem.at[j]
        )
        for j in range(4)
    ]
    for copy in loads:
        copy.start()
    stores = []

    def store(source, target):
        copy = pltpu.make_async_copy(source, target, out_sem.at[len(stores)])
        copy.start()
        stores.append(copy)

    for j in range(4):
        loads[j].wait()
        for i in range(per):
            value = in_buf[j * per + i, :attn_rows, :].astype(f32)
            square_buf[j, i * attn_rows : (i + 1) * attn_rows, :] = value
        store(square_buf.at[j], squares[j])
        for i in range(j * per, (j + 1) * per):
            value = in_buf[i, attn_rows:, :].astype(f32)
            img_buf[i * img_rows : (i + 1) * img_rows, :] = value
        first, last = [min(t * per * img_rows, feat) for t in (j, j + 1)]
        if last > first:
            store(img_buf.at[first:last], img_ref.at[first:last])
    box_ref[...] = img_buf[feat : feat + box_ref.shape[0], :]
    for pick, ref in zip(picks, vectors):
        ref[...] = img_buf[feat + pick, :]
    for i in range(long_ref.shape[0] // width):
        long_ref[i * width : (i + 1) * width] = img_buf[feat + 32 + i, :]
    for copy in stores:
        copy.wait()


def widen_rest(parts, attn_rows, feat, boxes, long, picks):
    devices, rows, width = parts.shape
    shapes = [(width, width)] * 4 + [(feat, width), (boxes, width)]
    shapes += [(width,)] * len(picks) + [(long,)]
    return pl.pallas_call(
        functools.partial(widen_rest_kernel, attn_rows, feat, picks),
        out_shape=[jax.ShapeDtypeStruct(t, f32) for t in shapes],
        in_specs=[pl.BlockSpec(memory_space=pl.ANY)],
        out_specs=[pl.BlockSpec(memory_space=pl.ANY)] * 5
        + [pl.BlockSpec(memory_space=pltpu.VMEM)] * (len(picks) + 2),
        scratch_shapes=[
            pltpu.VMEM((devices, rows, width), bf16),
            pltpu.VMEM((4, width, width), f32),
            pltpu.VMEM((devices * (rows - attn_rows), width), f32),
            pltpu.SemaphoreType.DMA((4,)),
            pltpu.SemaphoreType.DMA((8,)),
        ],
        compiler_params=pltpu.CompilerParams(vmem_limit_bytes=LIMIT),
        cost_estimate=cost(0, parts.size * 6),
        name="widen_rest",
    )(parts)


def run_feed_forward(captions, counts, n1, mixed, cot, weights, cut, wo, bu, bd, g1, g2, beta2):
    seqs = captions.shape[0]
    total, d = n1.shape
    devices = weights.shape[0]
    down = weights.shape[1] // 2
    ff = devices * down
    blocks = ff // d

    def part(rows, index):
        return pl.BlockSpec(
            (devices, rows, d), lambda s, *_: (0, index, 0), pipeline_mode=pl.Buffered(1)
        )

    if cut % 8 == 0:
        ups = [part(cut, blocks + j) for j in range(blocks)]
        up_weights = [weights] * blocks
    else:
        ups = [whole((d, d))] * blocks
        up_weights = [
            weights[:, down + j * cut : down + (j + 1) * cut].reshape(d, d) for j in range(blocks)
        ]

    L = total // seqs
    row = tile((L, d))
    wide = tile((L, ff))
    vec = whole((d,))
    shapes = [
        jax.ShapeDtypeStruct((total, d), bf16),
        jax.ShapeDtypeStruct((total, ff), bf16),
        jax.ShapeDtypeStruct((total, d), bf16),
        jax.ShapeDtypeStruct((total, ff), bf16),
        jax.ShapeDtypeStruct((total, d), f32),
        jax.ShapeDtypeStruct((total, d), bf16),
        jax.ShapeDtypeStruct((total, d), bf16),
        jax.ShapeDtypeStruct((8, d), f32),
        jax.ShapeDtypeStruct((blocks, d), f32),
    ]
    return pl.pallas_call(
        feed_forward,
        out_shape=shapes,
        grid_spec=pltpu.PrefetchScalarGridSpec(
            num_scalar_prefetch=2,
            grid=(seqs,),
            in_specs=[row, row, row, part(down, 0)]
            + ups
            + [whole((d, d)), whole((ff,)), vec, vec, vec, vec],
            out_specs=[row, wide, row, wide, row, row, row, still((8, d)), still((blocks, d))],
            scratch_shapes=[pltpu.VMEM((L, ff), f32), pltpu.VMEM((blocks, d, d), bf16)],
        ),
        compiler_params=pltpu.CompilerParams(
            dimension_semantics=("arbitrary",), vmem_limit_bytes=LIMIT
        ),
        cost_estimate=cost(2 * total * d * (4 * ff + d), total * (ff * 4 + d * 18) + d * ff * 4, total * ff),
        name="feed_forward",
    )(captions, counts, n1, mixed, cot, weights, *up_weights, wo, bu, bd, g1, g2, beta2)


def run_attention_backward(geometry, counts, offset, q, k, v, p, gc, gm, wq, wk, wv):
    seqs, _, L, _ = p.shape
    total, d = q.shape
    row = tile((L, d))
    half = tile((L // 2, d))
    mat = whole((d, d))
    received = geometry[0] * geometry[2]
    shapes = [jax.ShapeDtypeStruct((total, d), bf16)] * 3 + [
        jax.ShapeDtypeStruct((total // 2, d), bf16),
        jax.ShapeDtypeStruct((received, d), bf16),
        jax.ShapeDtypeStruct((8, d), f32),
    ]
    return pl.pallas_call(
        functools.partial(attention_backward, *geometry),
        out_shape=shapes,
        grid_spec=pltpu.PrefetchScalarGridSpec(
            num_scalar_prefetch=2,
            grid=(seqs,),
            in_specs=[row, row, row, tile((1, HEADS, L, L)), row, row, mat, mat, mat],
            out_specs=[row, row, row, half, still((received, d)), still((8, d))],
            scratch_shapes=[pltpu.VMEM((received, d), f32)],
        ),
        compiler_params=pltpu.CompilerParams(
            dimension_semantics=("arbitrary",), vmem_limit_bytes=LIMIT
        ),
        cost_estimate=cost(2 * total * d * (3 * d + 4 * L * 4), total * d * 20 + seqs * HEADS * L * L * 2),
        name="attention_backward",
    )(counts, offset, q, k, v, p, gc, gm, wq, wk, wv)


def weight_grad_kernel(lhs_of, rhs_of, groups, core_ref, *refs):
    lhs_refs = refs[: max(lhs_of) + 1]
    rhs_refs = refs[len(lhs_refs) : len(lhs_refs) + max(rhs_of) + 1]
    outs = refs[len(lhs_refs) + len(rhs_refs) : -1]
    acc_ref = refs[-1]
    step = pl.program_id(0)
    core = core_ref[0]
    kinds = {}
    for i, kind in enumerate(zip(lhs_of, rhs_of)):
        kinds.setdefault(kind, []).append(i)
    for (a, b), steps in kinds.items():

        @pl.when((step >= steps[0]) & (step <= steps[-1]))
        def _(a=a, b=b):
            value = tn(lhs_refs[a][...], rhs_refs[b][...]).astype(bf16)
            acc_ref[...] = value.reshape(acc_ref.shape)

    for i in range(outs[0].shape[0]):
        for side in (0, 1):
            at = 0
            for ref in outs[side * groups : (side + 1) * groups]:
                rows = ref.shape[1]
                ref[i] = acc_ref[2 * i + (1 - core if side == 0 else core), at : at + rows, :]
                at += rows


def weight_grads(core, devices, lhs, rhs, lhs_of, rhs_of, lhs_maps, rhs_maps, width, groups, name):
    steps = len(lhs_of)
    total = lhs[0].shape[0]
    rows = steps * width // devices
    per = width // rows
    outs = [rows // groups] * (2 * groups)
    specs = [pl.BlockSpec((total, width), m) for m in lhs_maps + rhs_maps]
    out = pl.pallas_call(
        functools.partial(weight_grad_kernel, lhs_of, rhs_of, groups),
        out_shape=[jax.ShapeDtypeStruct((devices // 2, r, width), bf16) for r in outs],
        grid_spec=pltpu.PrefetchScalarGridSpec(
            num_scalar_prefetch=1,
            grid=(steps,),
            in_specs=specs,
            out_specs=[pl.BlockSpec((per // 2, r, width), lambda s, *_: (s, 0, 0)) for r in outs],
            scratch_shapes=[pltpu.VMEM((per, rows, width), bf16)],
        ),
        compiler_params=pltpu.CompilerParams(
            dimension_semantics=("arbitrary",), vmem_limit_bytes=LIMIT
        ),
        cost_estimate=cost(2 * total * width * width * steps, steps * width * (total + width) * 2),
        name=name,
    )(core, *lhs, *rhs)
    return list(zip(out[:groups], out[groups:]))


def axis_bits(name):
    size = lax.axis_size(name)
    bits = []
    step = 1
    while step < size:
        bits.append((name, step))
        step *= 2
    return bits


def bit_layout():
    return axis_bits("enc")[::-1] + axis_bits("dp")[::-1]


def my_bit(bit):
    return (lax.axis_index(bit[0]) // bit[1]) % 2


def swap_bit(tensor, bit):
    name, step = bit
    size = lax.axis_size(name)
    return lax.ppermute(tensor, name, [(i, i ^ step) for i in range(size)])


def stage_orders():
    dp_bits, enc_bits = axis_bits("dp"), axis_bits("enc")
    near, middle = dp_bits[:1], dp_bits[1:]
    half = len(middle) // 2
    return (
        near + middle + enc_bits,
        near + middle[half:] + middle[:half] + enc_bits,
    )


def add_low(kept, came):
    return (kept.astype(f32) + came.astype(f32)).astype(bf16)


class Scatter:
    def __init__(self, away, kept, order):
        self.order = list(order)
        self.layout = bit_layout()
        self.value = (away, kept)
        self.fresh = True

    def prepare(self):
        bit = self.order[0]
        axis = self.layout.index(bit)
        mine = my_bit(bit)
        self.value = tuple(
            add_low(*[lax.dynamic_index_in_dim(t, i, axis, keepdims=False) for t in self.value])
            for i in (1 - mine, mine)
        )
        self.fresh = True

    def stage(self):
        if not self.fresh:
            self.prepare()
        self.fresh = False
        bit = self.order.pop(0)
        self.layout.remove(bit)
        away, kept = self.value
        shape = (2,) * len(self.layout) + kept.shape[-2:]
        self.value = (kept.reshape(shape), swap_bit(away, bit).reshape(shape))
        return away

    def total(self):
        return add_low(*self.value)


class Gather:
    def __init__(self, rows, order, layout=()):
        self.order = list(order)[::-1]
        self.layout = list(layout)
        self.value = rows

    def stage(self):
        bit = self.order.pop(0)
        sent = self.value
        came = swap_bit(sent, bit)
        self.layout = [b for b in bit_layout() if b in self.layout or b == bit]
        axis = self.layout.index(bit)
        shape = sent.shape[:axis] + (2,) + sent.shape[axis:]
        at = lax.broadcasted_iota(jnp.int32, shape, axis)
        self.value = jnp.where(
            at == my_bit(bit), jnp.expand_dims(sent, axis), jnp.expand_dims(came, axis)
        )
        return sent

    def rows(self):
        return self.value.reshape((-1,) + self.value.shape[-2:])

    def halves(self):
        (bit,) = self.order
        came = swap_bit(self.value, bit)
        shape = (-1,) + came.shape[-2:]
        return self.value.reshape(shape), came.reshape(shape)

    def split(self, at, orders):
        values = (self.value[..., :at, :], self.value[..., at:, :])
        return [
            Gather(value, [b for b in order if b not in self.layout], self.layout)
            for value, order in zip(values, orders)
        ]


def fence(movers, *values):
    leaves, tree = jax.tree.flatten(([m.value for m in movers], values))
    held, values = jax.tree.unflatten(tree, lax.optimization_barrier(leaves))
    for mover, value in zip(movers, held):
        mover.value = value
    return values


def in_turn(*movers):
    sent = []
    for mover in movers:
        fence([mover], sent)
        sent = mover.stage()


class Sum:
    def __init__(self, parts, orders):
        far = len(axis_bits("enc"))
        self.movers = [Scatter(*part, order) for part, order in zip(parts, orders)]
        self.steps = [self.run] * (len(orders[0]) - far) + [self.merge] + [self.run] * (far - 1)

    @property
    def value(self):
        return [m.value for m in self.movers]

    @value.setter
    def value(self, values):
        for mover, value in zip(self.movers, values):
            mover.value = value

    def stage(self):
        return self.steps.pop(0)() if self.steps else []

    def run(self):
        return [mover.stage() for mover in self.movers]

    def prepare(self):
        for mover in self.movers:
            mover.prepare()

    def merge(self):
        first = self.movers[0]
        first.value = tuple(jnp.concatenate(t, -2) for t in zip(*[m.value for m in self.movers]))
        self.movers = [first]
        return self.run()

    def total(self):
        return self.movers[0].total()


def body(
    text,
    region_feats,
    boxes,
    caption_count,
    region_count,
    region_offset,
    w_img,
    w_box,
    b_img,
    g_reg,
    beta_reg,
    w_query,
    b_query,
    w_key,
    w_value,
    b_value,
    w_out,
    b_out,
    g_one,
    beta_one,
    w_up,
    b_up,
    w_down,
    b_down,
    g_two,
    beta_two,
    cotangent,
):
    axes = ("enc", "dp")
    orders = stage_orders()
    model_width = text.shape[1]
    ff_blocks = w_up.shape[1] // model_width
    cut = w_query.shape[0]
    far = axis_bits("enc")

    middle = len(orders[0]) - 1 - len(far)
    core = (lax.axis_index("dp") % 2).astype(jnp.int32).reshape(1)

    up_blocks = w_up.reshape(cut, ff_blocks, model_width).transpose(1, 0, 2)
    ff_shard = jnp.concatenate([w_down, up_blocks.reshape(ff_blocks * cut, model_width)], 0)
    rows_up = cut
    img = Gather(w_img, far)
    attn = Gather(jnp.concatenate([w_query, w_key, w_value, w_out], 0), far)
    img.stage()
    (ff_shard,) = fence([img, attn], ff_shard)
    while img.order:
        img.stage()
        attn.stage()
        (ff_shard,) = fence([img, attn], ff_shard)
    img = img.split(w_img.shape[0] // 2, orders)
    attn.stage()
    for step in range(middle):
        for part in img:
            part.stage()
        (ff_shard,) = fence([*img, attn], ff_shard)
        if step == 0:
            ff_weights = lax.all_gather(ff_shard, axes, axis=0)
    attn = attn.split(2 * cut, orders)
    img_halves = fence(attn, *[t for part in img for t in part.halves()])
    for part in attn:
        part.stage()
    device_count = lax.axis_size(axes)
    seq_count = caption_count.shape[0]
    sent_rows, feat = region_feats.shape
    per_peer = sent_rows // device_count
    pad = 8 * (-(-per_peer // 8))
    pad = 1 << (pad - 1).bit_length()
    box_count = boxes.shape[0]
    geometry = (pad, per_peer, device_count)
    pre_norm, encoded, img_full = run_image_encode(
        geometry, core, region_feats, boxes, img_halves, w_box, b_img, g_reg, beta_reg
    )
    img_full = img_full.reshape(feat, model_width)
    (encoded,) = fence(attn, encoded)
    received = lax.all_to_all(encoded, axes, split_axis=0, concat_axis=0, tiled=True)
    for _ in range(middle - 1):
        for part in attn:
            part.stage()
        (received,) = fence(attn, received)
    for part in attn:
        part.stage()
    query_full, key_full, value_full, out_full = [
        t.reshape(-1, model_width)
        for part in attn
        for t in (part.rows()[:, :cut], part.rows()[:, cut:])
    ]
    (
        hidden_in,
        queries,
        keys,
        values,
        probs,
        context,
        mixed,
        normed_one,
    ) = run_attention_forward(
        geometry,
        caption_count,
        region_count,
        region_offset,
        received,
        text,
        query_full,
        key_full,
        value_full,
        out_full,
        b_query,
        b_value,
        b_out,
        g_one,
        beta_one,
    )
    (
        output,
        activated,
        grad_down_out,
        grad_gate,
        grad_mixed,
        grad_attn,
        grad_context,
        sums,
        grad_b_up,
    ) = run_feed_forward(
        caption_count,
        region_count,
        normed_one,
        mixed,
        cotangent,
        ff_weights,
        rows_up,
        out_full,
        b_up,
        b_down,
        g_one,
        g_two,
        beta_two,
    )
    fixed = lambda s, *_: (0, 0)
    moving = lambda s, *_: (0, s)
    (down,) = weight_grads(
        core,
        device_count,
        [activated],
        [grad_down_out],
        [0] * ff_blocks,
        [0] * ff_blocks,
        [moving],
        [fixed],
        model_width,
        1,
        "grad_w_down",
    )
    (up,) = weight_grads(
        core,
        device_count,
        [normed_one],
        [grad_gate],
        [0] * ff_blocks,
        [0] * ff_blocks,
        [fixed],
        [moving],
        model_width,
        1,
        "grad_w_up",
    )
    ff = Sum([down, up], orders)
    ff.stage()
    sent = ff.stage()
    grad_context, _ = fence([], grad_context, sent)
    grad_query, grad_keys, grad_values, grad_text, grad_slots, attn_sums = run_attention_backward(
        geometry,
        region_count,
        region_offset,
        queries,
        keys,
        values,
        probs,
        grad_context,
        grad_mixed,
        query_full,
        key_full,
        value_full,
    )
    grad_query, grad_keys, grad_values, grad_slots, attn_sums = fence(
        [ff], grad_query, grad_keys, grad_values, grad_slots, attn_sums
    )
    back = lax.all_to_all(grad_slots, axes, split_axis=0, concat_axis=0, tiled=True)
    ff.stage()
    attn_parts = weight_grads(
        core,
        device_count,
        [hidden_in, context],
        [grad_query, grad_keys, grad_values, grad_attn],
        [0, 0, 0, 1],
        [0, 1, 2, 3],
        [fixed] * 2,
        [fixed] * 4,
        model_width,
        2,
        "grad_w_attn",
    )
    attn = Sum(attn_parts, orders)
    (back,) = fence([ff, attn], back)
    while len(ff.steps) > len(far):
        ff.stage()
        fence([ff])
    in_turn(ff, attn)
    attn.prepare()
    small_rows = 40
    chunk = 8 * (-(-(feat + small_rows) // (8 * device_count)))
    grad_pre, img_parts = run_image_backward(
        geometry,
        chunk,
        core,
        region_feats,
        boxes,
        pre_norm,
        back,
        g_reg,
        sums,
        attn_sums,
        grad_b_up,
    )
    img = Sum(img_parts, orders)
    img.stage()
    fence([ff, attn, img])
    while ff.steps:
        if len(ff.steps) > 1:
            in_turn(ff)
        else:
            in_turn(ff, attn)
            img.prepare()
        fence([ff, attn, img])
    ff = Gather(ff.total(), far)
    in_turn(ff, img, attn)
    fence([attn, img, ff])
    while img.steps:
        in_turn(attn, img)
        fence([attn, img, ff])
    rest = jnp.concatenate([attn.total(), img.total()], 0)
    rest_all = lax.all_gather(rest, axes, axis=0)
    _, grad_pre = fence([ff], rest, grad_pre)
    while ff.order:
        ff.stage()
        fence([ff])
    down, up = ff.split(w_down.shape[0], orders)
    while len(down.order) > 1:
        down.stage()
        up.stage()
        fence([down, up])
    down_halves, up_halves = down.halves(), up.halves()
    grad_w_down = join_blocks(
        core, down_halves, (ff_blocks * model_width, model_width), (1, 0)
    )
    grad_w_up = join_blocks(core, up_halves, (model_width, ff_blocks * model_width), (0, 1))
    grad_feats = jnp.einsum("rb,ab->ra", grad_pre, img_full, preferred_element_type=f32).astype(bf16)
    grad_boxes = jnp.einsum("cd,rd->cr", w_box, grad_pre, preferred_element_type=f32).astype(bf16)
    (
        grad_w_query,
        grad_w_key,
        grad_w_value,
        grad_w_out,
        grad_w_img,
        grad_w_box,
        grad_b_img,
        grad_g_reg,
        grad_beta_reg,
        grad_g_two,
        grad_beta_two,
        grad_b_down,
        grad_g_one,
        grad_beta_one,
        grad_b_out,
        grad_b_query,
        grad_b_value,
        grad_b_up,
    ) = widen_rest(
        rest_all,
        4 * cut,
        feat,
        box_count,
        b_up.shape[0],
        (8, 9, 10, 16, 17, 18, 19, 20, 21, 24, 25),
    )
    return (
        output,
        grad_text,
        grad_feats,
        grad_boxes,
        grad_w_img,
        grad_w_box,
        grad_b_img,
        grad_g_reg,
        grad_beta_reg,
        grad_w_query,
        grad_b_query,
        grad_w_key,
        grad_w_value,
        grad_b_value,
        grad_w_out,
        grad_b_out,
        grad_g_one,
        grad_beta_one,
        grad_w_up,
        grad_b_up,
        grad_w_down,
        grad_b_down,
        grad_g_two,
        grad_beta_two,
    )


def solution(mesh):
    return jax.shard_map(
        body,
        mesh=mesh,
        in_specs=(
            P(("enc", "dp"), None),
            P(("enc", "dp"), None),
            P(None, ("enc", "dp")),
            P(("enc", "dp")),
            P(("enc", "dp")),
            P(("enc", "dp")),
            P(("enc", "dp"), None),
            P(),
            P(),
            P(),
            P(),
            P(("enc", "dp"), None),
            P(),
            P(("enc", "dp"), None),
            P(("enc", "dp"), None),
            P(),
            P(("enc", "dp"), None),
            P(),
            P(),
            P(),
            P(("enc", "dp"), None),
            P(),
            P(("enc", "dp"), None),
            P(),
            P(),
            P(),
            P(("enc", "dp"), None),
        ),
        out_specs=(
            P(("enc", "dp"), None),
            P(("enc", "dp"), None),
            P(("enc", "dp"), None),
            P(None, ("enc", "dp")),
            P(),
            P(),
            P(),
            P(),
            P(),
            P(),
            P(),
            P(),
            P(),
            P(),
            P(),
            P(),
            P(),
            P(),
            P(),
            P(),
            P(),
            P(),
            P(),
            P(),
        ),
        check_vma=False,
    )
```
